32 devices in a mesh: seq: 4 (over y, x), ctx: 8 (over z, core).
Axes of the slice: x: 2, y: 2, z: 4, core: 2. Of those that a mesh axis runs over, the one named last changes fastest.
Arguments:
- block_in: bfloat16 [4, 1024, 1024], P('seq', 'ctx'), may hold values from -6 to 6
- cotangent: bfloat16 [4, 1024, 1024], P('seq', 'ctx'), may hold values from -6 to 6
- segments: int32 [4, 1024], P('seq', 'ctx'), may hold values from 0 to 3, never falling along the last dimension, each value on 1 to 512 neighbouring positions
- ln_gain: bfloat16 [1024], P(('seq', 'ctx')), may hold values from 0.5 to 1.5
- ln_bias: bfloat16 [1024], P(('seq', 'ctx')), may hold values from -3 to 3
- w_qkv: bfloat16 [1024, 3072], P(('seq', 'ctx')), as said below
- b_qkv: bfloat16 [3072], P(('seq', 'ctx')), may hold values from -3 to 3
- w_out: bfloat16 [1024, 1024], P(('seq', 'ctx')), may hold values from -0.75 to 0.75
- b_out: bfloat16 [1024], P(('seq', 'ctx')), may hold values from -3 to 3
- w_fc1: bfloat16 [1024, 4096], P(('seq', 'ctx')), may hold values from -0.1875 to 0.1875
- b_fc1: bfloat16 [4096], P(('seq', 'ctx')), may hold values from -3 to 3
- w_fc2: bfloat16 [1024, 4096], P(('seq', 'ctx')), may hold values from -0.09375 to 0.09375
- b_fc2: bfloat16 [1024], P(('seq', 'ctx')), may hold values from -3 to 3
Outputs:
- block_out: bfloat16 [4, 1024, 1024], P('seq', 'ctx')
- in_grad: float32 [4, 1024, 1024], P('seq', 'ctx')
- grad_ln_gain: float32 [1024], P(('seq', 'ctx'))
- grad_ln_bias: float32 [1024], P(('seq', 'ctx'))
- grad_w_qkv: float32 [1024, 3072], P(('seq', 'ctx'))
- grad_b_qkv: float32 [3072], P(('seq', 'ctx'))
- grad_w_out: float32 [1024, 1024], P(('seq', 'ctx'))
- grad_b_out: float32 [1024], P(('seq', 'ctx'))
- grad_w_fc1: float32 [1024, 4096], P(('seq', 'ctx'))
- grad_b_fc1: float32 [4096], P(('seq', 'ctx'))
- grad_w_fc2: float32 [1024, 4096], P(('seq', 'ctx'))
- grad_b_fc2: float32 [1024], P(('seq', 'ctx'))
The draws below stay inside these ranges and needn't reach their ends.
Inputs may be any that keep to these rules, and one draw needn't show every extreme that they name: `segments`: segment ids never fall along a sequence, start at 0 and name 4 documents, each one contiguous run. `w_qkv`: columns are queries, keys, values in that order, each 16 heads of 64 features in a row.
All inputs are finite; a program needn't handle non-finite values.
Results may differ from the reference program's by a relative error of at most 0.0094.
Values may be sent and summed in bfloat16 or wider, within the bound.
No kernel may reach another device: no remote copies, remote signals or barrier semaphores. Data moves between devices by JAX's collectives and lax.ppermute only.
A program may use at most 192 MiB of HBM per device.

```python
import math
import jax
import jax.numpy as jnp
import numpy as np
from jax import lax

D = 1024
HEADS = 16
HEAD_DIM = 64
ROT = 16
FF = 4096
DOCS = 4
SEQ_LEN = 1024
SEQS = 4


def draw_w_qkv(key, part):
    base = jax.random.normal(key, (D, 3 * D), jnp.float32) * D ** (-0.5)
    return base.astype(jnp.bfloat16)


def spiked(entries, key, source, target, blocks, factor):
    def block_of(axis_at):
        return (jnp.arange(entries.shape[axis_at]) // (entries.shape[axis_at] // blocks)).reshape((-1,) + (1,) * (entries.ndim - 1 - axis_at))

    one_side = jax.random.permutation(key, blocks)[block_of(target)]
    other_side = (block_of(target) + blocks // 2) % blocks
    return jnp.where((block_of(source) == one_side) | (block_of(source) == other_side), factor * entries, entries)


def block_scale(key, dims, cuts, least, top_value):
    loudness, own = 1.0, jax.random.fold_in(key, 6)
    for dim, shards_of in cuts:
        draws = jnp.exp(jax.random.uniform(jax.random.fold_in(own, dim), (shards_of,), jnp.float32, least / len(cuts), top_value / len(cuts)))
        loudness = loudness * jnp.repeat(draws, dims[dim] // shards_of).reshape([-1 if axis == dim else 1 for axis in range(len(dims))])
    return loudness


def split_up(count, total, most, skew):
    weights = [(1 << 20) // math.isqrt(grade ** skew) + 1 for grade in range(2, count + 1)]
    surplus, given = total - most - (count - 1), [1] * (count - 1)
    while surplus > 0:
        movable = [i for i in range(count - 1) if given[i] < most]
        whole, left = sum([weights[i] for i in movable]), surplus
        for i in movable:
            more = min(most - given[i], max(1, left * weights[i] // whole), surplus)
            given[i] = given[i] + more
            surplus = surplus - more
    return np.array([most] + given)


def ragged_sizes(key, number_of, total, limit, slope):
    if number_of == 2:
        one = jax.random.randint(key, (), max(1, total - limit), min(limit, total - 1) + 1)
        return jnp.stack([one, total - one])
    tallies = jnp.asarray(split_up(number_of, total, limit, slope), jnp.int32)
    twos = (number_of - 1) // 2
    source_of, receiver = tallies[1:1 + 2 * twos:2], tallies[2:2 + 2 * twos:2]
    room = jnp.minimum(source_of - 1, limit - receiver)
    shifted = jax.random.randint(jax.random.fold_in(key, 1), (twos,), 0, 1 << 20) % (room + 1)
    tallies = tallies.at[1:1 + 2 * twos:2].set(source_of - shifted).at[2:2 + 2 * twos:2].set(receiver + shifted)
    return tallies[jax.random.permutation(jax.random.fold_in(key, 2), number_of)]


def scatter_about(key, extent, scale, limit, pieces=(), held_as=jnp.bfloat16):
    result = scale * jax.random.normal(key, extent, jnp.float32)
    if pieces:
        result = result * block_scale(key, extent, pieces, -0.22, 0.18)
    return jnp.clip(result, -limit, limit).astype(held_as)


def noise_with(rng, extent, scale, most, cuts, heavy, kind=jnp.bfloat16):
    values = scale * jax.random.normal(rng, extent, jnp.float32)
    if cuts:
        values = values * block_scale(rng, extent, cuts, -0.22, 0.18)
    return jnp.clip(spiked(values, jax.random.fold_in(rng, 3), *heavy), -most, most).astype(kind)


def setup_inputs(seed: int = 0) -> dict:
    arg_keys = jax.random.split(jax.random.key(seed), 14)
    return {
        "block_in": scatter_about(arg_keys[0], (SEQS, SEQ_LEN, D), 1.0, 6.0, ((0, 4), (1, 8))),
        "cotangent": noise_with(arg_keys[1], (SEQS, SEQ_LEN, D), 1.0, 6.0, ((0, 4), (1, 8)), (1, 2, 8, 2.0)),
        "segments": jax.vmap(lambda own: jnp.searchsorted(jnp.cumsum(ragged_sizes(own, DOCS, SEQ_LEN, SEQ_LEN // 2, 0)), jnp.arange(SEQ_LEN), side="right"))(jax.random.split(arg_keys[2], SEQS)).reshape((SEQS, SEQ_LEN)).astype(jnp.int32),
        "ln_gain": jnp.clip(1.0 + 0.1 * jax.random.normal(arg_keys[3], (D,), jnp.float32), 0.5, 1.5).astype(jnp.bfloat16),
        "ln_bias": scatter_about(arg_keys[4], (D,), 0.5, 3.0, ((0, 32),)),
        "w_qkv": draw_w_qkv(jax.random.fold_in(arg_keys[13], 71), 0),
        "b_qkv": scatter_about(arg_keys[6], (3 * D,), 0.5, 3.0, ((0, 32),)),
        "w_out": scatter_about(arg_keys[7], (D, D), (D // 16) ** -0.5, 0.75, ((0, 32),)),
        "b_out": scatter_about(arg_keys[8], (D,), 0.5, 3.0, ((0, 32),)),
        "w_fc1": scatter_about(arg_keys[9], (D, FF), D ** -0.5, 0.1875, ((0, 32),)),
        "b_fc1": scatter_about(arg_keys[10], (FF,), 0.5, 3.0, ((0, 32),)),
        "w_fc2": scatter_about(arg_keys[11], (D, FF), FF ** -0.5, 0.09375, ((0, 32),)),
        "b_fc2": scatter_about(arg_keys[12], (D,), 0.5, 3.0, ((0, 32),)),
    }


@jax.custom_vjp
def low(v):
    return lax.optimization_barrier(v.astype(jnp.bfloat16)).astype(jnp.float32)

@jax.custom_vjp
def low_back(v):
    return v

def low_keep(v):
    return (low(v), None)

def low_pass(kept, grad):
    return (grad,)

def back_keep(v):
    return (v, None)

def back_low(kept, grad):
    return (low(grad),)
low.defvjp(low_keep, low_pass)
low_back.defvjp(back_keep, back_low)
HIGH = lax.Precision.HIGHEST
norm_eps = 1e-05
big_negative = -1e+30

def positions_of(seg_rows):
    index = lax.broadcasted_iota(jnp.int32, seg_rows.shape, 1)
    change = jnp.concatenate([jnp.ones((seg_rows.shape[0], 1), jnp.bool_), seg_rows[:, 1:] != seg_rows[:, :-1]], axis=1)
    first = lax.cummax(jnp.where(change, index, jnp.zeros_like(index)), axis=1)
    return index - first

def rotary_tables(pos):
    half = ROT // 2
    freq = jnp.power(jnp.float32(10000.0), -2.0 * jnp.arange(half, dtype=jnp.float32) / ROT)
    angle = pos.astype(jnp.float32)[..., None, None] * freq
    return (jnp.cos(angle), jnp.sin(angle))

def rotate(values, cos_t, sin_t):
    half = ROT // 2
    first = values[..., :half]
    second = values[..., half:ROT]
    return jnp.concatenate([first * cos_t - second * sin_t, second * cos_t + first * sin_t, values[..., ROT:]], axis=-1)

def layer(xv, seg_row, gain, lnb, wqkv, bqkv, wout, bout, wfc1, bfc1, wfc2, bfc2):
    length = xv.shape[0]
    mean_removed = xv - lax.optimization_barrier(jnp.mean(xv, axis=1, keepdims=True))
    inverse_deviation = lax.rsqrt(lax.optimization_barrier(jnp.mean(mean_removed * mean_removed, axis=1, keepdims=True)) + norm_eps)
    normalized_rows = low(mean_removed * inverse_deviation * gain + lnb)
    qkv = low_back(jnp.dot(normalized_rows, wqkv, precision=HIGH) + bqkv)
    pos = positions_of(seg_row[None, :])[0]
    cos_t, sin_t = rotary_tables(pos)
    shape3 = (length, HEADS, HEAD_DIM)
    queries = low(rotate(qkv[:, :D].reshape(shape3), cos_t, sin_t))
    keys = low(rotate(qkv[:, D:2 * D].reshape(shape3), cos_t, sin_t))
    values = low(qkv[:, 2 * D:].reshape(shape3))
    index = jnp.arange(length)
    allowed = (seg_row[:, None] == seg_row[None, :]) & (index[None, :] <= index[:, None])
    group = math.gcd(HEADS, 8)
    count = HEADS // group

    def split(tensor):
        return tensor.reshape(length, count, group, HEAD_DIM).transpose(1, 0, 2, 3)

    def block(item):
        q_grp, k_grp, v_grp = item
        raw = low_back(jnp.einsum('qgd,kgd->gqk', q_grp, k_grp, precision=HIGH))
        scores = jnp.where(allowed[None], raw * 0.125, big_negative)
        top = lax.optimization_barrier(jnp.max(scores, axis=2, keepdims=True))
        expd = jnp.exp(scores - top)
        probs = expd / lax.optimization_barrier(jnp.sum(expd, axis=2, keepdims=True))
        return jnp.einsum('gqk,kgd->qgd', low(probs), v_grp, precision=HIGH)
    blocks = lax.map(jax.checkpoint(block), (split(queries), split(keys), split(values)))
    attn = low(low_back(blocks.transpose(1, 0, 2, 3).reshape(length, D)))
    fc = low_back(jnp.dot(normalized_rows, wfc1, precision=HIGH) + bfc1)
    act = low(jax.nn.gelu(fc, approximate=True))
    return xv + jnp.dot(attn, wout, precision=HIGH) + bout + jnp.dot(act, wfc2.T, precision=HIGH) + bfc2

def reference(block_in, cotangent, segments, ln_gain, ln_bias, w_qkv, b_qkv, w_out, b_out, w_fc1, b_fc1, w_fc2, b_fc2):
    params = tuple((p.astype(jnp.float32) for p in (ln_gain, ln_bias, w_qkv, b_qkv, w_out, b_out, w_fc1, b_fc1, w_fc2, b_fc2)))

    def step(total, item):
        x_seq, c_seq, s_seq = item
        out, pull = jax.vjp(lambda xv, *pv: layer(xv, s_seq, *pv), x_seq.astype(jnp.float32), *params)
        grads = pull(c_seq.astype(jnp.float32))
        total = tuple((t + g for t, g in zip(total, grads[1:])))
        return (total, (out.astype(jnp.bfloat16), grads[0]))
    init = tuple((jnp.zeros_like(p) for p in params))
    total, (outs, in_grads) = lax.scan(step, init, (block_in, cotangent, segments))
    return (outs, in_grads, total[0], total[1], total[2], total[3], total[4], total[5], total[6], total[7], total[8], total[9])
```

```python
import math

import jax
import jax.numpy as jnp
from jax import lax
from jax.experimental import pallas as pl
from jax.experimental.pallas import tpu as pltpu
from jax.sharding import PartitionSpec as P

HEADS = 16
HEAD_DIM = 64
ROT = 16
HALF = ROT // 2

norm_eps = 1e-05
big_negative = -1e30
f32 = jnp.float32
bf16 = jnp.bfloat16


def rows_dot(left, right):
    return lax.dot_general(left, right, (((0,), (0,)), ((), ())), preferred_element_type=f32)


def cols_dot(left, right):
    return lax.dot_general(left, right, (((1,), (1,)), ((), ())), preferred_element_type=f32)


def dot(left, right):
    return lax.dot_general(left, right, (((1,), (0,)), ((), ())), preferred_element_type=f32)


def whole(n):
    return [pl.BlockSpec(memory_space=pltpu.VMEM)] * n


def roll_lanes(x, shift):
    width = x.shape[1]
    shift = shift % width
    if width % 128 == 0:
        return pltpu.roll(x, shift, 1)
    return jnp.concatenate([x[:, width - shift :], x[:, : width - shift]], axis=1)


def norm_kernel(where_ref, own_ref, other_ref, gain_ref, bias_ref, h_ref, xhat_ref):
    piece = own_ref.shape[1]
    core = where_ref[0]
    for ref, slot in ((own_ref, core), (other_ref, 1 - core)):
        x = ref[0].astype(f32)
        centred = x - jnp.mean(x, axis=1, keepdims=True)
        xhat = centred * lax.rsqrt(jnp.mean(centred * centred, axis=1, keepdims=True) + norm_eps)
        rows = pl.ds(pl.multiple_of(slot * piece, piece), piece)
        xhat_ref[rows, :] = xhat.astype(bf16)
        h_ref[rows, :] = (xhat * gain_ref[...] + bias_ref[...]).astype(bf16)


def norm_call(where, own, other, gain, bias):
    count, piece, width = own.shape
    row = pl.BlockSpec((1, width), lambda j, w: (0, 0))
    part = pl.BlockSpec((1, piece, width), lambda j, w: (j, 0, 0))
    out = pl.BlockSpec((2 * piece, width), lambda j, w: (lax.rem(w[1] + j, count), 0))
    return pl.pallas_call(
        norm_kernel,
        grid_spec=pltpu.PrefetchScalarGridSpec(
            num_scalar_prefetch=1,
            grid=(count,),
            in_specs=[part, part, row, row],
            out_specs=[out, out],
        ),
        out_shape=[jax.ShapeDtypeStruct((2 * count * piece, width), bf16)] * 2,
        name="norm",
    )(where, own, other, gain, bias)


def weave_kernel(where_ref, own_ref, other_ref, out_ref):
    piece = own_ref.shape[1]
    core = where_ref[0]
    for ref, slot in ((own_ref, core), (other_ref, 1 - core)):
        out_ref[pl.ds(pl.multiple_of(slot * piece, piece), piece), :] = ref[0]


def weave_call(where, own, other):
    count, piece, width = own.shape
    part = pl.BlockSpec((1, piece, width), lambda j, w: (j, 0, 0))
    out = pl.BlockSpec((2 * piece, width), lambda j, w: (lax.rem(w[1] + j, count), 0))
    return pl.pallas_call(
        weave_kernel,
        grid_spec=pltpu.PrefetchScalarGridSpec(
            num_scalar_prefetch=1, grid=(count,), in_specs=[part, part], out_specs=out
        ),
        out_shape=jax.ShapeDtypeStruct((2 * count * piece, width), own.dtype),
        name="weave",
    )(where, own, other)


def place_kernel(where_ref, *refs):
    *pieces, out_ref = refs
    for ref, at in zip(pieces, range(len(pieces))):
        out_ref[where_ref[at]] = ref[...]


def place_call(order, pieces):
    shape = (len(pieces),) + pieces[0].shape
    return pl.pallas_call(
        place_kernel,
        in_specs=[pl.BlockSpec(memory_space=pltpu.SMEM)] + whole(len(pieces)),
        out_specs=whole(1)[0],
        out_shape=jax.ShapeDtypeStruct(shape, pieces[0].dtype),
        name="place",
    )(order, *pieces)


def rope(x, cos_full, low_sin, high_sin, sign):
    return (
        x * cos_full
        + sign * (roll_lanes(x, HALF) * high_sin - roll_lanes(x, -HALF) * low_sin)
    )


def scores_of(keys, queries_t, first, begin, here, limit):
    raw = dot(keys[:limit], queries_t[:, begin : begin + here])
    key_at = lax.broadcasted_iota(jnp.int32, raw.shape, 0)
    query_at = lax.broadcasted_iota(jnp.int32, raw.shape, 1) + begin
    allowed = (key_at <= query_at) & (key_at >= first[:, begin : begin + here])
    return jnp.where(allowed, raw * 0.125, big_negative)


def attend_kernel(block, heads, qkv_ref, cos_ref, low_ref, high_ref, first_ref, out_ref, lse_ref, kept_ref, out_t):
    seq_len = qkv_ref.shape[0]
    width = heads * HEAD_DIM
    cos_full, low_sin, high_sin = cos_ref[...], low_ref[...], high_ref[...]
    q = rope(qkv_ref[:, :width], cos_full, low_sin, high_sin, 1.0)
    k = rope(qkv_ref[:, width : 2 * width], cos_full, low_sin, high_sin, 1.0)
    v = qkv_ref[:, 2 * width :]
    kb = k.astype(bf16)
    kept_ref[:, :width] = q.astype(bf16)
    kept_ref[:, width : 2 * width] = kb
    kept_ref[:, 2 * width :] = v.astype(bf16)
    q_t = q.T.astype(bf16)
    v_t = v.T.astype(bf16)
    first = first_ref[...]
    for head in range(heads):
        lanes = slice(head * HEAD_DIM, (head + 1) * HEAD_DIM)
        keys, queries_t, values_t = kb[:, lanes], q_t[lanes], v_t[lanes]
        for begin in range(0, seq_len, block):
            limit = begin + block
            scores = scores_of(keys, queries_t, first, begin, block, limit)
            top = jnp.max(scores, axis=0, keepdims=True)
            expd = jnp.exp(scores - top)
            total = jnp.sum(expd, axis=0, keepdims=True)
            probs = (expd * (1.0 / total)).astype(bf16)
            out_t[lanes, begin:limit] = dot(values_t[:, :limit], probs)
            lse_ref[head : head + 1, begin:limit] = top + jnp.log(total)
    out_ref[...] = out_t[...].T.astype(bf16)


def attend_call(block, heads, qkv, tables, first):
    seq_len, total = qkv.shape
    width = total // 3
    return pl.pallas_call(
        lambda *refs: attend_kernel(block, heads, *refs),
        in_specs=whole(5),
        out_specs=whole(3),
        out_shape=[
            jax.ShapeDtypeStruct((seq_len, width), bf16),
            jax.ShapeDtypeStruct((heads, seq_len), f32),
            jax.ShapeDtypeStruct((seq_len, total), bf16),
        ],
        scratch_shapes=[pltpu.VMEM((width, seq_len), f32)],
        name="attend",
    )(qkv, *tables, first)


def attend_back_kernel(
    block, heads, kept_ref, grad_ref, lse_ref, cos_ref, low_ref, high_ref, first_ref, out_ref, sum_ref, dq_t, dk, dv
):
    seq_len = kept_ref.shape[0]
    width = heads * HEAD_DIM
    q = kept_ref[:, :width]
    k = kept_ref[:, width : 2 * width]
    v = kept_ref[:, 2 * width :]
    grad = grad_ref[...]
    q_t = q.astype(f32).T.astype(bf16)
    k_t = k.astype(f32).T.astype(bf16)
    grad_t = grad.astype(f32).T.astype(bf16)
    first = first_ref[...]
    for head in range(heads):
        lanes = slice(head * HEAD_DIM, (head + 1) * HEAD_DIM)
        q_h, k_h, v_h, grad_h = q[:, lanes], k[:, lanes], v[:, lanes], grad[:, lanes]
        for begin in reversed(range(0, seq_len, block)):
            limit = begin + block
            scores = scores_of(k_h, q_t[lanes], first, begin, block, limit)
            probs = jnp.exp(scores - lse_ref[head : head + 1, begin:limit])
            grad_p = dot(v_h[:limit], grad_t[lanes, begin:limit])
            delta = jnp.sum(probs * grad_p, axis=0, keepdims=True)
            grad_s = (probs * (grad_p - delta) * 0.125).astype(bf16)
            dk_here = dot(grad_s, q_h[begin:limit])
            dv_here = dot(probs.astype(bf16), grad_h[begin:limit])
            if limit == seq_len:
                dk[head] = dk_here
                dv[head] = dv_here
            else:
                dk[head, :limit] += dk_here
                dv[head, :limit] += dv_here
            dq_t[lanes, begin:limit] = dot(k_t[lanes, :limit], grad_s)
    cos_full, low_sin, high_sin = cos_ref[...], low_ref[...], high_ref[...]
    dk_all = jnp.concatenate([dk[head] for head in range(heads)], axis=1)
    dv_all = jnp.concatenate([dv[head] for head in range(heads)], axis=1)
    for at, value in (
        (0, rope(dq_t[...].T, cos_full, low_sin, high_sin, -1.0)),
        (1, rope(dk_all, cos_full, low_sin, high_sin, -1.0)),
        (2, dv_all),
    ):
        rounded = value.astype(bf16)
        cols = slice(at * width, (at + 1) * width)
        out_ref[:, cols] = rounded
        sum_ref[:, cols] = jnp.sum(rounded.astype(f32), axis=0, keepdims=True)


def attend_back_call(block, heads, kept, grad, lse, tables, first):
    seq_len, total = kept.shape
    width = total // 3
    return pl.pallas_call(
        lambda *refs: attend_back_kernel(block, heads, *refs),
        in_specs=whole(7),
        out_specs=whole(2),
        out_shape=[
            jax.ShapeDtypeStruct((seq_len, total), bf16),
            jax.ShapeDtypeStruct((1, total), f32),
        ],
        scratch_shapes=[
            pltpu.VMEM((width, seq_len), f32),
            pltpu.VMEM((heads, seq_len, HEAD_DIM), f32),
            pltpu.VMEM((heads, seq_len, HEAD_DIM), f32),
        ],
        name="attend_back",
    )(kept, grad, lse, *tables, first)


def body(
    block_in,
    cotangent,
    segments,
    ln_gain,
    ln_bias,
    w_qkv,
    b_qkv,
    w_out,
    b_out,
    w_fc1,
    b_fc1,
    w_fc2,
    b_fc2,
):
    seqs, ctxs = lax.axis_size("seq"), lax.axis_size("ctx")
    s, c = lax.axis_index("seq"), lax.axis_index("ctx")
    _, piece, width = block_in.shape
    seq_len = piece * ctxs
    share = w_qkv.shape[0]
    hidden = w_fc1.shape[1]
    cut = hidden // ctxs
    heads = HEADS // ctxs
    group = HEAD_DIM // share
    lanes = ctxs // group
    rows_s = ctxs * share
    zs = ctxs // 2
    z, core = c // 2, c % 2
    sub, lane = c % group, c // group
    where = jnp.stack([core, z]).astype(jnp.int32)
    order_s = jnp.stack([(s + k) % seqs for k in range(seqs)]).astype(jnp.int32)

    def from_z(k):
        return [(i, ((i // 2 - k) % zs) * 2 + i % 2) for i in range(ctxs)]

    swap = [(i, i ^ 1) for i in range(ctxs)]

    def from_s(k):
        return [(i, (i - k) % seqs) for i in range(seqs)]

    def spread_ctx(local):
        mine = jnp.stack([local] + [lax.ppermute(local, "ctx", from_z(k)) for k in range(1, zs)])
        return mine, lax.ppermute(mine, "ctx", swap)

    def reduce_ctx(partial):
        blocks = partial.reshape(zs, 2, piece, width)
        theirs = lax.dynamic_index_in_dim(blocks, 1 - core, 1, keepdims=False)
        mine = lax.dynamic_index_in_dim(blocks, core, 1, keepdims=False).astype(f32)
        mine = mine + lax.ppermute(theirs, "ctx", swap).astype(f32)
        total = lax.dynamic_index_in_dim(mine, z, 0, keepdims=False)
        rounded = mine.astype(bf16)
        for k in range(1, zs):
            send = lax.dynamic_index_in_dim(rounded, (z - k) % zs, 0, keepdims=False)
            total = total + lax.ppermute(send, "ctx", from_z(k)).astype(f32)
        return total

    def spread_seq(local):
        return [local] + [lax.ppermute(local, "seq", from_s(k)) for k in range(1, seqs)]

    def reduce_seq(blocks):
        total = lax.dynamic_index_in_dim(blocks, s, 0, keepdims=False).astype(f32)
        for k in range(1, seqs):
            send = lax.dynamic_index_in_dim(blocks, (s - k) % seqs, 0, keepdims=False)
            total = total + lax.ppermute(send, "seq", from_s(k)).astype(f32)
        return total

    def swap_ctx(blocks):
        return lax.all_to_all(blocks, "ctx", split_axis=0, concat_axis=0, tiled=True)

    total_heads = 3 * heads * HEAD_DIM
    per_head = w_qkv.reshape(share, 3, group, heads, lanes, HEAD_DIM)
    per_head = per_head.transpose(4, 2, 0, 1, 3, 5).reshape(ctxs, share, total_heads)
    small = jnp.concatenate(
        [ln_gain, ln_bias, b_out, b_fc2, b_qkv, b_fc1, segments.reshape(piece).astype(bf16)]
    )
    small_rows = -(-small.shape[0] // total_heads)
    small = jnp.pad(small, (0, small_rows * total_heads - small.shape[0]))
    small = jnp.broadcast_to(
        small.reshape(1, small_rows, total_heads), (ctxs, small_rows, total_heads)
    )
    got_qkv = swap_ctx(jnp.concatenate([per_head, small], axis=1))
    fc = jnp.concatenate(
        [w_fc1.reshape(share, ctxs, cut), w_fc2.reshape(share, ctxs, cut)], axis=2
    ).transpose(1, 0, 2)
    got_fc = swap_ctx(fc)
    x_own, x_other = spread_ctx(block_in[0])
    all_qkv = place_call(order_s, spread_seq(got_qkv))
    w_qkv_c = all_qkv[:, :, :share].reshape(width, total_heads)
    smalls = all_qkv[:, :, share:].reshape(seqs * ctxs, small_rows * total_heads)
    all_out = place_call(order_s, spread_seq(w_out))
    all_fc = place_call(order_s, spread_seq(got_fc.reshape(rows_s, 2 * cut))).reshape(width, 2 * cut)
    w_fc1_c, w_fc2_c = all_fc[:, :cut], all_fc[:, cut:]
    halves = []
    for k in range(group):
        send = lax.dynamic_slice_in_dim(all_out, (sub ^ k) * heads, heads, 0)
        halves.append(
            send if k == 0 else lax.ppermute(send, "ctx", [(i, i ^ k) for i in range(ctxs)])
        )
    order_g = jnp.stack([sub ^ k for k in range(group)]).astype(jnp.int32)
    w_out_c = place_call(order_g, halves).transpose(1, 0, 2, 3).reshape(heads * HEAD_DIM, width)

    def small_part(begin, count):
        return smalls[:, begin * share : (begin + count) * share].reshape(-1)

    gain = small_part(0, 1).astype(f32).reshape(1, width)
    shift = small_part(1, 1).astype(f32).reshape(1, width)
    bias_out = small_part(2, 1).astype(f32) + small_part(3, 1).astype(f32)
    bias_qkv = small_part(4, 3).reshape(3, group, heads, lanes, HEAD_DIM)
    bias_qkv = lax.dynamic_slice(bias_qkv, (0, sub, 0, lane, 0), (3, 1, heads, 1, HEAD_DIM))
    bias_qkv = bias_qkv.reshape(1, total_heads).astype(f32)
    bias_fc1 = lax.dynamic_slice_in_dim(small_part(7, 4), c * cut, cut, 0).astype(f32)

    seg = got_qkv[:, share:].reshape(ctxs, -1)[:, 11 * share : 11 * share + piece]
    seg = seg.reshape(1, seq_len)
    first = jnp.zeros((1, seq_len), jnp.int32)
    for name in range(1, 4):
        begin = jnp.sum((seg < name).astype(jnp.int32))
        first = jnp.where(seg >= name, begin, first)
    pos = lax.broadcasted_iota(jnp.int32, (1, seq_len), 1) - first
    freq = jnp.power(f32(10000.0), -2.0 * jnp.arange(HALF, dtype=f32) / ROT)
    angle = (pos.astype(f32) * freq[:, None]).T
    cos_t, sin_t = jnp.cos(angle), jnp.sin(angle)
    ones = jnp.ones((seq_len, HEAD_DIM - ROT), f32)
    zero = jnp.zeros((seq_len, HEAD_DIM - ROT), f32)
    empty = jnp.zeros((seq_len, HALF), f32)
    tables = (
        jnp.concatenate([cos_t, cos_t, ones] * heads, axis=1),
        jnp.concatenate([sin_t, empty, zero] * heads, axis=1),
        jnp.concatenate([empty, sin_t, zero] * heads, axis=1),
    )

    h, xhat = norm_call(where, x_own, x_other, gain, shift)
    block = min(256, seq_len)
    qkv = dot(h, w_qkv_c) + bias_qkv
    attn, lse, kept = attend_call(block, heads, qkv, tables, first)
    pre_act = dot(h, w_fc1_c) + bias_fc1
    act = jax.nn.gelu(pre_act, approximate=True).astype(bf16)
    mixed = (dot(attn, w_out_c) + cols_dot(act, w_fc2_c)).astype(bf16)
    x_here = block_in[0].astype(f32)
    block_out = (x_here + reduce_ctx(mixed) + bias_out).astype(bf16)

    dy_own, dy_other = spread_ctx(cotangent[0])
    dy = weave_call(where, dy_own, dy_other)
    grad_act = dot(dy, w_fc2_c)
    gelu_pull = jax.vjp(lambda value: jax.nn.gelu(value, approximate=True), pre_act)[1]
    grad_pre = gelu_pull(grad_act)[0].astype(bf16)
    grad_fc = jnp.concatenate([rows_dot(h, grad_pre), rows_dot(dy, act)], axis=1).astype(bf16)
    grad_bfc1 = jnp.sum(grad_pre, axis=0, dtype=f32)
    grad_attn = cols_dot(dy, w_out_c).astype(bf16)
    grad_qkv, grad_bqkv = attend_back_call(block, heads, kept, grad_attn, lse, tables, first)
    grad_h = cols_dot(grad_pre, w_fc1_c) + cols_dot(grad_qkv, w_qkv_c)
    grad_gain = jnp.sum(grad_h * xhat.astype(f32), axis=0)
    grad_shift = jnp.sum(grad_h, axis=0)
    grad_wqkv = rows_dot(h, grad_qkv).astype(bf16)
    grad_wout = rows_dot(attn, dy).astype(bf16)

    fc_sum = reduce_seq(grad_fc.reshape(seqs, rows_s, 2 * cut)).astype(bf16)
    fc_mine = swap_ctx(fc_sum.reshape(ctxs, share, 2 * cut)).astype(f32)
    out_wfc1 = fc_mine[:, :, :cut].transpose(1, 0, 2).reshape(share, hidden)
    out_wfc2 = fc_mine[:, :, cut:].transpose(1, 0, 2).reshape(share, hidden)
    qkv_sum = reduce_seq(grad_wqkv.reshape(seqs, rows_s, total_heads)).astype(bf16)
    qkv_mine = swap_ctx(qkv_sum.reshape(ctxs, share, total_heads)).astype(f32)
    out_wqkv = qkv_mine.reshape(lanes, group, share, 3, heads, HEAD_DIM)
    out_wqkv = out_wqkv.transpose(2, 3, 1, 4, 0, 5).reshape(share, 3 * width)
    wout_blocks = grad_wout.reshape(heads, group, share, width)
    halves = []
    for k in range(group):
        send = lax.dynamic_index_in_dim(wout_blocks, sub ^ k, 1, keepdims=False)
        halves.append(
            send if k == 0 else lax.ppermute(send, "ctx", [(i, i ^ k) for i in range(ctxs)])
        )
    wout_all = place_call(order_g, halves).reshape(seqs, share, width)
    out_wout = reduce_seq(wout_all)

    bqkv_full = lax.dynamic_update_slice(
        jnp.zeros((3, group, heads, lanes, HEAD_DIM), f32),
        grad_bqkv.reshape(3, 1, heads, 1, HEAD_DIM),
        (0, sub, 0, lane, 0),
    )
    bfc1_full = lax.dynamic_update_slice(jnp.zeros((hidden,), f32), grad_bfc1, (c * cut,))
    grad_y = cotangent[0].astype(f32)
    owners = seqs * ctxs
    vector = jnp.concatenate(
        [
            part.reshape(owners, -1)
            for part in (grad_gain, grad_shift, jnp.sum(grad_y, axis=0), bqkv_full, bfc1_full)
        ],
        axis=1,
    )
    vector = lax.all_to_all(vector, ("seq", "ctx"), split_axis=0, concat_axis=0, tiled=True)
    vector = jnp.sum(vector, axis=0)
    cuts = [vector[a * share : b * share] for a, b in ((0, 1), (1, 2), (2, 3), (3, 6), (6, 10))]

    dh = reduce_ctx(grad_h.astype(bf16))
    centred = x_here - jnp.mean(x_here, axis=1, keepdims=True)
    rstd = lax.rsqrt(jnp.mean(centred * centred, axis=1, keepdims=True) + norm_eps)
    xhat_here = centred * rstd
    scaled = dh * gain
    grad_in = grad_y + rstd * (
        scaled
        - jnp.mean(scaled, axis=1, keepdims=True)
        - xhat_here * jnp.mean(scaled * xhat_here, axis=1, keepdims=True)
    )
    return (
        block_out[None],
        grad_in[None],
        cuts[0],
        cuts[1],
        out_wqkv,
        cuts[3],
        out_wout,
        cuts[2],
        out_wfc1,
        cuts[4],
        out_wfc2,
        cuts[2],
    )


def solution(mesh):
    both = ("seq", "ctx")
    tokens, flat, matrix = P("seq", "ctx", None), P(both), P(both, None)
    in_specs = (tokens, tokens, P("seq", "ctx"), flat, flat) + (matrix, flat) * 4
    out_specs = (tokens, tokens, flat, flat) + (matrix, flat) * 4
    return jax.shard_map(body, mesh=mesh, in_specs=in_specs, out_specs=out_specs, check_vma=False)
```

```python
import jax
import jax.numpy as jnp
from jax import lax
from jax.experimental import pallas as pl
from jax.experimental.pallas import tpu as pltpu
from jax.sharding import PartitionSpec as P

HEADS = 16
HEAD_DIM = 64
ROT = 16
HALF = ROT // 2
SMALL = 128

norm_eps = 1e-05
big_negative = -1e30
f32 = jnp.float32
bf16 = jnp.bfloat16


def dot(left, right):
    return lax.dot_general(left, right, (((1,), (0,)), ((), ())), preferred_element_type=f32)


def rows_dot(left, right):
    return lax.dot_general(left, right, (((0,), (0,)), ((), ())), preferred_element_type=f32)


def cols_dot(left, right):
    return lax.dot_general(left, right, (((1,), (1,)), ((), ())), preferred_element_type=f32)


def shape(dims, kind=bf16):
    return jax.ShapeDtypeStruct(dims, kind)


def call(kernel, outs, scratch, scalars, operands, after=(), cost=None):
    vmem = pl.BlockSpec(memory_space=pltpu.VMEM)
    in_specs = (
        [pl.BlockSpec(memory_space=pltpu.SMEM)]
        + [vmem] * len(operands)
        + [pl.BlockSpec(memory_space=pl.ANY)] * len(after)
    )
    count = len(operands)

    def wrapped(*refs):
        kernel(refs[0], *refs[1 : 1 + count], *refs[1 + count + len(after) :])

    flops, moved = cost or (0, 0)
    moved = moved or sum(a.size * a.dtype.itemsize for a in operands)
    results = pl.pallas_call(
        wrapped,
        in_specs=in_specs,
        out_specs=[vmem] * len(outs),
        out_shape=outs,
        scratch_shapes=scratch,
        cost_estimate=pl.CostEstimate(flops=flops, bytes_accessed=moved, transcendentals=0),
    )(scalars, *operands, *after)
    return list(results)


def rows_at(index, count):
    return pl.ds(pl.multiple_of(index * count, count), count)


def roll_lanes(x, shift):
    width = x.shape[1]
    shift = shift % width
    if width % 128 == 0:
        return pltpu.roll(x, shift, 1)
    return jnp.concatenate([x[:, width - shift :], x[:, : width - shift]], axis=1)


CORE, Z, S, SUB, _ = range(5)


def head_lanes(to, part, i, heads, group, lanes, width):
    return part * width + (((to % group) * heads + i) * lanes + to // group) * HEAD_DIM


def pack_call(scalars, group, heads, lanes, w_qkv, w_fc1, w_fc2, vectors, seg):
    share, hidden = w_fc1.shape
    count = group * lanes
    cut = hidden // count
    total = 3 * heads * HEAD_DIM
    width = w_qkv.shape[1] // 3

    def kernel(_, qkv_ref, fc1_ref, fc2_ref, *refs):
        *small_refs, seg_ref, out_ref, small = refs
        small[...] = jnp.zeros_like(small)
        for at, ref in enumerate(small_refs):
            small[at : at + 1, : ref.shape[0]] = ref[...].astype(f32).reshape(1, -1)
        at = len(small_refs)
        small[at : at + 1, : seg_ref.shape[1]] = seg_ref[...].astype(f32)
        rounded = small[...].astype(bf16)
        for to in range(count):
            for part in range(3):
                for i in range(heads):
                    begin = head_lanes(to, part, i, heads, group, lanes, width)
                    put = (part * heads + i) * HEAD_DIM
                    out_ref[to, :, put : put + HEAD_DIM] = qkv_ref[:, begin : begin + HEAD_DIM]
            base = total + SMALL
            out_ref[to, :, total:base] = rounded
            out_ref[to, :, base : base + cut] = fc1_ref[:, to * cut : (to + 1) * cut]
            out_ref[to, :, base + cut :] = fc2_ref[:, to * cut : (to + 1) * cut]

    return call(
        kernel,
        [shape((count, share, total + SMALL + 2 * cut))],
        [pltpu.VMEM((share, SMALL), f32)],
        scalars,
        (w_qkv, w_fc1, w_fc2, *vectors, seg),
    )[0]


def spread_out_call(scalars, pieces, rows, share, width, group, heads):
    seqs = len(pieces)
    lanes = pieces[0].shape[1]
    chunks = -(-width // lanes)

    def kernel(at, *refs):
        in_refs, small_ref, part_refs, stage = refs[:seqs], refs[seqs], refs[seqs + 1 : -1], refs[-1]
        for k, ref in enumerate(in_refs):
            slot = lax.rem(at[S] + k, seqs)
            small_ref[rows_at(slot, rows), :] = ref[:rows, lanes - SMALL :]
            for j in range(chunks):
                upto = min(width - j * lanes, lanes)
                begin = rows + j * share
                stage[slot, :, j * lanes : j * lanes + upto] = ref[begin : begin + share, :upto]
        for k, ref in enumerate(part_refs):
            for i in range(heads):
                ref[i] = stage[(at[SUB] ^ k) * heads + i]

    return call(
        kernel,
        [shape((seqs * rows, SMALL))] + [shape((heads, share, width))] * group,
        [pltpu.VMEM((seqs, share, width), bf16)],
        scalars,
        pieces,
    )


def rope(x, cos_full, low_sin, high_sin, sign):
    return x * cos_full + sign * (
        roll_lanes(x, HALF) * high_sin - roll_lanes(x, -HALF) * low_sin
    )


def scores_of(keys, queries_t, first, begin, here, limit):
    raw = dot(keys[:limit], queries_t[:, begin : begin + here])
    key_at = lax.broadcasted_iota(jnp.int32, raw.shape, 0)
    query_at = lax.broadcasted_iota(jnp.int32, raw.shape, 1) + begin
    allowed = (key_at <= query_at) & (key_at >= first[:, begin : begin + here])
    return jnp.where(allowed, raw, big_negative)


def slots(at, refs):
    count = len(refs) // 2
    for k in range(count):
        here = 2 * lax.rem(at[Z] + k, count)
        yield refs[k], here + at[CORE]
        yield refs[count + k], here + 1 - at[CORE]


def attend_call(scalars, block, heads, rows, pieces, gain, shift, weights, bias, tables, first):
    piece, width = pieces[0].shape
    seq_len = piece * len(pieces)
    seqs = len(weights)
    total = 3 * heads * HEAD_DIM
    own = heads * HEAD_DIM
    tile = min(256, seq_len)

    def kernel(at, *refs):
        n = len(pieces)
        x_refs, (gain_ref, shift_ref), w_refs = refs[:n], refs[n : n + 2], refs[n + 2 : n + 2 + seqs]
        bias_ref, cos_ref, low_ref, high_ref, first_ref = refs[n + 2 + seqs : n + 7 + seqs]
        h_ref, xhat_ref, out_ref, lse_ref, kept_ref, w_ref, x_all, qkv, out_t = refs[n + 7 + seqs :]
        for ref, slot in slots(at, x_refs):
            x_all[rows_at(slot, piece), :] = ref[...]
        for k, ref in enumerate(w_refs):
            w_ref[rows_at(lax.rem(at[S] + k, seqs), rows), :] = ref[:rows, :total]

        def norm_tile(t, carry):
            here = rows_at(t, tile)
            x = x_all[here, :].astype(f32)
            centred = x - jnp.mean(x, axis=1, keepdims=True)
            rstd = lax.rsqrt(jnp.mean(centred * centred, axis=1, keepdims=True) + norm_eps)
            xhat = centred * rstd
            xhat_ref[here, :] = xhat.astype(bf16)
            h = (xhat * gain_ref[...] + shift_ref[...]).astype(bf16)
            h_ref[here, :] = h
            qkv[here, :] = dot(h, w_ref[...]) + bias_ref[...]
            return carry

        lax.fori_loop(0, seq_len // tile, norm_tile, 0)
        cos_full, low_sin, high_sin = cos_ref[...], low_ref[...], high_ref[...]
        q = rope(qkv[:, :own], cos_full, low_sin, high_sin, 1.0) * 0.125
        k = rope(qkv[:, own : 2 * own], cos_full, low_sin, high_sin, 1.0)
        v = qkv[:, 2 * own :]
        kb = k.astype(bf16)
        kept_ref[:, :own] = q.astype(bf16)
        kept_ref[:, own : 2 * own] = kb
        kept_ref[:, 2 * own :] = v.astype(bf16)
        q_t = q.T.astype(bf16)
        v_t = v.T.astype(bf16)
        begins = first_ref[...]
        for head in range(heads):
            lanes = slice(head * HEAD_DIM, (head + 1) * HEAD_DIM)
            keys, queries_t, values_t = kb[:, lanes], q_t[lanes], v_t[lanes]
            for begin in range(0, seq_len, block):
                limit = begin + block
                scores = scores_of(keys, queries_t, begins, begin, block, limit)
                top = jnp.max(scores, axis=0, keepdims=True)
                expd = jnp.exp(scores - top)
                sums = jnp.sum(expd, axis=0, keepdims=True)
                probs = (expd * (1.0 / sums)).astype(bf16)
                out_t[lanes, begin:limit] = dot(values_t[:, :limit], probs)
                lse_ref[head : head + 1, begin:limit] = top + jnp.log(sums)
        out_ref[...] = out_t[...].T.astype(bf16)

    return call(
        kernel,
        [
            shape((seq_len, width)),
            shape((seq_len, width)),
            shape((seq_len, own)),
            shape((heads, seq_len), f32),
            shape((seq_len, total)),
            shape((width, total)),
        ],
        [
            pltpu.VMEM((seq_len, width), bf16),
            pltpu.VMEM((seq_len, total), f32),
            pltpu.VMEM((own, seq_len), f32),
        ],
        scalars,
        (*pieces, gain, shift, *weights, bias, *tables, first),
        cost=(4 * seq_len * width * total, 0),
    )


def attend_back_call(scalars, block, heads, kept, grad, lse, tables, first, after):
    seq_len, total = kept.shape
    own = total // 3

    def kernel(
        at, kept_ref, grad_ref, lse_ref, cos_ref, low_ref, high_ref, first_ref, out_ref, sum_ref, dq_t, dk, dv
    ):
        q = kept_ref[:, :own]
        k = kept_ref[:, own : 2 * own]
        v = kept_ref[:, 2 * own :]
        grad = grad_ref[...]
        q_t = q.astype(f32).T.astype(bf16)
        k_t = k.astype(f32).T.astype(bf16)
        grad_t = grad.astype(f32).T.astype(bf16)
        begins = first_ref[...]
        for head in range(heads):
            lanes = slice(head * HEAD_DIM, (head + 1) * HEAD_DIM)
            q_h, k_h, v_h, grad_h = q[:, lanes], k[:, lanes], v[:, lanes], grad[:, lanes]
            for begin in reversed(range(0, seq_len, block)):
                limit = begin + block
                scores = scores_of(k_h, q_t[lanes], begins, begin, block, limit)
                probs = jnp.exp(scores - lse_ref[head : head + 1, begin:limit])
                grad_p = dot(v_h[:limit], grad_t[lanes, begin:limit])
                delta = jnp.sum(probs * grad_p, axis=0, keepdims=True)
                grad_s = (probs * (grad_p - delta)).astype(bf16)
                dk_here = dot(grad_s, q_h[begin:limit])
                dv_here = dot(probs.astype(bf16), grad_h[begin:limit])
                if limit == seq_len:
                    dk[head] = dk_here
                    dv[head] = dv_here
                else:
                    dk[head, :limit] += dk_here
                    dv[head, :limit] += dv_here
                dq_t[lanes, begin:limit] = dot(k_t[lanes, :limit], grad_s)
        cos_full, low_sin, high_sin = cos_ref[...], low_ref[...], high_ref[...]
        dk_all = jnp.concatenate([dk[head] for head in range(heads)], axis=1)
        dv_all = jnp.concatenate([dv[head] for head in range(heads)], axis=1)
        for part, value in (
            (0, rope(dq_t[...].T * 0.125, cos_full, low_sin, high_sin, -1.0)),
            (1, rope(dk_all, cos_full, low_sin, high_sin, -1.0)),
            (2, dv_all),
        ):
            rounded = value.astype(bf16)
            cols = slice(part * own, (part + 1) * own)
            out_ref[:, cols] = rounded
            sum_ref[:, cols] = jnp.sum(rounded.astype(f32), axis=0, keepdims=True)

    return call(
        kernel,
        [shape((seq_len, total)), shape((1, total), f32)],
        [
            pltpu.VMEM((own, seq_len), f32),
            pltpu.VMEM((heads, seq_len, HEAD_DIM), f32),
            pltpu.VMEM((heads, seq_len, HEAD_DIM), f32),
        ],
        scalars,
        (kept, grad, lse, *tables, first),
        after,
        cost=(10 * seq_len * seq_len * own, 0),
    )


ROOT = 0.7978845608028654
CUBIC = 0.044715


def split_rows(at, z, piece, value, stage, mine_ref, theirs_ref):
    stage[...] = value.astype(bf16)
    mine_ref[rows_at(z, piece), :] = stage[rows_at(at[CORE], piece), :]
    theirs_ref[rows_at(z, piece), :] = stage[rows_at(1 - at[CORE], piece), :]


def forward_call(scalars, rows, piece, h, weights, bias, attn, w_out):
    seq_len, width = h.shape
    cut = weights[0].shape[1] // 2
    seqs = len(weights)
    tile = 2 * piece
    half = seq_len // 2

    def kernel(at, h_ref, *refs):
        w_refs, (bias_ref, attn_ref, w_out_ref) = refs[:seqs], refs[seqs : seqs + 3]
        w_ref, fc_ref, act_ref, mine_ref, theirs_ref, stage = refs[seqs + 3 :]
        for k, ref in enumerate(w_refs):
            w_ref[rows_at(lax.rem(at[S] + k, seqs), rows), :] = ref[...]

        def step(t, carry):
            here = rows_at(t, tile)
            v = dot(h_ref[here, :], w_ref[:, :cut]) + bias_ref[...]
            fc_ref[here, :] = v
            act = (0.5 * v * (1.0 + jnp.tanh(ROOT * (v + CUBIC * (v * v * v))))).astype(bf16)
            act_ref[here, :] = act
            out = dot(attn_ref[here, :], w_out_ref[...]) + cols_dot(act, w_ref[:, cut:])
            split_rows(at, t, piece, out, stage, mine_ref, theirs_ref)
            return carry

        lax.fori_loop(0, seq_len // tile, step, 0)

    return call(
        kernel,
        [
            shape((width, 2 * cut)),
            shape((seq_len, cut), f32),
            shape((seq_len, cut)),
            shape((half, width)),
            shape((half, width)),
        ],
        [pltpu.VMEM((tile, width), bf16)],
        scalars,
        (h, *weights, bias, attn, w_out),
        cost=(4 * seq_len * width * cut, 0),
    )


def middle_call(scalars, piece, mine, theirs):
    half, width = mine.shape
    count = half // piece

    def kernel(at, mine_ref, theirs_ref, keep_ref, *sends):
        for k in range(count):
            here = rows_at(lax.rem(at[Z] + count - k, count), piece)
            value = mine_ref[here, :].astype(f32) + theirs_ref[here, :].astype(f32)
            if k == 0:
                keep_ref[...] = value
            else:
                sends[k - 1][...] = value.astype(bf16)

    return call(
        kernel,
        [shape((piece, width), f32)] + [shape((piece, width))] * (count - 1),
        [],
        scalars,
        (mine, theirs),
    )


def backward_call(scalars, pieces, weight, w_out, fc):
    piece, width = pieces[0].shape
    seq_len, cut = fc.shape
    own = w_out.shape[0]
    tile = min(256, seq_len)

    def kernel(at, *refs):
        n = len(pieces)
        dy_refs, (w_ref, w_out_ref, fc_ref), (dy_ref, dfc_ref, dattn_ref, sum_ref) = (
            refs[:n],
            refs[n : n + 3],
            refs[n + 3 :],
        )
        for ref, slot in slots(at, dy_refs):
            dy_ref[rows_at(slot, piece), :] = ref[...]
        sum_ref[...] = jnp.zeros_like(sum_ref)

        def step(t, carry):
            here = rows_at(t, tile)
            dy = dy_ref[here, :]
            v = fc_ref[here, :]
            square = v * v
            t_v = jnp.tanh(ROOT * (v + CUBIC * (square * v)))
            slope = 0.5 * (1.0 + t_v) + 0.5 * v * (1.0 - t_v * t_v) * (
                ROOT * (1.0 + (3.0 * CUBIC) * square)
            )
            dfc = (dot(dy, w_ref[:, cut:]) * slope).astype(bf16)
            dfc_ref[here, :] = dfc
            sum_ref[...] += jnp.sum(dfc.astype(f32), axis=0, keepdims=True)
            dattn_ref[here, :] = cols_dot(dy, w_out_ref[...]).astype(bf16)
            return carry

        lax.fori_loop(0, seq_len // tile, step, 0)

    return call(
        kernel,
        [shape((seq_len, width)), shape((seq_len, cut)), shape((seq_len, own)), shape((1, cut), f32)],
        [],
        scalars,
        (*pieces, weight, w_out, fc),
        cost=(2 * seq_len * width * cut, 0),
    )


def input_grad_call(scalars, piece, dfc, weight, dqkv, w_qkv, xhat):
    seq_len, cut = dfc.shape
    width = weight.shape[0]
    tile = 2 * piece
    half = seq_len // 2

    def kernel(at, dfc_ref, w_ref, dqkv_ref, w_qkv_ref, xhat_ref, mine_ref, theirs_ref, gain_ref, shift_ref, stage):
        gain_ref[...] = jnp.zeros_like(gain_ref)
        shift_ref[...] = jnp.zeros_like(shift_ref)

        def step(t, carry):
            here = rows_at(t, tile)
            value = cols_dot(dfc_ref[here, :], w_ref[:, :cut]) + cols_dot(
                dqkv_ref[here, :], w_qkv_ref[...]
            )
            gain_ref[...] += jnp.sum(value * xhat_ref[here, :].astype(f32), axis=0, keepdims=True)
            shift_ref[...] += jnp.sum(value, axis=0, keepdims=True)
            split_rows(at, t, piece, value, stage, mine_ref, theirs_ref)
            return carry

        lax.fori_loop(0, seq_len // tile, step, 0)

    return call(
        kernel,
        [shape((half, width)), shape((half, width)), shape((1, width), f32), shape((1, width), f32)],
        [pltpu.VMEM((tile, width), bf16)],
        scalars,
        (dfc, weight, dqkv, w_qkv, xhat),
        cost=(2 * seq_len * width * cut, 0),
    )


def split_fc_call(scalars, seqs, grad_fc1, grad_fc2):
    width, cut = grad_fc1.shape
    rows = width // seqs

    def kernel(at, one_ref, two_ref, *outs):
        for k, ref in enumerate(outs):
            here = rows_at(lax.rem(at[S] + seqs - k, seqs), rows)
            ref[:, :cut] = one_ref[here, :]
            ref[:, cut:] = two_ref[here, :]

    return call(kernel, [shape((rows, 2 * cut))] * seqs, [], scalars, (grad_fc1, grad_fc2))


def small_rows(share):
    return 5, (2 if share >= 10 else 1)


def put_small(block_ref, base, share, lane0, values):
    kinds, parts = small_rows(share)
    for kind, value in enumerate(values):
        high = value.astype(bf16)
        block_ref[base + kind : base + kind + 1, lane0 : lane0 + value.shape[1]] = high.astype(f32)
        if parts == 2:
            row = base + kinds + kind
            block_ref[row : row + 1, lane0 : lane0 + value.shape[1]] = value - high.astype(f32)


def split_qkv_call(scalars, seqs, share, group, heads, grad_qkv, grad_out, halves, vectors):
    width, total = grad_qkv.shape
    rows = width // seqs
    lanes = total + SMALL
    chunks = -(-width // lanes)
    out_rows = rows + chunks * share
    ctxs = rows // share

    def kernel(at, qkv_ref, out_grad_ref, *refs):
        half_refs, refs = refs[: group - 1], refs[group - 1 :]
        vector_refs, outs, stage, small = refs[:5], refs[5 : 5 + seqs], refs[-2], refs[-1]

        def put_out(slot, value):
            for j in range(chunks):
                upto = min(width - j * lanes, lanes)
                begin = rows + j * share
                stage[slot, begin : begin + share, :upto] = value[:, j * lanes : j * lanes + upto]

        for k in range(group):
            for i in range(heads):
                slot = (at[SUB] ^ k) * heads + i
                if k:
                    put_out(slot, half_refs[k - 1][i])
                else:
                    here = pl.ds(pl.multiple_of(i * HEAD_DIM + at[SUB] * share, share), share)
                    put_out(slot, out_grad_ref[here, :])
        small[...] = jnp.zeros_like(small)
        sizes = [ref.shape[1] // (seqs * ctxs) for ref in vector_refs]
        for seq in range(seqs):
            for ctx in range(ctxs):
                owner = seq * ctxs + ctx
                values = [
                    ref[:, owner * n : (owner + 1) * n] for ref, n in zip(vector_refs, sizes)
                ]
                put_small(small, ctx * share, share, 0, values)
            stage[seq, :rows, :total] = qkv_ref[seq * rows : (seq + 1) * rows, :]
            stage[seq, :rows, total:] = small[...].astype(bf16)
        for k, ref in enumerate(outs):
            ref[...] = stage[lax.rem(at[S] + seqs - k, seqs)]

    return call(
        kernel,
        [shape((out_rows, lanes))] * seqs,
        [pltpu.VMEM((seqs, out_rows, lanes), bf16), pltpu.VMEM((rows, SMALL), f32)],
        scalars,
        (grad_qkv, grad_out, *halves, *vectors),
    )


def sum_qkv_call(scalars, share, width, rows, pieces):
    lanes = pieces[0].shape[1]
    chunks = -(-width // lanes)
    kinds, parts = small_rows(share)
    ctxs = rows // share

    def kernel(at, *refs):
        in_refs, out_ref, w_out_ref, sums = refs[: len(pieces)], refs[-3], refs[-2], refs[-1]
        sums[...] = sum(ref[...].astype(f32) for ref in in_refs)
        for j in range(chunks):
            upto = min(width - j * lanes, lanes)
            begin = rows + j * share
            w_out_ref[:, j * lanes : j * lanes + upto] = sums[begin : begin + share, :upto]
        if parts == 2:
            for ctx in range(ctxs):
                base = ctx * share
                here = sums[base : base + kinds, lanes - SMALL :]
                left = sums[base + kinds : base + 2 * kinds, lanes - SMALL :]
                value = here + left
                high = value.astype(bf16).astype(f32)
                sums[base : base + kinds, lanes - SMALL :] = high
                sums[base + kinds : base + 2 * kinds, lanes - SMALL :] = value - high
        out_ref[...] = sums[:rows, :].astype(bf16)

    return call(
        kernel,
        [shape((rows, lanes)), shape((share, width), f32)],
        [pltpu.VMEM(pieces[0].shape, f32)],
        scalars,
        pieces,
    )


def home_fc_call(scalars, got):
    ctxs, share, double = got.shape
    cut = double // 2

    def kernel(at, got_ref, one_ref, two_ref):
        for ctx in range(ctxs):
            cols = slice(ctx * cut, (ctx + 1) * cut)
            one_ref[:, cols] = got_ref[ctx, :, :cut].astype(f32)
            two_ref[:, cols] = got_ref[ctx, :, cut:].astype(f32)

    return call(kernel, [shape((share, ctxs * cut), f32)] * 2, [], scalars, (got,))


def home_qkv_call(scalars, group, heads, lanes, width, got):
    ctxs, share, _ = got.shape
    total = 3 * heads * HEAD_DIM
    kinds, parts = small_rows(share)
    sizes = (share, share, share, 3 * share, 4 * share)

    def kernel(at, got_ref, out_ref, *small_refs):
        for ctx in range(ctxs):
            for part in range(3):
                for i in range(heads):
                    put = head_lanes(ctx, part, i, heads, group, lanes, width)
                    take = (part * heads + i) * HEAD_DIM
                    out_ref[:, put : put + HEAD_DIM] = got_ref[
                        ctx, :, take : take + HEAD_DIM
                    ].astype(f32)
        sums = sum(got_ref[ctx, :, total:].astype(f32) for ctx in range(ctxs))
        for kind, ref in enumerate(small_refs):
            value = sums[kind : kind + 1, :]
            if parts == 2:
                value = value + sums[kinds + kind : kinds + kind + 1, :]
            ref[...] = value[:, : sizes[kind]]

    return call(
        kernel,
        [shape((share, 3 * width), f32)] + [shape((1, n), f32) for n in sizes],
        [],
        scalars,
        (got,),
    )


def finish_call(scalars, x, dy, gain, keep, parts):
    def kernel(at, x_ref, dy_ref, gain_ref, keep_ref, *refs):
        *part_refs, out_ref = refs
        dh = keep_ref[...] + sum(ref[...].astype(f32) for ref in part_refs)
        here = x_ref[...].astype(f32)
        centred = here - jnp.mean(here, axis=1, keepdims=True)
        rstd = lax.rsqrt(jnp.mean(centred * centred, axis=1, keepdims=True) + norm_eps)
        xhat = centred * rstd
        scaled = dh * gain_ref[...]
        out_ref[...] = dy_ref[...].astype(f32) + rstd * (
            scaled
            - jnp.mean(scaled, axis=1, keepdims=True)
            - xhat * jnp.mean(scaled * xhat, axis=1, keepdims=True)
        )

    return call(kernel, [shape(x.shape, f32)], [], scalars, (x, dy, gain, keep, *parts))[0]


def body(
    block_in,
    cotangent,
    segments,
    ln_gain,
    ln_bias,
    w_qkv,
    b_qkv,
    w_out,
    b_out,
    w_fc1,
    b_fc1,
    w_fc2,
    b_fc2,
):
    seqs, ctxs = lax.axis_size("seq"), lax.axis_size("ctx")
    s, c = lax.axis_index("seq"), lax.axis_index("ctx")
    _, piece, width = block_in.shape
    seq_len = piece * ctxs
    share = w_qkv.shape[0]
    hidden = w_fc1.shape[1]
    cut = hidden // ctxs
    heads = HEADS // ctxs
    group = HEAD_DIM // share
    lanes = ctxs // group
    rows = ctxs * share
    zs = ctxs // 2
    sub, lane = c % group, c // group
    scalars = jnp.stack([c % 2, c // 2, s, sub, lane]).astype(jnp.int32)
    total = 3 * heads * HEAD_DIM
    x_here, dy_here = block_in[0], cotangent[0]

    def from_z(k):
        return [(i, ((i // 2 - k) % zs) * 2 + i % 2) for i in range(ctxs)]

    def from_s(k):
        return [(i, (i - k) % seqs) for i in range(seqs)]

    def partner(k):
        return [(i, i ^ k) for i in range(ctxs)]

    def along(axis, parts, pairs):
        return [lax.ppermute(part, axis, pair) for part, pair in zip(parts, pairs)]

    hops_z = [from_z(k) for k in range(1, zs)]
    hops_s = [from_s(k) for k in range(1, seqs)]
    hops_g = [partner(k) for k in range(1, group)]

    def spread_ctx(local):
        mine = [local] + along("ctx", [local] * (zs - 1), hops_z)
        return mine + along("ctx", mine, [partner(1)] * zs)

    def swap_ctx(blocks):
        return lax.all_to_all(blocks, "ctx", split_axis=0, concat_axis=0, tiled=True)

    packed = pack_call(
        scalars,
        group,
        heads,
        lanes,
        w_qkv,
        w_fc1,
        w_fc2,
        (ln_gain, ln_bias, b_out, b_fc2, b_qkv, b_fc1),
        segments,
    )
    got = swap_ctx(packed)
    wide = total + SMALL
    chunks = -(-width // wide)
    padded = jnp.pad(w_out, ((0, 0), (0, chunks * wide - width)))
    joint = jnp.concatenate(
        [got[:, :, :wide].reshape(rows, wide)]
        + [padded[:, j * wide : (j + 1) * wide] for j in range(chunks)]
    )
    joint = [joint] + along("seq", [joint] * (seqs - 1), hops_s)
    fc_here = got[:, :, wide:].reshape(rows, 2 * cut)
    w_fc = [fc_here] + along("seq", [fc_here] * (seqs - 1), hops_s)
    x_all = spread_ctx(x_here)
    dy_all = spread_ctx(dy_here)

    seg = got[:, 6, total : total + piece].reshape(1, seq_len)
    first = jnp.zeros((1, seq_len), jnp.int32)
    for name in range(1, 4):
        begin = jnp.sum((seg < name).astype(jnp.int32))
        first = jnp.where(seg >= name, begin, first)
    pos = lax.broadcasted_iota(jnp.int32, (1, seq_len), 1) - first
    freq = jnp.power(f32(10000.0), -2.0 * jnp.arange(HALF, dtype=f32) / ROT)
    angle = (pos.astype(f32) * freq[:, None]).T
    cos_t, sin_t = jnp.cos(angle), jnp.sin(angle)
    ones = jnp.ones((seq_len, HEAD_DIM - ROT), f32)
    zero = jnp.zeros((seq_len, HEAD_DIM - ROT), f32)
    empty = jnp.zeros((seq_len, HALF), f32)
    tables = (
        jnp.concatenate([cos_t, cos_t, ones] * heads, axis=1),
        jnp.concatenate([sin_t, empty, zero] * heads, axis=1),
        jnp.concatenate([empty, sin_t, zero] * heads, axis=1),
    )

    smalls, *out_parts = spread_out_call(scalars, joint, rows, share, width, group, heads)
    out_parts = out_parts[:1] + along("ctx", out_parts[1:], hops_g)
    smalls = smalls.reshape(seqs * ctxs, share, SMALL)

    def small_part(at, count):
        return smalls[:, at, : count * share].reshape(-1)

    gain = small_part(0, 1).astype(f32).reshape(1, width)
    shift = small_part(1, 1).astype(f32).reshape(1, width)
    bias_out = small_part(2, 1).astype(f32) + small_part(3, 1).astype(f32)
    bias_qkv = small_part(4, 3).reshape(3, group, heads, lanes, HEAD_DIM)
    bias_qkv = lax.dynamic_slice(bias_qkv, (0, sub, 0, lane, 0), (3, 1, heads, 1, HEAD_DIM))
    bias_qkv = bias_qkv.reshape(1, total).astype(f32)
    bias_fc1 = lax.dynamic_slice_in_dim(small_part(5, 4), c * cut, cut, 0)
    bias_fc1 = bias_fc1.astype(f32).reshape(1, cut)
    ordered = jnp.stack(out_parts)[jnp.stack([sub ^ k for k in range(group)])]
    w_out_c = ordered.transpose(1, 0, 2, 3).reshape(heads * HEAD_DIM, width)

    block = min(256, seq_len)
    h, xhat, attn, lse, kept, w_qkv_c = attend_call(
        scalars, block, heads, rows, x_all, gain, shift, joint, bias_qkv, tables, first
    )
    w_fc_c, fc, act, out_mine, out_theirs = forward_call(
        scalars, rows, piece, h, w_fc, bias_fc1, attn, w_out_c
    )
    out_theirs = along("ctx", [out_theirs], [partner(1)])[0]
    out_keep, *out_sends = middle_call(scalars, piece, out_mine, out_theirs)
    out_parts = along("ctx", out_sends, hops_z)
    block_out = x_here.astype(f32) + out_keep + bias_out
    for part in out_parts:
        block_out = block_out + part.astype(f32)
    block_out = block_out.astype(bf16)

    dy, dfc, dattn, sum_fc1 = backward_call(scalars, dy_all, w_fc_c, w_out_c, fc)
    grad_fc1 = rows_dot(h, dfc).astype(bf16)
    grad_fc2 = rows_dot(dy, act).astype(bf16)
    fc_parts = split_fc_call(scalars, seqs, grad_fc1, grad_fc2)
    fc_parts = fc_parts[:1] + along("seq", fc_parts[1:], hops_s)
    grad_out = rows_dot(attn, dy).astype(bf16)
    blocks = grad_out.reshape(heads, group, share, width)
    halves = [lax.dynamic_index_in_dim(blocks, sub ^ k, 1, keepdims=False) for k in range(1, group)]
    halves = along("ctx", halves, hops_g)
    dqkv, sum_qkv = attend_back_call(
        scalars, block, heads, kept, dattn, lse, tables, first, (fc_parts[0],)
    )
    dh_mine, dh_theirs, sum_gain, sum_shift = input_grad_call(
        scalars, piece, dfc, w_fc_c, dqkv, w_qkv_c, xhat
    )
    dh_theirs = along("ctx", [dh_theirs], [partner(1)])[0]
    grad_qkv = rows_dot(h, dqkv).astype(bf16)
    full_qkv = lax.dynamic_update_slice(
        jnp.zeros((3, group, heads, lanes, HEAD_DIM), f32),
        sum_qkv.reshape(3, 1, heads, 1, HEAD_DIM),
        (0, sub, 0, lane, 0),
    ).reshape(1, 3 * width)
    full_fc1 = lax.dynamic_update_slice(
        jnp.zeros((1, hidden), f32), sum_fc1, (0, c * cut)
    )
    sum_y = jnp.sum(dy_here.astype(f32), axis=0, keepdims=True)
    qkv_parts = split_qkv_call(
        scalars,
        seqs,
        share,
        group,
        heads,
        grad_qkv,
        grad_out,
        halves,
        (sum_gain, sum_shift, sum_y, full_qkv, full_fc1),
    )
    qkv_parts = qkv_parts[:1] + along("seq", qkv_parts[1:], hops_s)
    dh_keep, *dh_sends = middle_call(scalars, piece, dh_mine, dh_theirs)
    dh_parts = along("ctx", dh_sends, hops_z)

    fc_sum = sum(part.astype(f32) for part in fc_parts).astype(bf16)
    fc_home = swap_ctx(fc_sum.reshape(ctxs, share, 2 * cut))
    qkv_sum, out_wout = sum_qkv_call(scalars, share, width, rows, qkv_parts)
    qkv_home = swap_ctx(qkv_sum.reshape(ctxs, share, wide))
    grad_in = finish_call(scalars, x_here, dy_here, gain, dh_keep, dh_parts)
    out_wfc1, out_wfc2 = home_fc_call(scalars, fc_home)
    out_wqkv, *small = home_qkv_call(scalars, group, heads, lanes, width, qkv_home)
    small = [value.reshape(-1) for value in small]
    return (
        block_out[None],
        grad_in[None],
        small[0],
        small[1],
        out_wqkv,
        small[3],
        out_wout,
        small[2],
        out_wfc1,
        small[4],
        out_wfc2,
        small[2],
    )


def solution(mesh):
    both = ("seq", "ctx")
    tokens, flat, matrix = P("seq", "ctx", None), P(both), P(both, None)
    in_specs = (tokens, tokens, P("seq", "ctx"), flat, flat) + (matrix, flat) * 4
    out_specs = (tokens, tokens, flat, flat) + (matrix, flat) * 4
    return jax.shard_map(body, mesh=mesh, in_specs=in_specs, out_specs=out_specs, check_vma=False)
```

```python
import math

import jax
import jax.numpy as jnp
from jax import lax
from jax.experimental import pallas as pl
from jax.experimental.pallas import tpu as pltpu
from jax.sharding import PartitionSpec as P

HEADS = 16
HEAD_DIM = 64
ROT = 16
HALF = ROT // 2
SMALL = 128

norm_eps = 1e-05
big_negative = -1e30
f32 = jnp.float32
bf16 = jnp.bfloat16


def dot(left, right):
    return lax.dot_general(left, right, (((1,), (0,)), ((), ())), preferred_element_type=f32)


def rows_dot(left, right):
    return lax.dot_general(left, right, (((0,), (0,)), ((), ())), preferred_element_type=f32)


def cols_dot(left, right):
    return lax.dot_general(left, right, (((1,), (1,)), ((), ())), preferred_element_type=f32)


def shape(dims, kind=bf16):
    return jax.ShapeDtypeStruct(dims, kind)


def held(array):
    *lead, low, high = (1, 1, *array.shape)
    size = jnp.dtype(array.dtype).itemsize
    lines = 32 // size
    return math.prod(lead) * (-(-low // lines) * lines) * (-(-high // 128) * 128) * size


def call(kernel, outs, scratch, scalars, operands, far=(), far_outs=(), after=(), room=3, cost=None):
    vmem = pl.BlockSpec(memory_space=pltpu.VMEM)
    hbm = pl.BlockSpec(memory_space=pl.ANY)
    count = len(operands) + len(far)

    def wrapped(*refs):
        kernel(refs[0], *refs[1 : 1 + count], *refs[1 + count + len(after) :])

    flops, moved = cost or (0, 0)
    moved = moved or sum(held(a) for a in [*operands, *far])
    limit = None
    if room:
        limit = sum(held(a) for a in scratch if "sem" not in str(a.dtype)) + (room << 20)
    results = pl.pallas_call(
        wrapped,
        in_specs=[pl.BlockSpec(memory_space=pltpu.SMEM)]
        + [vmem] * len(operands)
        + [hbm] * len(far)
        + [pl.BlockSpec(memory_space=pl.ANY)] * len(after),
        out_specs=[vmem] * len(outs) + [hbm] * len(far_outs),
        out_shape=[*outs, *far_outs],
        scratch_shapes=scratch,
        compiler_params=pltpu.CompilerParams(vmem_limit_bytes=limit),
        cost_estimate=pl.CostEstimate(flops=flops, bytes_accessed=moved, transcendentals=0),
    )(scalars, *operands, *far, *after)
    return list(results)


def start_all(pairs, sems):
    copies = [
        pltpu.make_async_copy(source, target, sems.at[at]) for at, (source, target) in enumerate(pairs)
    ]
    for copy in copies:
        copy.start()
    return copies


def wait_all(copies):
    for copy in copies:
        copy.wait()


def sems(count):
    return pltpu.SemaphoreType.DMA((count,))


def rows_at(index, count):
    return pl.ds(pl.multiple_of(index * count, count), count)


CORE, Z, S, SUB, LANE = range(5)


def padded(total):
    return -(-total // 128) * 128


def head_lanes(to, part, i, heads, group, lanes, width):
    return part * width + (((to % group) * heads + i) * lanes + to // group) * HEAD_DIM


def pack_call(scalars, group, heads, lanes, w_qkv, w_fc1, w_fc2, vectors, seg):
    share, hidden = w_fc1.shape
    count = group * lanes
    cut = hidden // count
    total = 3 * heads * HEAD_DIM
    width = w_qkv.shape[1] // 3

    def kernel(_, qkv_ref, fc1_ref, fc2_ref, *refs):
        *small_refs, seg_ref, out_ref, small = refs
        small[...] = jnp.zeros_like(small)
        for at, ref in enumerate(small_refs):
            small[at : at + 1, : ref.shape[0]] = ref[...].astype(f32).reshape(1, -1)
        at = len(small_refs)
        small[at : at + 1, : seg_ref.shape[1]] = seg_ref[...].astype(f32)
        rounded = small[...].astype(bf16)
        for to in range(count):
            for part in range(3):
                for i in range(heads):
                    begin = head_lanes(to, part, i, heads, group, lanes, width)
                    put = (part * heads + i) * HEAD_DIM
                    out_ref[to, :, put : put + HEAD_DIM] = qkv_ref[:, begin : begin + HEAD_DIM]
            base = padded(total) + SMALL
            out_ref[to, :, base - SMALL : base] = rounded
            out_ref[to, :, base : base + cut] = fc1_ref[:, to * cut : (to + 1) * cut]
            out_ref[to, :, base + cut :] = fc2_ref[:, to * cut : (to + 1) * cut]

    return call(
        kernel,
        [shape((count, share, padded(total) + SMALL + 2 * cut))],
        [pltpu.VMEM((share, SMALL), f32)],
        scalars,
        (w_qkv, w_fc1, w_fc2, *vectors, seg),
        room=0,
    )[0]


def spread_out_call(scalars, pieces, rows, share, width, group, heads, lanes, cut):
    seqs = len(pieces)
    wide = pieces[0].shape[1]
    chunks = -(-width // wide)
    total = 3 * heads * HEAD_DIM
    ctxs = rows // share
    sizes = (share, share, share, share, 3 * share, 4 * share)

    def kernel(at, *refs):
        far_refs, refs = refs[:seqs], refs[seqs:]
        *refs, local, sem = refs
        wait_all(start_all([(ref, local.at[k]) for k, ref in enumerate(far_refs)], sem))
        in_refs = [local.at[k] for k in range(seqs)]
        gain_ref, shift_ref, out_ref, qkv_ref, fc_ref = refs[:5]
        part_refs, stage, rows_refs, full = refs[5 : 5 + group], refs[5 + group], refs[6 + group : -1], refs[-1]
        for k, ref in enumerate(in_refs):
            slot = lax.rem(at[S] + k, seqs)
            for ctx in range(ctxs):
                block = ref[ctx * share : ctx * share + len(sizes), wide - SMALL :].astype(f32)
                for kind, n in enumerate(sizes):
                    rows_refs[kind][slot, :, ctx * n : (ctx + 1) * n] = block[kind : kind + 1, :n]
            for j in range(chunks):
                upto = min(width - j * wide, wide)
                begin = rows + j * share
                stage[slot, :, j * wide : j * wide + upto] = ref[begin : begin + share, :upto]
        for seq in range(seqs):
            cols = slice(seq * rows, (seq + 1) * rows)
            gain_ref[:, cols] = rows_refs[0][seq]
            shift_ref[:, cols] = rows_refs[1][seq]
            out_ref[:, cols] = rows_refs[2][seq] + rows_refs[3][seq]
            full[:, 3 * seq * rows : 3 * (seq + 1) * rows] = rows_refs[4][seq]
        for part in range(3):
            for i in range(heads):
                head = (at[SUB] * heads + i) * lanes + at[LANE]
                pair = full[:, pl.ds(pl.multiple_of(part * width + head // 2 * 128, 128), 128)]
                put = (part * heads + i) * HEAD_DIM
                low = jnp.full((1, HEAD_DIM), lax.rem(head, 2), jnp.int32) == 0
                qkv_ref[:, put : put + HEAD_DIM] = jnp.where(
                    low, pair[:, :HEAD_DIM], pair[:, HEAD_DIM:]
                )
        per_seq = 4 * rows
        begin = (at[LANE] * group + at[SUB]) * cut
        fc_ref[...] = rows_refs[5][
            begin // per_seq, :, pl.ds(pl.multiple_of(lax.rem(begin, per_seq), 128), cut)
        ]
        for k, ref in enumerate(part_refs):
            for i in range(heads):
                ref[i] = stage[(at[SUB] ^ k) * heads + i]

    return call(
        kernel,
        [shape((1, width), f32)] * 3
        + [shape((1, total), f32), shape((1, cut), f32)]
        + [shape((heads, share, width))] * group,
        [pltpu.VMEM((seqs, share, width), bf16)]
        + [pltpu.VMEM((seqs, 1, ctxs * n), f32) for n in sizes]
        + [pltpu.VMEM((1, 3 * width), f32), pltpu.VMEM((seqs, *pieces[0].shape), bf16), sems(seqs)],
        scalars,
        (),
        far=pieces,
    )


def tables_call(scalars, joint, rows, share, piece):
    ctxs = rows // share
    seq_len = ctxs * piece
    total = joint.shape[1] - SMALL
    powers = [float(10000.0 ** (-2.0 * i / ROT)) for i in range(HALF)]

    def kernel(at, far_ref, first_ref, cos_ref, sin_ref, seg_ref, joint_ref, sem):
        wait_all(start_all([(far_ref, joint_ref)], sem))
        for ctx in range(ctxs):
            block = joint_ref[ctx * share : ctx * share + 8, total : total + piece].astype(f32)
            seg_ref[:, ctx * piece : (ctx + 1) * piece] = block[6:7]
        seg = seg_ref[...]
        first = jnp.zeros((1, seq_len), f32)
        for name in range(1, 4):
            begin = jnp.sum((seg < name).astype(f32), axis=1, keepdims=True)
            first = jnp.where(seg >= name, begin, first)
        first_ref[...] = first.astype(jnp.int32)
        pos = lax.broadcasted_iota(jnp.int32, (HALF, seq_len), 1).astype(f32) - first
        which = lax.broadcasted_iota(jnp.int32, (HALF, seq_len), 0)
        freq = jnp.full((HALF, seq_len), powers[0], f32)
        for i in range(1, HALF):
            freq = jnp.where(which == i, powers[i], freq)
        angle = pos * freq
        cos_ref[...] = jnp.cos(angle)
        sin_ref[...] = jnp.sin(angle)

    return call(
        kernel,
        [shape((1, seq_len), jnp.int32), shape((HALF, seq_len), f32), shape((HALF, seq_len), f32)],
        [pltpu.VMEM((1, seq_len), f32), pltpu.VMEM(joint.shape, bf16), sems(1)],
        scalars,
        (),
        far=(joint,),
    )


def rope_t(x_t, cos_t, sin_t):
    parts = []
    for base in range(0, x_t.shape[0], HEAD_DIM):
        one, two = x_t[base : base + HALF], x_t[base + HALF : base + ROT]
        parts += [
            one * cos_t - two * sin_t,
            two * cos_t + one * sin_t,
            x_t[base + ROT : base + HEAD_DIM],
        ]
    return jnp.concatenate(parts, axis=0)


def scores_of(keys, queries_t, first, begin, here, limit):
    raw = dot(keys[:limit], queries_t[:, begin : begin + here])
    first = first[:, begin : begin + here]
    key_at = lax.broadcasted_iota(jnp.int32, (here, here), 0)
    query_at = lax.broadcasted_iota(jnp.int32, (here, here), 1)
    causal = (key_at <= query_at) & (key_at + begin >= first)
    parts = []
    if begin:
        early = lax.broadcasted_iota(jnp.int32, (begin, here), 0) >= first
        parts.append(jnp.where(early, raw[:begin], big_negative))
    parts.append(jnp.where(causal, raw[begin:], big_negative))
    return jnp.concatenate(parts, axis=0) if begin else parts[0]


def slots(at, refs):
    count = len(refs) // 2
    for k in range(count):
        here = 2 * lax.rem(at[Z] + k, count)
        yield refs[k], here + at[CORE]
        yield refs[count + k], here + 1 - at[CORE]


def attend_call(scalars, block, heads, rows, pieces, gain, shift, weights, bias, tables):
    piece, width = pieces[0].shape
    seq_len = piece * len(pieces)
    seqs = len(weights)
    total = 3 * heads * HEAD_DIM
    own = heads * HEAD_DIM
    tile = min(256, seq_len)

    def kernel(at, *refs):
        n = len(pieces)
        gain_ref, shift_ref, bias_ref, first_ref, cos_ref, sin_ref = refs[:6]
        x_refs, w_refs = refs[6 : 6 + n], refs[6 + n : 6 + n + seqs]
        h_ref, xhat_ref, out_ref, lse_ref, kept_ref, turned_ref, w_ref = refs[
            6 + n + seqs : 13 + n + seqs
        ]
        x_all, qkv, out_t, sem = refs[13 + n + seqs :]
        pairs = [(ref, x_all.at[rows_at(slot, piece), :]) for ref, slot in slots(at, x_refs)]
        pairs += [
            (ref.at[:rows, : padded(total)], w_ref.at[rows_at(lax.rem(at[S] + k, seqs), rows), :])
            for k, ref in enumerate(w_refs)
        ]
        wait_all(start_all(pairs, sem))

        def norm_tile(t, carry):
            here = rows_at(t, tile)
            x = x_all[here, :].astype(f32)
            centred = x - jnp.mean(x, axis=1, keepdims=True)
            rstd = lax.rsqrt(jnp.mean(centred * centred, axis=1, keepdims=True) + norm_eps)
            xhat = centred * rstd
            xhat_ref[here, :] = xhat.astype(bf16)
            h = (xhat * gain_ref[...] + shift_ref[...]).astype(bf16)
            h_ref[here, :] = h
            qkv[here, :] = dot(h, w_ref[:, :total]) + bias_ref[...]
            return carry

        lax.fori_loop(0, seq_len // tile, norm_tile, 0)
        cos_t, sin_t = cos_ref[...], sin_ref[...]
        q_t = rope_t(qkv[:, :own].T, cos_t, sin_t) * 0.125
        k_t = rope_t(qkv[:, own : 2 * own].T, cos_t, sin_t)
        v = qkv[:, 2 * own :]
        kb = k_t.T.astype(bf16)
        kept_ref[:, :own] = q_t.T.astype(bf16)
        kept_ref[:, own : 2 * own] = kb
        kept_ref[:, 2 * own :] = v.astype(bf16)
        q_t = q_t.astype(bf16)
        v_t = v.T.astype(bf16)
        turned_ref[:own] = q_t
        turned_ref[own:] = k_t.astype(bf16)
        begins = first_ref[...]
        for head in range(heads):
            lanes = slice(head * HEAD_DIM, (head + 1) * HEAD_DIM)
            keys, queries_t, values_t = kb[:, lanes], q_t[lanes], v_t[lanes]
            for begin in range(0, seq_len, block):
                limit = begin + block
                scores = scores_of(keys, queries_t, begins, begin, block, limit)
                top = jnp.max(scores, axis=0, keepdims=True)
                expd = jnp.exp(scores - top)
                sums = jnp.sum(expd, axis=0, keepdims=True)
                out = dot(values_t[:, :limit], expd.astype(bf16))
                out_t[lanes, begin:limit] = out * (1.0 / sums)
                lse_ref[head : head + 1, begin:limit] = top + jnp.log(sums)
        out_ref[...] = out_t[...].T.astype(bf16)

    return call(
        kernel,
        [
            shape((seq_len, width)),
            shape((seq_len, width)),
            shape((seq_len, own)),
            shape((heads, seq_len), f32),
            shape((seq_len, total)),
            shape((2 * own, seq_len)),
            shape((width, padded(total))),
        ],
        [
            pltpu.VMEM((seq_len, width), bf16),
            pltpu.VMEM((seq_len, total), f32),
            pltpu.VMEM((own, seq_len), f32),
            sems(len(pieces) + seqs),
        ],
        scalars,
        (gain, shift, bias, *tables),
        far=(*pieces, *weights),
        room=8 * (seq_len // 1024) ** 2,
        cost=(4 * seq_len * width * total, 0),
    )


def attend_back_call(scalars, block, heads, kept, turned, grad, lse, tables, after):
    seq_len, total = kept.shape
    own = total // 3

    def kernel(
        at, kept_ref, turned_ref, grad_ref, lse_ref, first_ref, cos_ref, sin_ref, out_ref, sum_ref, dq_t, dk, dv
    ):
        q = kept_ref[:, :own]
        k = kept_ref[:, own : 2 * own]
        v = kept_ref[:, 2 * own :]
        grad = grad_ref[...]
        q_t, k_t = turned_ref[:own], turned_ref[own:]
        grad_t = grad.astype(f32).T.astype(bf16)
        begins = first_ref[...]
        for head in range(heads):
            lanes = slice(head * HEAD_DIM, (head + 1) * HEAD_DIM)
            q_h, k_h, v_h, grad_h = q[:, lanes], k[:, lanes], v[:, lanes], grad[:, lanes]
            for begin in reversed(range(0, seq_len, block)):
                limit = begin + block
                scores = scores_of(k_h, q_t[lanes], begins, begin, block, limit)
                probs = jnp.exp(scores - lse_ref[head : head + 1, begin:limit])
                grad_p = dot(v_h[:limit], grad_t[lanes, begin:limit])
                delta = jnp.sum(probs * grad_p, axis=0, keepdims=True)
                grad_s = (probs * (grad_p - delta)).astype(bf16)
                dk_here = dot(grad_s, q_h[begin:limit])
                dv_here = dot(probs.astype(bf16), grad_h[begin:limit])
                if limit == seq_len:
                    dk[head] = dk_here
                    dv[head] = dv_here
                else:
                    dk[head, :limit] += dk_here
                    dv[head, :limit] += dv_here
                dq_t[lanes, begin:limit] = dot(k_t[lanes, :limit], grad_s)
        cos_t, sin_t = cos_ref[...], -sin_ref[...]
        dk_all = jnp.concatenate([dk[head] for head in range(heads)], axis=1)
        dv_all = jnp.concatenate([dv[head] for head in range(heads)], axis=1)
        for part, value in (
            (0, rope_t(dq_t[...] * 0.125, cos_t, sin_t).T),
            (1, rope_t(dk_all.T, cos_t, sin_t).T),
            (2, dv_all),
        ):
            rounded = value.astype(bf16)
            cols = slice(part * own, (part + 1) * own)
            out_ref[:, cols] = rounded
            sum_ref[:, cols] = jnp.sum(rounded.astype(f32), axis=0, keepdims=True)

    return call(
        kernel,
        [shape((seq_len, total)), shape((1, total), f32)],
        [
            pltpu.VMEM((own, seq_len), f32),
            pltpu.VMEM((heads, seq_len, HEAD_DIM), f32),
            pltpu.VMEM((heads, seq_len, HEAD_DIM), f32),
        ],
        scalars,
        (kept, turned, grad, lse, *tables),
        after=after,
        room=8 * (seq_len // 1024) ** 2,
        cost=(10 * seq_len * seq_len * own, 0),
    )


ROOT = 0.7978845608028654
CUBIC = 0.044715


def split_rows(at, z, piece, value, stage, mine_ref, theirs_ref, sem):
    stage[z] = value.astype(bf16)
    mine_ref[rows_at(z, piece), :] = stage[z, rows_at(at[CORE], piece), :]
    out_rows(at, z, piece, stage, theirs_ref, sem).start()


def out_rows(at, z, piece, stage, theirs_ref, sem):
    return pltpu.make_async_copy(
        stage.at[z, rows_at(1 - at[CORE], piece), :], theirs_ref.at[rows_at(z, piece), :], sem.at[z]
    )


def forward_call(scalars, rows, piece, h, weights, bias, attn, out_parts):
    seq_len, width = h.shape
    cut = weights[0].shape[1] // 2
    seqs = len(weights)
    tile = 2 * piece
    half = seq_len // 2
    count = seq_len // tile

    heads, share, _ = out_parts[0].shape
    group = len(out_parts)

    def kernel(at, h_ref, bias_ref, attn_ref, *refs):
        w_refs, part_refs, refs = refs[:seqs], refs[seqs : seqs + group], refs[seqs + group :]
        w_ref, slope_ref, act_ref, mine_ref, w_out_ref, theirs_ref, stage, sem, sem_out = refs
        pairs = [
            (ref, w_ref.at[rows_at(lax.rem(at[S] + k, seqs), rows), :])
            for k, ref in enumerate(w_refs)
        ]
        for k, ref in enumerate(part_refs):
            for i in range(heads):
                begin = i * HEAD_DIM + (at[SUB] ^ k) * share
                here = pl.ds(pl.multiple_of(begin, share), share)
                pairs.append((ref.at[i], w_out_ref.at[here, :]))
        wait_all(start_all(pairs, sem))

        def step(t, carry):
            here = rows_at(t, tile)
            v = dot(h_ref[here, :], w_ref[:, :cut]) + bias_ref[...]
            square = v * v
            t_v = jnp.tanh(ROOT * (v + CUBIC * (square * v)))
            halved = 0.5 * (1.0 + t_v)
            act = (v * halved).astype(bf16)
            act_ref[here, :] = act
            slope = halved + 0.5 * v * (1.0 - t_v * t_v) * (ROOT * (1.0 + (3.0 * CUBIC) * square))
            slope_ref[here, :] = slope.astype(bf16)
            out = dot(attn_ref[here, :], w_out_ref[...]) + cols_dot(act, w_ref[:, cut:])
            split_rows(at, t, piece, out, stage, mine_ref, theirs_ref, sem_out)
            return carry

        lax.fori_loop(0, count, step, 0)
        wait_all([out_rows(at, z, piece, stage, theirs_ref, sem_out) for z in range(count)])

    return call(
        kernel,
        [
            shape((width, 2 * cut)),
            shape((seq_len, cut)),
            shape((seq_len, cut)),
            shape((half, width)),
            shape((heads * HEAD_DIM, width)),
        ],
        [pltpu.VMEM((count, tile, width), bf16), sems(seqs + group * heads), sems(count)],
        scalars,
        (h, bias, attn),
        far=(*weights, *out_parts),
        far_outs=[shape((half, width))],
        cost=(4 * seq_len * width * cut, 0),
    )


def middle_call(scalars, piece, mine, theirs):
    half, width = mine.shape
    count = half // piece

    def kernel(at, mine_ref, theirs_ref, keep_ref, *refs):
        sends, (got, made, sem, sem_out) = refs[: count - 1], refs[count - 1 :]
        here = [rows_at(lax.rem(at[Z] + count - k, count), piece) for k in range(count)]
        order = [*range(1, count), 0]
        copies = start_all([(theirs_ref.at[here[k], :], got.at[k]) for k in order], sem)
        outs = []
        for copy, k in zip(copies, order):
            copy.wait()
            value = mine_ref[here[k], :].astype(f32) + got[k].astype(f32)
            if k == 0:
                keep_ref[...] = value
            else:
                made[k - 1] = value.astype(bf16)
                out = pltpu.make_async_copy(made.at[k - 1], sends[k - 1], sem_out.at[k - 1])
                out.start()
                outs.append(out)
        wait_all(outs)

    return call(
        kernel,
        [shape((piece, width), f32)],
        [
            pltpu.VMEM((count, piece, width), bf16),
            pltpu.VMEM((count - 1, piece, width), bf16),
            sems(count),
            sems(count - 1),
        ],
        scalars,
        (mine,),
        far=(theirs,),
        far_outs=[shape((piece, width))] * (count - 1),
    )


def backward_call(scalars, pieces, weight, w_out, slope):
    piece, width = pieces[0].shape
    seq_len, cut = slope.shape
    own = w_out.shape[0]
    tile = min(256, seq_len)

    def kernel(at, *refs):
        n = len(pieces)
        (w_ref, w_out_ref, slope_ref), dy_refs = refs[:3], refs[3 : 3 + n]
        dy_ref, dfc_ref, dattn_ref, sum_ref, sem = refs[3 + n :]
        pairs = [(ref, dy_ref.at[rows_at(slot, piece), :]) for ref, slot in slots(at, dy_refs)]
        wait_all(start_all(pairs, sem))
        sum_ref[...] = jnp.zeros_like(sum_ref)

        def step(t, carry):
            here = rows_at(t, tile)
            dy = dy_ref[here, :]
            dfc = (dot(dy, w_ref[:, cut:]) * slope_ref[here, :].astype(f32)).astype(bf16)
            dfc_ref[here, :] = dfc
            sum_ref[...] += jnp.sum(dfc.astype(f32), axis=0, keepdims=True)
            dattn_ref[here, :] = cols_dot(dy, w_out_ref[...]).astype(bf16)
            return carry

        lax.fori_loop(0, seq_len // tile, step, 0)

    return call(
        kernel,
        [shape((seq_len, width)), shape((seq_len, cut)), shape((seq_len, own)), shape((1, cut), f32)],
        [sems(len(pieces))],
        scalars,
        (weight, w_out, slope),
        far=pieces,
        cost=(2 * seq_len * width * cut, 0),
    )


def input_grad_call(scalars, piece, dfc, weight, dqkv, w_qkv, xhat):
    seq_len, cut = dfc.shape
    width = weight.shape[0]
    total = dqkv.shape[1]
    tile = 2 * piece
    half = seq_len // 2
    count = seq_len // tile

    def kernel(at, dfc_ref, w_ref, dqkv_ref, w_qkv_ref, xhat_ref, mine_ref, gain_ref, shift_ref, theirs_ref, stage, sem_out):
        gain_ref[...] = jnp.zeros_like(gain_ref)
        shift_ref[...] = jnp.zeros_like(shift_ref)

        def step(t, carry):
            here = rows_at(t, tile)
            value = cols_dot(dfc_ref[here, :], w_ref[:, :cut]) + cols_dot(
                dqkv_ref[here, :], w_qkv_ref[:, :total]
            )
            gain_ref[...] += jnp.sum(value * xhat_ref[here, :].astype(f32), axis=0, keepdims=True)
            shift_ref[...] += jnp.sum(value, axis=0, keepdims=True)
            split_rows(at, t, piece, value, stage, mine_ref, theirs_ref, sem_out)
            return carry

        lax.fori_loop(0, count, step, 0)
        wait_all([out_rows(at, z, piece, stage, theirs_ref, sem_out) for z in range(count)])

    return call(
        kernel,
        [shape((half, width)), shape((1, width), f32), shape((1, width), f32)],
        [pltpu.VMEM((count, tile, width), bf16), sems(count)],
        scalars,
        (dfc, weight, dqkv, w_qkv, xhat),
        far_outs=[shape((half, width))],
        cost=(2 * seq_len * width * cut, 0),
    )


def split_fc_call(scalars, seqs, grad_fc1, grad_fc2):
    width, cut = grad_fc1.shape
    rows = width // seqs

    def kernel(at, one_ref, two_ref, *refs):
        *outs, sem = refs
        pairs = []
        for k, ref in enumerate(outs):
            here = rows_at(lax.rem(at[S] + seqs - k, seqs), rows)
            pairs += [
                (one_ref.at[here, :], ref.at[:, :cut]),
                (two_ref.at[here, :], ref.at[:, cut:]),
            ]
        wait_all(start_all(pairs, sem))

    return call(
        kernel,
        [],
        [sems(2 * seqs)],
        scalars,
        (grad_fc1, grad_fc2),
        far_outs=[shape((rows, 2 * cut))] * seqs,
    )


def sum_fc_call(scalars, pieces):
    rows, lanes = pieces[0].shape
    count = len(pieces)
    tiles = 2
    tile = rows // tiles

    def kernel(at, *refs):
        far_refs, (out_ref, got, made, sem, sem_out) = refs[:count], refs[count:]
        starts = [slice(t * tile, (t + 1) * tile) for t in range(tiles)]
        copies = start_all(
            [(ref.at[here, :], got.at[k, here, :]) for here in starts for k, ref in enumerate(far_refs)],
            sem,
        )
        outs = []
        for t, here in enumerate(starts):
            wait_all(copies[t * count : (t + 1) * count])
            made[here, :] = sum(got[k, here, :].astype(f32) for k in range(count)).astype(bf16)
            out = pltpu.make_async_copy(made.at[here, :], out_ref.at[here, :], sem_out.at[t])
            out.start()
            outs.append(out)
        wait_all(outs)

    return call(
        kernel,
        [],
        [
            pltpu.VMEM((count, rows, lanes), bf16),
            pltpu.VMEM((rows, lanes), bf16),
            sems(tiles * count),
            sems(tiles),
        ],
        scalars,
        (),
        far=pieces,
        far_outs=[shape((rows, lanes))],
    )[0]


def small_rows(share):
    return 5, (2 if share >= 10 else 1)


def put_small(block_ref, base, share, lane0, values):
    kinds, parts = small_rows(share)
    for kind, value in enumerate(values):
        high = value.astype(bf16)
        block_ref[base + kind : base + kind + 1, lane0 : lane0 + value.shape[1]] = high.astype(f32)
        if parts == 2:
            row = base + kinds + kind
            block_ref[row : row + 1, lane0 : lane0 + value.shape[1]] = value - high.astype(f32)


def split_qkv_call(scalars, seqs, share, group, heads, lanes_c, grad_qkv, grad_out, halves, vectors):
    width, total = grad_qkv.shape
    rows = width // seqs
    lanes = padded(total) + SMALL
    chunks = -(-width // lanes)
    out_rows = rows + chunks * share
    ctxs = rows // share

    def kernel(at, qkv_ref, out_grad_ref, *refs):
        half_refs, refs = refs[: group - 1], refs[group - 1 :]
        (gain_ref, shift_ref, dy_ref, sum_qkv_ref, sum_fc_ref) = refs[:5]
        outs, (stage, small, full_y, full_qkv, full_fc, sem) = refs[5 : 5 + seqs], refs[5 + seqs :]
        full_y[...] = jnp.sum(dy_ref[...].astype(f32), axis=0, keepdims=True)
        full_qkv[...] = jnp.zeros_like(full_qkv)
        full_fc[...] = jnp.zeros_like(full_fc)
        cut = sum_fc_ref.shape[1]
        begin = (at[LANE] * group + at[SUB]) * cut
        full_fc[:, pl.ds(pl.multiple_of(begin, cut), cut)] = sum_fc_ref[...]
        nothing = jnp.zeros((1, HEAD_DIM), f32)
        for part in range(3):
            for i in range(heads):
                head = (at[SUB] * heads + i) * lanes_c + at[LANE]
                take = (part * heads + i) * HEAD_DIM
                value = sum_qkv_ref[:, take : take + HEAD_DIM]
                low = jnp.full((1, 2 * HEAD_DIM), lax.rem(head, 2), jnp.int32) == 0
                put = pl.ds(pl.multiple_of(part * width + head // 2 * 128, 128), 128)
                full_qkv[:, put] = jnp.where(
                    low,
                    jnp.concatenate([value, nothing], axis=1),
                    jnp.concatenate([nothing, value], axis=1),
                )
        vector_refs = (gain_ref, shift_ref, full_y, full_qkv, full_fc)

        def put_out(slot, value):
            for j in range(chunks):
                upto = min(width - j * lanes, lanes)
                begin = rows + j * share
                stage[slot, begin : begin + share, :upto] = value[:, j * lanes : j * lanes + upto]

        for k in range(group):
            for i in range(heads):
                slot = (at[SUB] ^ k) * heads + i
                if k:
                    put_out(slot, half_refs[k - 1][i])
                else:
                    here = pl.ds(pl.multiple_of(i * HEAD_DIM + at[SUB] * share, share), share)
                    put_out(slot, out_grad_ref[here, :])
        small[...] = jnp.zeros_like(small)
        sizes = [ref.shape[1] // (seqs * ctxs) for ref in vector_refs]
        for seq in range(seqs):
            for ctx in range(ctxs):
                owner = seq * ctxs + ctx
                values = [
                    ref[:, owner * n : (owner + 1) * n] for ref, n in zip(vector_refs, sizes)
                ]
                put_small(small, ctx * share, share, 0, values)
            stage[seq, :rows, :total] = qkv_ref[seq * rows : (seq + 1) * rows, :]
            stage[seq, :rows, lanes - SMALL :] = small[...].astype(bf16)
        wait_all(
            start_all(
                [(stage.at[lax.rem(at[S] + seqs - k, seqs)], ref) for k, ref in enumerate(outs)], sem
            )
        )

    return call(
        kernel,
        [],
        [
            pltpu.VMEM((seqs, out_rows, lanes), bf16),
            pltpu.VMEM((rows, SMALL), f32),
            pltpu.VMEM((1, width), f32),
            pltpu.VMEM((1, 3 * width), f32),
            pltpu.VMEM((1, 4 * width), f32),
            sems(seqs),
        ],
        scalars,
        (grad_qkv, grad_out, *halves, *vectors),
        far_outs=[shape((out_rows, lanes))] * seqs,
    )


def sum_qkv_call(scalars, share, width, rows, pieces):
    lanes = pieces[0].shape[1]
    chunks = -(-width // lanes)
    kinds, parts = small_rows(share)
    ctxs = rows // share

    def kernel(at, *refs):
        far_refs, (w_out_ref, out_ref, sums, got, made, sem, sem_out) = (
            refs[: len(pieces)],
            refs[len(pieces) :],
        )
        wait_all(start_all([(ref, got.at[k]) for k, ref in enumerate(far_refs)], sem))
        sums[...] = sum(got[k].astype(f32) for k in range(len(pieces)))
        for j in range(chunks):
            upto = min(width - j * lanes, lanes)
            begin = rows + j * share
            w_out_ref[:, j * lanes : j * lanes + upto] = sums[begin : begin + share, :upto]
        if parts == 2:
            for ctx in range(ctxs):
                base = ctx * share
                here = sums[base : base + kinds, lanes - SMALL :]
                left = sums[base + kinds : base + 2 * kinds, lanes - SMALL :]
                value = here + left
                high = value.astype(bf16).astype(f32)
                sums[base : base + kinds, lanes - SMALL :] = high
                sums[base + kinds : base + 2 * kinds, lanes - SMALL :] = value - high
        made[...] = sums[:rows, :].astype(bf16)
        wait_all(start_all([(made, out_ref)], sem_out))

    return call(
        kernel,
        [shape((share, width), f32)],
        [
            pltpu.VMEM(pieces[0].shape, f32),
            pltpu.VMEM((len(pieces), *pieces[0].shape), bf16),
            pltpu.VMEM((rows, lanes), bf16),
            sems(len(pieces)),
            sems(1),
        ],
        scalars,
        (),
        far=pieces,
        far_outs=[shape((rows, lanes))],
    )


def home_fc_call(scalars, got):
    ctxs, share, double = got.shape
    cut = double // 2

    def kernel(at, got_ref, one_ref, two_ref):
        for ctx in range(ctxs):
            cols = slice(ctx * cut, (ctx + 1) * cut)
            one_ref[:, cols] = got_ref[ctx, :, :cut].astype(f32)
            two_ref[:, cols] = got_ref[ctx, :, cut:].astype(f32)

    return call(kernel, [shape((share, ctxs * cut), f32)] * 2, [], scalars, (got,), room=0)


def home_qkv_call(scalars, group, heads, lanes, width, got):
    ctxs, share, wide = got.shape
    kinds, parts = small_rows(share)
    sizes = (share, share, share, 3 * share, 4 * share, share)
    kind_of = (0, 1, 2, 3, 4, 2)

    def kernel(at, got_ref, out_ref, *small_refs):
        for ctx in range(ctxs):
            for part in range(3):
                for i in range(heads):
                    put = head_lanes(ctx, part, i, heads, group, lanes, width)
                    take = (part * heads + i) * HEAD_DIM
                    out_ref[:, put : put + HEAD_DIM] = got_ref[
                        ctx, :, take : take + HEAD_DIM
                    ].astype(f32)
        sums = sum(got_ref[ctx, :, wide - SMALL :].astype(f32) for ctx in range(ctxs))
        for kind, n, ref in zip(kind_of, sizes, small_refs):
            value = sums[kind : kind + 1, :]
            if parts == 2:
                value = value + sums[kinds + kind : kinds + kind + 1, :]
            ref[...] = value[:, :n]

    return call(
        kernel,
        [shape((share, 3 * width), f32)] + [shape((1, n), f32) for n in sizes],
        [],
        scalars,
        (got,),
        room=0,
    )


def finish_call(scalars, x, dy, gain, keep, parts):
    def kernel(at, x_ref, dy_ref, gain_ref, keep_ref, *refs):
        *part_refs, out_ref = refs
        dh = keep_ref[...] + sum(ref[...].astype(f32) for ref in part_refs)
        here = x_ref[...].astype(f32)
        centred = here - jnp.mean(here, axis=1, keepdims=True)
        rstd = lax.rsqrt(jnp.mean(centred * centred, axis=1, keepdims=True) + norm_eps)
        xhat = centred * rstd
        scaled = dh * gain_ref[...]
        out_ref[...] = dy_ref[...].astype(f32) + rstd * (
            scaled
            - jnp.mean(scaled, axis=1, keepdims=True)
            - xhat * jnp.mean(scaled * xhat, axis=1, keepdims=True)
        )

    return call(kernel, [shape(x.shape, f32)], [], scalars, (x, dy, gain, keep, *parts), room=0)[0]


def body(
    block_in,
    cotangent,
    segments,
    ln_gain,
    ln_bias,
    w_qkv,
    b_qkv,
    w_out,
    b_out,
    w_fc1,
    b_fc1,
    w_fc2,
    b_fc2,
):
    seqs, ctxs = lax.axis_size("seq"), lax.axis_size("ctx")
    s, c = lax.axis_index("seq"), lax.axis_index("ctx")
    _, piece, width = block_in.shape
    seq_len = piece * ctxs
    share = w_qkv.shape[0]
    hidden = w_fc1.shape[1]
    cut = hidden // ctxs
    heads = HEADS // ctxs
    group = HEAD_DIM // share
    lanes = ctxs // group
    rows = ctxs * share
    zs = ctxs // 2
    sub, lane = c % group, c // group
    scalars = jnp.stack([c % 2, c // 2, s, sub, lane]).astype(jnp.int32)
    total = 3 * heads * HEAD_DIM
    x_here, dy_here = block_in[0], cotangent[0]

    def from_z(k):
        return [(i, ((i // 2 - k) % zs) * 2 + i % 2) for i in range(ctxs)]

    def from_s(k):
        return [(i, (i - k) % seqs) for i in range(seqs)]

    def partner(k):
        return [(i, i ^ k) for i in range(ctxs)]

    def along(axis, parts, pairs):
        return [lax.ppermute(part, axis, pair) for part, pair in zip(parts, pairs)]

    hops_z = [from_z(k) for k in range(1, zs)]
    hops_s = [from_s(k) for k in range(1, seqs)]
    hops_g = [partner(k) for k in range(1, group)]

    def spread_ctx(local):
        mine = [local] + along("ctx", [local] * (zs - 1), hops_z)
        return mine + along("ctx", mine, [partner(1)] * zs)

    def swap_ctx(blocks):
        return lax.all_to_all(blocks, "ctx", split_axis=0, concat_axis=0, tiled=True)

    packed = pack_call(
        scalars,
        group,
        heads,
        lanes,
        w_qkv,
        w_fc1,
        w_fc2,
        (ln_gain, ln_bias, b_out, b_fc2, b_qkv, b_fc1),
        segments,
    )
    got = swap_ctx(packed)
    wide = padded(total) + SMALL
    chunks = -(-width // wide)
    w_out_wide = jnp.pad(w_out, ((0, 0), (0, chunks * wide - width)))
    joint = jnp.concatenate(
        [got[:, :, :wide].reshape(rows, wide)]
        + [w_out_wide[:, j * wide : (j + 1) * wide] for j in range(chunks)]
    )
    joint = [joint] + along("seq", [joint] * (seqs - 1), hops_s)
    fc_here = got[:, :, wide:].reshape(rows, 2 * cut)
    w_fc = [fc_here] + along("seq", [fc_here] * (seqs - 1), hops_s)
    x_all = spread_ctx(x_here)
    dy_all = spread_ctx(dy_here)

    tables = tables_call(scalars, joint[0], rows, share, piece)
    gain, shift, bias_out, bias_qkv, bias_fc1, *out_parts = spread_out_call(
        scalars, joint, rows, share, width, group, heads, lanes, cut
    )
    out_parts = out_parts[:1] + along("ctx", out_parts[1:], hops_g)

    block = min(256, seq_len)
    h, xhat, attn, lse, kept, turned, w_qkv_c = attend_call(
        scalars, block, heads, rows, x_all, gain, shift, joint, bias_qkv, tables
    )
    w_fc_c, slope, act, out_mine, w_out_c, out_theirs = forward_call(
        scalars, rows, piece, h, w_fc, bias_fc1, attn, out_parts
    )
    out_theirs = along("ctx", [out_theirs], [partner(1)])[0]
    out_keep, *out_sends = middle_call(scalars, piece, out_mine, out_theirs)
    out_parts = along("ctx", out_sends, hops_z)
    block_out = x_here.astype(f32) + out_keep + bias_out
    for part in out_parts:
        block_out = block_out + part.astype(f32)
    block_out = block_out.astype(bf16)

    dy, dfc, dattn, sum_fc1 = backward_call(scalars, dy_all, w_fc_c, w_out_c, slope)
    grad_fc1 = rows_dot(h, dfc).astype(bf16)
    grad_fc2 = rows_dot(dy, act).astype(bf16)
    fc_parts = split_fc_call(scalars, seqs, grad_fc1, grad_fc2)
    fc_parts = fc_parts[:1] + along("seq", fc_parts[1:], hops_s)
    grad_out = rows_dot(attn, dy).astype(bf16)
    blocks = grad_out.reshape(heads, group, share, width)
    halves = [lax.dynamic_index_in_dim(blocks, sub ^ k, 1, keepdims=False) for k in range(1, group)]
    halves = along("ctx", halves, hops_g)
    dqkv, sum_qkv = attend_back_call(
        scalars, block, heads, kept, turned, dattn, lse, tables, (fc_parts[0],)
    )
    dh_mine, sum_gain, sum_shift, dh_theirs = input_grad_call(
        scalars, piece, dfc, w_fc_c, dqkv, w_qkv_c, xhat
    )
    dh_theirs = along("ctx", [dh_theirs], [partner(1)])[0]
    grad_qkv = rows_dot(h, dqkv).astype(bf16)
    qkv_parts = split_qkv_call(
        scalars,
        seqs,
        share,
        group,
        heads,
        lanes,
        grad_qkv,
        grad_out,
        halves,
        (sum_gain, sum_shift, dy_here, sum_qkv, sum_fc1),
    )
    qkv_parts = qkv_parts[:1] + along("seq", qkv_parts[1:], hops_s)
    dh_keep, *dh_sends = middle_call(scalars, piece, dh_mine, dh_theirs)
    dh_parts = along("ctx", dh_sends, hops_z)

    fc_sum = sum_fc_call(scalars, fc_parts)
    fc_home = swap_ctx(fc_sum.reshape(ctxs, share, 2 * cut))
    out_wout, qkv_sum = sum_qkv_call(scalars, share, width, rows, qkv_parts)
    qkv_home = swap_ctx(qkv_sum.reshape(ctxs, share, wide))
    grad_in = finish_call(scalars, x_here, dy_here, gain, dh_keep, dh_parts)
    out_wfc1, out_wfc2 = home_fc_call(scalars, fc_home)
    out_wqkv, *small = home_qkv_call(scalars, group, heads, lanes, width, qkv_home)
    small = [value.reshape(-1) for value in small]
    return (
        block_out[None],
        grad_in[None],
        small[0],
        small[1],
        out_wqkv,
        small[3],
        out_wout,
        small[2],
        out_wfc1,
        small[4],
        out_wfc2,
        small[5],
    )


def solution(mesh):
    both = ("seq", "ctx")
    tokens, flat, matrix = P("seq", "ctx", None), P(both), P(both, None)
    in_specs = (tokens, tokens, P("seq", "ctx"), flat, flat) + (matrix, flat) * 4
    out_specs = (tokens, tokens, flat, flat) + (matrix, flat) * 4
    return jax.shard_map(body, mesh=mesh, in_specs=in_specs, out_specs=out_specs, check_vma=False)
```

```python
import math

import jax
import jax.numpy as jnp
from jax import lax
from jax.experimental import pallas as pl
from jax.experimental.pallas import tpu as pltpu
from jax.sharding import PartitionSpec as P

HEADS = 16
HEAD_DIM = 64
ROT = 16
HALF = ROT // 2
SMALL = 128

norm_eps = 1e-05
big_negative = -1e30
f32 = jnp.float32
bf16 = jnp.bfloat16


def dot(left, right):
    return lax.dot_general(left, right, (((1,), (0,)), ((), ())), preferred_element_type=f32)


def rows_dot(left, right):
    return lax.dot_general(left, right, (((0,), (0,)), ((), ())), preferred_element_type=f32)


def cols_dot(left, right):
    return lax.dot_general(left, right, (((1,), (1,)), ((), ())), preferred_element_type=f32)


def shape(dims, kind=bf16):
    return jax.ShapeDtypeStruct(dims, kind)


def held(array):
    *lead, low, high = (1, 1, *array.shape)
    size = jnp.dtype(array.dtype).itemsize
    lines = 32 // size
    return math.prod(lead) * (-(-low // lines) * lines) * (-(-high // 128) * 128) * size


def call(kernel, outs, scratch, scalars, operands, far=(), far_outs=(), after=(), room=3, cost=None):
    vmem = pl.BlockSpec(memory_space=pltpu.VMEM)
    hbm = pl.BlockSpec(memory_space=pl.ANY)
    count = len(operands) + len(far)

    def wrapped(*refs):
        kernel(refs[0], *refs[1 : 1 + count], *refs[1 + count + len(after) :])

    flops, moved = cost or (0, 0)
    moved = moved or sum(held(a) for a in [*operands, *far])
    limit = None
    if room:
        limit = sum(held(a) for a in scratch if "sem" not in str(a.dtype)) + (room << 20)
    results = pl.pallas_call(
        wrapped,
        in_specs=[pl.BlockSpec(memory_space=pltpu.SMEM)]
        + [vmem] * len(operands)
        + [hbm] * len(far)
        + [pl.BlockSpec(memory_space=pl.ANY)] * len(after),
        out_specs=[vmem] * len(outs) + [hbm] * len(far_outs),
        out_shape=[*outs, *far_outs],
        scratch_shapes=scratch,
        compiler_params=pltpu.CompilerParams(vmem_limit_bytes=limit),
        cost_estimate=pl.CostEstimate(flops=flops, bytes_accessed=moved, transcendentals=0),
    )(scalars, *operands, *far, *after)
    return list(results)


def start_all(pairs, sems):
    copies = [
        pltpu.make_async_copy(source, target, sems.at[at]) for at, (source, target) in enumerate(pairs)
    ]
    for copy in copies:
        copy.start()
    return copies


def wait_all(copies):
    for copy in copies:
        copy.wait()


def sems(count):
    return pltpu.SemaphoreType.DMA((count,))


def rows_at(index, count):
    return pl.ds(pl.multiple_of(index * count, count), count)


CORE, Z, S, SUB, LANE, CTX = range(6)


def at_c(at, k):
    return at[CTX] ^ k


def padded(total):
    return -(-total // 128) * 128


def head_lanes(to, part, i, heads, group, lanes, width):
    return part * width + (((to % group) * heads + i) * lanes + to // group) * HEAD_DIM


def pack_call(scalars, group, heads, lanes, w_qkv, w_fc1, w_fc2, vectors, seg):
    share, hidden = w_fc1.shape
    count = group * lanes
    cut = hidden // count
    total = 3 * heads * HEAD_DIM
    width = w_qkv.shape[1] // 3

    def kernel(at, qkv_ref, fc1_ref, fc2_ref, *refs):
        small_refs, seg_ref = refs[:6], refs[6]
        outs, (out_ref, small, sem) = refs[7 : 7 + count], refs[7 + count :]
        small[...] = jnp.zeros_like(small)
        for row, ref in enumerate(small_refs):
            small[row : row + 1, : ref.shape[0]] = ref[...].astype(f32).reshape(1, -1)
        last = len(small_refs)
        small[last : last + 1, : seg_ref.shape[1]] = seg_ref[...].astype(f32)
        rounded = small[...].astype(bf16)
        for to in range(count):
            for part in range(3):
                for i in range(heads):
                    begin = head_lanes(to, part, i, heads, group, lanes, width)
                    put = (part * heads + i) * HEAD_DIM
                    out_ref[to, :, put : put + HEAD_DIM] = qkv_ref[:, begin : begin + HEAD_DIM]
            base = padded(total) + SMALL
            out_ref[to, :, base - SMALL : base] = rounded
            out_ref[to, :, base : base + cut] = fc1_ref[:, to * cut : (to + 1) * cut]
            out_ref[to, :, base + cut :] = fc2_ref[:, to * cut : (to + 1) * cut]
        wait_all(start_all([(out_ref.at[at_c(at, k)], ref) for k, ref in enumerate(outs)], sem))

    return call(
        kernel,
        [],
        [
            pltpu.VMEM((count, share, padded(total) + SMALL + 2 * cut), bf16),
            pltpu.VMEM((share, SMALL), f32),
            sems(count),
        ],
        scalars,
        (w_qkv, w_fc1, w_fc2, *vectors, seg),
        far_outs=[shape((share, padded(total) + SMALL + 2 * cut))] * count,
        room=0,
    )


def collect_call(scalars, pieces, w_out, wide):
    count = len(pieces)
    share, lanes = pieces[0].shape
    width = w_out.shape[1]
    chunks = -(-width // wide)
    rows = count * share

    def kernel(at, *refs):
        far_refs, w_out_ref, (joint_ref, fc_ref, sem) = refs[:count], refs[count], refs[count + 1 :]
        pairs = []
        for k, ref in enumerate(far_refs):
            here = rows_at(at_c(at, k), share)
            pairs += [
                (ref.at[:, :wide], joint_ref.at[here, :]),
                (ref.at[:, wide:], fc_ref.at[here, :]),
            ]
        for j in range(chunks):
            upto = min(width - j * wide, wide)
            begin = rows + j * share
            pairs.append(
                (
                    w_out_ref.at[:, j * wide : j * wide + upto],
                    joint_ref.at[begin : begin + share, :upto],
                )
            )
        wait_all(start_all(pairs, sem))

    return call(
        kernel,
        [shape((rows + chunks * share, wide)), shape((rows, lanes - wide))],
        [sems(2 * count + chunks)],
        scalars,
        (),
        far=(*pieces, w_out),
    )


def spread_out_call(scalars, pieces, rows, share, width, group, heads, lanes, cut):
    seqs = len(pieces)
    wide = pieces[0].shape[1]
    chunks = -(-width // wide)
    total = 3 * heads * HEAD_DIM
    ctxs = rows // share
    sizes = (share, share, share, share, 3 * share, 4 * share)

    def kernel(at, *refs):
        far_refs, refs = refs[:seqs], refs[seqs:]
        *refs, local, sem = refs
        wait_all(start_all([(ref, local.at[k]) for k, ref in enumerate(far_refs)], sem))
        in_refs = [local.at[k] for k in range(seqs)]
        gain_ref, shift_ref, out_ref, qkv_ref, fc_ref = refs[:5]
        part_refs, stage, rows_refs, full = refs[5 : 5 + group], refs[5 + group], refs[6 + group : -1], refs[-1]
        for k, ref in enumerate(in_refs):
            slot = lax.rem(at[S] + k, seqs)
            for ctx in range(ctxs):
                block = ref[ctx * share : ctx * share + len(sizes), wide - SMALL :].astype(f32)
                for kind, n in enumerate(sizes):
                    rows_refs[kind][slot, :, ctx * n : (ctx + 1) * n] = block[kind : kind + 1, :n]
            for j in range(chunks):
                upto = min(width - j * wide, wide)
                begin = rows + j * share
                stage[slot, :, j * wide : j * wide + upto] = ref[begin : begin + share, :upto]
        for seq in range(seqs):
            cols = slice(seq * rows, (seq + 1) * rows)
            gain_ref[:, cols] = rows_refs[0][seq]
            shift_ref[:, cols] = rows_refs[1][seq]
            out_ref[:, cols] = rows_refs[2][seq] + rows_refs[3][seq]
            full[:, 3 * seq * rows : 3 * (seq + 1) * rows] = rows_refs[4][seq]
        for part in range(3):
            for i in range(heads):
                head = (at[SUB] * heads + i) * lanes + at[LANE]
                pair = full[:, pl.ds(pl.multiple_of(part * width + head // 2 * 128, 128), 128)]
                put = (part * heads + i) * HEAD_DIM
                low = jnp.full((1, HEAD_DIM), lax.rem(head, 2), jnp.int32) == 0
                qkv_ref[:, put : put + HEAD_DIM] = jnp.where(
                    low, pair[:, :HEAD_DIM], pair[:, HEAD_DIM:]
                )
        per_seq = 4 * rows
        begin = (at[LANE] * group + at[SUB]) * cut
        fc_ref[...] = rows_refs[5][
            begin // per_seq, :, pl.ds(pl.multiple_of(lax.rem(begin, per_seq), 128), cut)
        ]
        for k, ref in enumerate(part_refs):
            for i in range(heads):
                ref[i] = stage[(at[SUB] ^ k) * heads + i]

    return call(
        kernel,
        [shape((1, width), f32)] * 3
        + [shape((1, total), f32), shape((1, cut), f32)]
        + [shape((heads, share, width))] * group,
        [pltpu.VMEM((seqs, share, width), bf16)]
        + [pltpu.VMEM((seqs, 1, ctxs * n), f32) for n in sizes]
        + [pltpu.VMEM((1, 3 * width), f32), pltpu.VMEM((seqs, *pieces[0].shape), bf16), sems(seqs)],
        scalars,
        (),
        far=pieces,
    )


def tables_call(scalars, joint, rows, share, piece):
    ctxs = rows // share
    seq_len = ctxs * piece
    total = joint.shape[1] - SMALL
    powers = [float(10000.0 ** (-2.0 * i / ROT)) for i in range(HALF)]

    def kernel(at, far_ref, first_ref, cos_ref, sin_ref, seg_ref, joint_ref, sem):
        wait_all(start_all([(far_ref, joint_ref)], sem))
        for ctx in range(ctxs):
            block = joint_ref[ctx * share : ctx * share + 8, total : total + piece].astype(f32)
            seg_ref[:, ctx * piece : (ctx + 1) * piece] = block[6:7]
        seg = seg_ref[...]
        first = jnp.zeros((1, seq_len), f32)
        for name in range(1, 4):
            begin = jnp.sum((seg < name).astype(f32), axis=1, keepdims=True)
            first = jnp.where(seg >= name, begin, first)
        first_ref[...] = first.astype(jnp.int32)
        pos = lax.broadcasted_iota(jnp.int32, (HALF, seq_len), 1).astype(f32) - first
        which = lax.broadcasted_iota(jnp.int32, (HALF, seq_len), 0)
        freq = jnp.full((HALF, seq_len), powers[0], f32)
        for i in range(1, HALF):
            freq = jnp.where(which == i, powers[i], freq)
        angle = pos * freq
        cos_ref[...] = jnp.cos(angle)
        sin_ref[...] = jnp.sin(angle)

    return call(
        kernel,
        [shape((1, seq_len), jnp.int32), shape((HALF, seq_len), f32), shape((HALF, seq_len), f32)],
        [pltpu.VMEM((1, seq_len), f32), pltpu.VMEM(joint.shape, bf16), sems(1)],
        scalars,
        (),
        far=(joint,),
    )


def rope_t(x_t, cos_t, sin_t):
    parts = []
    for base in range(0, x_t.shape[0], HEAD_DIM):
        one, two = x_t[base : base + HALF], x_t[base + HALF : base + ROT]
        parts += [
            one * cos_t - two * sin_t,
            two * cos_t + one * sin_t,
            x_t[base + ROT : base + HEAD_DIM],
        ]
    return jnp.concatenate(parts, axis=0)


def scores_of(keys, queries_t, first, begin, here, limit):
    raw = dot(keys[:limit], queries_t[:, begin : begin + here])
    first = first[:, begin : begin + here]
    key_at = lax.broadcasted_iota(jnp.int32, (here, here), 0)
    query_at = lax.broadcasted_iota(jnp.int32, (here, here), 1)
    causal = (key_at <= query_at) & (key_at + begin >= first)
    parts = []
    if begin:
        early = lax.broadcasted_iota(jnp.int32, (begin, here), 0) >= first
        parts.append(jnp.where(early, raw[:begin], big_negative))
    parts.append(jnp.where(causal, raw[begin:], big_negative))
    return jnp.concatenate(parts, axis=0) if begin else parts[0]


def slots(at, refs):
    count = len(refs) // 2
    for k in range(count):
        here = 2 * lax.rem(at[Z] + k, count)
        yield refs[k], here + at[CORE]
        yield refs[count + k], here + 1 - at[CORE]


def attend_call(scalars, block, heads, rows, pieces, gain, shift, weights, bias, tables):
    piece, width = pieces[0].shape
    seq_len = piece * len(pieces)
    seqs = len(weights)
    total = 3 * heads * HEAD_DIM
    own = heads * HEAD_DIM
    tile = min(256, seq_len)

    def kernel(at, *refs):
        n = len(pieces)
        gain_ref, shift_ref, bias_ref, first_ref, cos_ref, sin_ref = refs[:6]
        x_refs, w_refs = refs[6 : 6 + n], refs[6 + n : 6 + n + seqs]
        h_ref, xhat_ref, out_ref, lse_ref, kept_ref, turned_ref, w_ref = refs[
            6 + n + seqs : 13 + n + seqs
        ]
        x_all, qkv, out_t, sem = refs[13 + n + seqs :]
        pairs = [(ref, x_all.at[rows_at(slot, piece), :]) for ref, slot in slots(at, x_refs)]
        pairs += [
            (ref.at[:rows, : padded(total)], w_ref.at[rows_at(lax.rem(at[S] + k, seqs), rows), :])
            for k, ref in enumerate(w_refs)
        ]
        wait_all(start_all(pairs, sem))

        def norm_tile(t, carry):
            here = rows_at(t, tile)
            x = x_all[here, :].astype(f32)
            centred = x - jnp.mean(x, axis=1, keepdims=True)
            rstd = lax.rsqrt(jnp.mean(centred * centred, axis=1, keepdims=True) + norm_eps)
            xhat = centred * rstd
            xhat_ref[here, :] = xhat.astype(bf16)
            h = (xhat * gain_ref[...] + shift_ref[...]).astype(bf16)
            h_ref[here, :] = h
            qkv[here, :] = dot(h, w_ref[:, :total]) + bias_ref[...]
            return carry

        lax.fori_loop(0, seq_len // tile, norm_tile, 0)
        cos_t, sin_t = cos_ref[...], sin_ref[...]
        q_t = rope_t(qkv[:, :own].T, cos_t, sin_t) * 0.125
        k_t = rope_t(qkv[:, own : 2 * own].T, cos_t, sin_t)
        v = qkv[:, 2 * own :]
        kb = k_t.T.astype(bf16)
        kept_ref[:, :own] = q_t.T.astype(bf16)
        kept_ref[:, own : 2 * own] = kb
        kept_ref[:, 2 * own :] = v.astype(bf16)
        q_t = q_t.astype(bf16)
        v_t = v.T.astype(bf16)
        turned_ref[:own] = q_t
        turned_ref[own:] = k_t.astype(bf16)
        begins = first_ref[...]
        for head in range(heads):
            lanes = slice(head * HEAD_DIM, (head + 1) * HEAD_DIM)
            keys, queries_t, values_t = kb[:, lanes], q_t[lanes], v_t[lanes]
            for begin in range(0, seq_len, block):
                limit = begin + block
                scores = scores_of(keys, queries_t, begins, begin, block, limit)
                top = jnp.max(scores, axis=0, keepdims=True)
                expd = jnp.exp(scores - top)
                sums = jnp.sum(expd, axis=0, keepdims=True)
                out = dot(values_t[:, :limit], expd.astype(bf16))
                out_t[lanes, begin:limit] = out * (1.0 / sums)
                lse_ref[head : head + 1, begin:limit] = top + jnp.log(sums)
        out_ref[...] = out_t[...].T.astype(bf16)

    return call(
        kernel,
        [
            shape((seq_len, width)),
            shape((seq_len, width)),
            shape((seq_len, own)),
            shape((heads, seq_len), f32),
            shape((seq_len, total)),
            shape((2 * own, seq_len)),
            shape((width, padded(total))),
        ],
        [
            pltpu.VMEM((seq_len, width), bf16),
            pltpu.VMEM((seq_len, total), f32),
            pltpu.VMEM((own, seq_len), f32),
            sems(len(pieces) + seqs),
        ],
        scalars,
        (gain, shift, bias, *tables),
        far=(*pieces, *weights),
        room=8 * (seq_len // 1024) ** 2,
        cost=(4 * seq_len * width * total, 0),
    )


def attend_back_call(scalars, block, heads, kept, turned, grad, lse, tables, after):
    seq_len, total = kept.shape
    own = total // 3

    def kernel(
        at, kept_ref, turned_ref, grad_ref, lse_ref, first_ref, cos_ref, sin_ref, out_ref, sum_ref, dq_t, dk, dv
    ):
        q = kept_ref[:, :own]
        k = kept_ref[:, own : 2 * own]
        v = kept_ref[:, 2 * own :]
        grad = grad_ref[...]
        q_t, k_t = turned_ref[:own], turned_ref[own:]
        grad_t = grad.astype(f32).T.astype(bf16)
        begins = first_ref[...]
        for head in range(heads):
            lanes = slice(head * HEAD_DIM, (head + 1) * HEAD_DIM)
            q_h, k_h, v_h, grad_h = q[:, lanes], k[:, lanes], v[:, lanes], grad[:, lanes]
            for begin in reversed(range(0, seq_len, block)):
                limit = begin + block
                scores = scores_of(k_h, q_t[lanes], begins, begin, block, limit)
                probs = jnp.exp(scores - lse_ref[head : head + 1, begin:limit])
                grad_p = dot(v_h[:limit], grad_t[lanes, begin:limit])
                delta = jnp.sum(probs * grad_p, axis=0, keepdims=True)
                grad_s = (probs * (grad_p - delta)).astype(bf16)
                dk_here = dot(grad_s, q_h[begin:limit])
                dv_here = dot(probs.astype(bf16), grad_h[begin:limit])
                if limit == seq_len:
                    dk[head] = dk_here
                    dv[head] = dv_here
                else:
                    dk[head, :limit] += dk_here
                    dv[head, :limit] += dv_here
                dq_t[lanes, begin:limit] = dot(k_t[lanes, :limit], grad_s)
        cos_t, sin_t = cos_ref[...], -sin_ref[...]
        dk_all = jnp.concatenate([dk[head] for head in range(heads)], axis=1)
        dv_all = jnp.concatenate([dv[head] for head in range(heads)], axis=1)
        for part, value in (
            (0, rope_t(dq_t[...] * 0.125, cos_t, sin_t).T),
            (1, rope_t(dk_all.T, cos_t, sin_t).T),
            (2, dv_all),
        ):
            rounded = value.astype(bf16)
            cols = slice(part * own, (part + 1) * own)
            out_ref[:, cols] = rounded
            sum_ref[:, cols] = jnp.sum(rounded.astype(f32), axis=0, keepdims=True)

    return call(
        kernel,
        [shape((seq_len, total)), shape((1, total), f32)],
        [
            pltpu.VMEM((own, seq_len), f32),
            pltpu.VMEM((heads, seq_len, HEAD_DIM), f32),
            pltpu.VMEM((heads, seq_len, HEAD_DIM), f32),
        ],
        scalars,
        (kept, turned, grad, lse, *tables),
        after=after,
        room=8 * (seq_len // 1024) ** 2,
        cost=(10 * seq_len * seq_len * own, 0),
    )


ROOT = 0.7978845608028654
CUBIC = 0.044715


def split_rows(at, z, piece, value, stage, mine_ref, theirs_ref, sem):
    stage[z] = value.astype(bf16)
    mine_ref[rows_at(z, piece), :] = stage[z, rows_at(at[CORE], piece), :]
    out_rows(at, z, piece, stage, theirs_ref, sem).start()


def out_rows(at, z, piece, stage, theirs_ref, sem):
    return pltpu.make_async_copy(
        stage.at[z, rows_at(1 - at[CORE], piece), :], theirs_ref.at[rows_at(z, piece), :], sem.at[z]
    )


def forward_call(scalars, rows, piece, h, weights, bias, attn, out_parts):
    seq_len, width = h.shape
    cut = weights[0].shape[1] // 2
    seqs = len(weights)
    tile = 2 * piece
    half = seq_len // 2
    count = seq_len // tile

    heads, share, _ = out_parts[0].shape
    group = len(out_parts)

    def kernel(at, h_ref, bias_ref, attn_ref, *refs):
        w_refs, part_refs, refs = refs[:seqs], refs[seqs : seqs + group], refs[seqs + group :]
        w_ref, slope_ref, act_ref, mine_ref, w_out_ref, theirs_ref, stage, sem, sem_out = refs
        pairs = [
            (ref, w_ref.at[rows_at(lax.rem(at[S] + k, seqs), rows), :])
            for k, ref in enumerate(w_refs)
        ]
        for k, ref in enumerate(part_refs):
            for i in range(heads):
                begin = i * HEAD_DIM + (at[SUB] ^ k) * share
                here = pl.ds(pl.multiple_of(begin, share), share)
                pairs.append((ref.at[i], w_out_ref.at[here, :]))
        wait_all(start_all(pairs, sem))

        def step(t, carry):
            here = rows_at(t, tile)
            v = dot(h_ref[here, :], w_ref[:, :cut]) + bias_ref[...]
            square = v * v
            t_v = jnp.tanh(ROOT * (v + CUBIC * (square * v)))
            halved = 0.5 * (1.0 + t_v)
            act = (v * halved).astype(bf16)
            act_ref[here, :] = act
            slope = halved + 0.5 * v * (1.0 - t_v * t_v) * (ROOT * (1.0 + (3.0 * CUBIC) * square))
            slope_ref[here, :] = slope.astype(bf16)
            out = dot(attn_ref[here, :], w_out_ref[...]) + cols_dot(act, w_ref[:, cut:])
            split_rows(at, t, piece, out, stage, mine_ref, theirs_ref, sem_out)
            return carry

        lax.fori_loop(0, count, step, 0)
        wait_all([out_rows(at, z, piece, stage, theirs_ref, sem_out) for z in range(count)])

    return call(
        kernel,
        [
            shape((width, 2 * cut)),
            shape((seq_len, cut)),
            shape((seq_len, cut)),
            shape((half, width)),
            shape((heads * HEAD_DIM, width)),
        ],
        [pltpu.VMEM((count, tile, width), bf16), sems(seqs + group * heads), sems(count)],
        scalars,
        (h, bias, attn),
        far=(*weights, *out_parts),
        far_outs=[shape((half, width))],
        cost=(4 * seq_len * width * cut, 0),
    )


def middle_call(scalars, piece, mine, theirs):
    half, width = mine.shape
    count = half // piece

    def kernel(at, mine_ref, theirs_ref, keep_ref, *refs):
        sends, (got, made, sem, sem_out) = refs[: count - 1], refs[count - 1 :]
        here = [rows_at(lax.rem(at[Z] + count - k, count), piece) for k in range(count)]
        order = [*range(1, count), 0]
        copies = start_all([(theirs_ref.at[here[k], :], got.at[k]) for k in order], sem)
        outs = []
        for copy, k in zip(copies, order):
            copy.wait()
            value = mine_ref[here[k], :].astype(f32) + got[k].astype(f32)
            if k == 0:
                keep_ref[...] = value
            else:
                made[k - 1] = value.astype(bf16)
                out = pltpu.make_async_copy(made.at[k - 1], sends[k - 1], sem_out.at[k - 1])
                out.start()
                outs.append(out)
        wait_all(outs)

    return call(
        kernel,
        [shape((piece, width), f32)],
        [
            pltpu.VMEM((count, piece, width), bf16),
            pltpu.VMEM((count - 1, piece, width), bf16),
            sems(count),
            sems(count - 1),
        ],
        scalars,
        (mine,),
        far=(theirs,),
        far_outs=[shape((piece, width))] * (count - 1),
    )


def backward_call(scalars, pieces, weight, w_out, slope):
    piece, width = pieces[0].shape
    seq_len, cut = slope.shape
    own = w_out.shape[0]
    tile = min(256, seq_len)

    def kernel(at, *refs):
        n = len(pieces)
        (w_ref, w_out_ref, slope_ref), dy_refs = refs[:3], refs[3 : 3 + n]
        dy_ref, dfc_ref, dattn_ref, sum_ref, sem = refs[3 + n :]
        pairs = [(ref, dy_ref.at[rows_at(slot, piece), :]) for ref, slot in slots(at, dy_refs)]
        wait_all(start_all(pairs, sem))
        sum_ref[...] = jnp.zeros_like(sum_ref)

        def step(t, carry):
            here = rows_at(t, tile)
            dy = dy_ref[here, :]
            dfc = (dot(dy, w_ref[:, cut:]) * slope_ref[here, :].astype(f32)).astype(bf16)
            dfc_ref[here, :] = dfc
            sum_ref[...] += jnp.sum(dfc.astype(f32), axis=0, keepdims=True)
            dattn_ref[here, :] = cols_dot(dy, w_out_ref[...]).astype(bf16)
            return carry

        lax.fori_loop(0, seq_len // tile, step, 0)

    return call(
        kernel,
        [shape((seq_len, width)), shape((seq_len, cut)), shape((seq_len, own)), shape((1, cut), f32)],
        [sems(len(pieces))],
        scalars,
        (weight, w_out, slope),
        far=pieces,
        cost=(2 * seq_len * width * cut, 0),
    )


def input_grad_call(scalars, piece, dfc, weight, dqkv, w_qkv, xhat):
    seq_len, cut = dfc.shape
    width = weight.shape[0]
    total = dqkv.shape[1]
    tile = 2 * piece
    half = seq_len // 2
    count = seq_len // tile

    def kernel(at, dfc_ref, w_ref, dqkv_ref, w_qkv_ref, xhat_ref, mine_ref, gain_ref, shift_ref, theirs_ref, stage, sem_out):
        gain_ref[...] = jnp.zeros_like(gain_ref)
        shift_ref[...] = jnp.zeros_like(shift_ref)

        def step(t, carry):
            here = rows_at(t, tile)
            value = cols_dot(dfc_ref[here, :], w_ref[:, :cut]) + cols_dot(
                dqkv_ref[here, :], w_qkv_ref[:, :total]
            )
            gain_ref[...] += jnp.sum(value * xhat_ref[here, :].astype(f32), axis=0, keepdims=True)
            shift_ref[...] += jnp.sum(value, axis=0, keepdims=True)
            split_rows(at, t, piece, value, stage, mine_ref, theirs_ref, sem_out)
            return carry

        lax.fori_loop(0, count, step, 0)
        wait_all([out_rows(at, z, piece, stage, theirs_ref, sem_out) for z in range(count)])

    return call(
        kernel,
        [shape((half, width)), shape((1, width), f32), shape((1, width), f32)],
        [pltpu.VMEM((count, tile, width), bf16), sems(count)],
        scalars,
        (dfc, weight, dqkv, w_qkv, xhat),
        far_outs=[shape((half, width))],
        cost=(2 * seq_len * width * cut, 0),
    )


def split_fc_call(scalars, seqs, grad_fc1, grad_fc2):
    width, cut = grad_fc1.shape
    rows = width // seqs

    def kernel(at, one_ref, two_ref, *refs):
        *outs, sem = refs
        pairs = []
        for k, ref in enumerate(outs):
            here = rows_at(lax.rem(at[S] + seqs - k, seqs), rows)
            pairs += [
                (one_ref.at[here, :], ref.at[:, :cut]),
                (two_ref.at[here, :], ref.at[:, cut:]),
            ]
        wait_all(start_all(pairs, sem))

    return call(
        kernel,
        [],
        [sems(2 * seqs)],
        scalars,
        (grad_fc1, grad_fc2),
        far_outs=[shape((rows, 2 * cut))] * seqs,
    )


def sum_fc_call(scalars, share, pieces):
    rows, lanes = pieces[0].shape
    count = len(pieces)
    tiles = 2
    ctxs = rows // share
    tile = rows // tiles

    def kernel(at, *refs):
        far_refs, outs, (got, made, sem, sem_out) = (
            refs[:count],
            refs[count : count + ctxs],
            refs[count + ctxs :],
        )
        starts = [slice(t * tile, (t + 1) * tile) for t in range(tiles)]
        copies = start_all(
            [(ref.at[here, :], got.at[k, here, :]) for here in starts for k, ref in enumerate(far_refs)],
            sem,
        )
        for t, here in enumerate(starts):
            wait_all(copies[t * count : (t + 1) * count])
            made[here, :] = sum(got[k, here, :].astype(f32) for k in range(count)).astype(bf16)
        wait_all(
            start_all(
                [(made.at[rows_at(at_c(at, k), share), :], ref) for k, ref in enumerate(outs)], sem_out
            )
        )

    return call(
        kernel,
        [],
        [
            pltpu.VMEM((count, rows, lanes), bf16),
            pltpu.VMEM((rows, lanes), bf16),
            sems(tiles * count),
            sems(ctxs),
        ],
        scalars,
        (),
        far=pieces,
        far_outs=[shape((share, lanes))] * ctxs,
    )


def small_rows(share):
    return 5, (2 if share >= 10 else 1)


def put_small(block_ref, base, share, lane0, values):
    kinds, parts = small_rows(share)
    for kind, value in enumerate(values):
        high = value.astype(bf16)
        block_ref[base + kind : base + kind + 1, lane0 : lane0 + value.shape[1]] = high.astype(f32)
        if parts == 2:
            row = base + kinds + kind
            block_ref[row : row + 1, lane0 : lane0 + value.shape[1]] = value - high.astype(f32)


def split_qkv_call(scalars, seqs, share, group, heads, lanes_c, grad_qkv, grad_out, halves, vectors):
    width, total = grad_qkv.shape
    rows = width // seqs
    lanes = padded(total) + SMALL
    chunks = -(-width // lanes)
    out_rows = rows + chunks * share
    ctxs = rows // share

    def kernel(at, qkv_ref, out_grad_ref, *refs):
        half_refs, refs = refs[: group - 1], refs[group - 1 :]
        (gain_ref, shift_ref, dy_ref, sum_qkv_ref, sum_fc_ref) = refs[:5]
        outs, (stage, small, full_y, full_qkv, full_fc, sem) = refs[5 : 5 + seqs], refs[5 + seqs :]
        full_y[...] = jnp.sum(dy_ref[...].astype(f32), axis=0, keepdims=True)
        full_qkv[...] = jnp.zeros_like(full_qkv)
        full_fc[...] = jnp.zeros_like(full_fc)
        cut = sum_fc_ref.shape[1]
        begin = (at[LANE] * group + at[SUB]) * cut
        full_fc[:, pl.ds(pl.multiple_of(begin, cut), cut)] = sum_fc_ref[...]
        nothing = jnp.zeros((1, HEAD_DIM), f32)
        for part in range(3):
            for i in range(heads):
                head = (at[SUB] * heads + i) * lanes_c + at[LANE]
                take = (part * heads + i) * HEAD_DIM
                value = sum_qkv_ref[:, take : take + HEAD_DIM]
                low = jnp.full((1, 2 * HEAD_DIM), lax.rem(head, 2), jnp.int32) == 0
                put = pl.ds(pl.multiple_of(part * width + head // 2 * 128, 128), 128)
                full_qkv[:, put] = jnp.where(
                    low,
                    jnp.concatenate([value, nothing], axis=1),
                    jnp.concatenate([nothing, value], axis=1),
                )
        vector_refs = (gain_ref, shift_ref, full_y, full_qkv, full_fc)

        def put_out(slot, value):
            for j in range(chunks):
                upto = min(width - j * lanes, lanes)
                begin = rows + j * share
                stage[slot, begin : begin + share, :upto] = value[:, j * lanes : j * lanes + upto]

        for k in range(group):
            for i in range(heads):
                slot = (at[SUB] ^ k) * heads + i
                if k:
                    put_out(slot, half_refs[k - 1][i])
                else:
                    here = pl.ds(pl.multiple_of(i * HEAD_DIM + at[SUB] * share, share), share)
                    put_out(slot, out_grad_ref[here, :])
        small[...] = jnp.zeros_like(small)
        sizes = [ref.shape[1] // (seqs * ctxs) for ref in vector_refs]
        for seq in range(seqs):
            for ctx in range(ctxs):
                owner = seq * ctxs + ctx
                values = [
                    ref[:, owner * n : (owner + 1) * n] for ref, n in zip(vector_refs, sizes)
                ]
                put_small(small, ctx * share, share, 0, values)
            stage[seq, :rows, :total] = qkv_ref[seq * rows : (seq + 1) * rows, :]
            stage[seq, :rows, lanes - SMALL :] = small[...].astype(bf16)
        wait_all(
            start_all(
                [(stage.at[lax.rem(at[S] + seqs - k, seqs)], ref) for k, ref in enumerate(outs)], sem
            )
        )

    return call(
        kernel,
        [],
        [
            pltpu.VMEM((seqs, out_rows, lanes), bf16),
            pltpu.VMEM((rows, SMALL), f32),
            pltpu.VMEM((1, width), f32),
            pltpu.VMEM((1, 3 * width), f32),
            pltpu.VMEM((1, 4 * width), f32),
            sems(seqs),
        ],
        scalars,
        (grad_qkv, grad_out, *halves, *vectors),
        far_outs=[shape((out_rows, lanes))] * seqs,
    )


def sum_qkv_call(scalars, share, width, rows, pieces):
    lanes = pieces[0].shape[1]
    chunks = -(-width // lanes)
    kinds, parts = small_rows(share)
    ctxs = rows // share

    def kernel(at, *refs):
        far_refs, w_out_ref, refs = refs[: len(pieces)], refs[len(pieces)], refs[len(pieces) + 1 :]
        outs, (sums, got, made, sem, sem_out) = refs[:ctxs], refs[ctxs:]
        wait_all(start_all([(ref, got.at[k]) for k, ref in enumerate(far_refs)], sem))
        sums[...] = sum(got[k].astype(f32) for k in range(len(pieces)))
        for j in range(chunks):
            upto = min(width - j * lanes, lanes)
            begin = rows + j * share
            w_out_ref[:, j * lanes : j * lanes + upto] = sums[begin : begin + share, :upto]
        if parts == 2:
            for ctx in range(ctxs):
                base = ctx * share
                here = sums[base : base + kinds, lanes - SMALL :]
                left = sums[base + kinds : base + 2 * kinds, lanes - SMALL :]
                value = here + left
                high = value.astype(bf16).astype(f32)
                sums[base : base + kinds, lanes - SMALL :] = high
                sums[base + kinds : base + 2 * kinds, lanes - SMALL :] = value - high
        made[...] = sums[:rows, :].astype(bf16)
        wait_all(
            start_all(
                [(made.at[rows_at(at_c(at, k), share), :], ref) for k, ref in enumerate(outs)], sem_out
            )
        )

    return call(
        kernel,
        [shape((share, width), f32)],
        [
            pltpu.VMEM(pieces[0].shape, f32),
            pltpu.VMEM((len(pieces), *pieces[0].shape), bf16),
            pltpu.VMEM((rows, lanes), bf16),
            sems(len(pieces)),
            sems(ctxs),
        ],
        scalars,
        (),
        far=pieces,
        far_outs=[shape((share, lanes))] * ctxs,
    )


def home_fc_call(scalars, pieces, after):
    ctxs = len(pieces)
    share, double = pieces[0].shape
    cut = double // 2

    def kernel(at, *refs):
        far_refs, (one_ref, two_ref, got, sem) = refs[:ctxs], refs[ctxs:]
        wait_all(start_all([(ref, got.at[at_c(at, k)]) for k, ref in enumerate(far_refs)], sem))
        for ctx in range(ctxs):
            cols = slice(ctx * cut, (ctx + 1) * cut)
            one_ref[:, cols] = got[ctx, :, :cut].astype(f32)
            two_ref[:, cols] = got[ctx, :, cut:].astype(f32)

    return call(
        kernel,
        [shape((share, ctxs * cut), f32)] * 2,
        [pltpu.VMEM((ctxs, share, double), bf16), sems(ctxs)],
        scalars,
        (),
        far=pieces,
        after=after,
        room=4,
    )


def home_qkv_call(scalars, group, heads, lanes, width, pieces, after):
    ctxs = len(pieces)
    share, wide = pieces[0].shape
    kinds, parts = small_rows(share)
    sizes = (share, share, share, 3 * share, 4 * share, share)
    kind_of = (0, 1, 2, 3, 4, 2)

    def kernel(at, *refs):
        far_refs, out_ref, refs = refs[:ctxs], refs[ctxs], refs[ctxs + 1 :]
        *small_refs, got_ref, sem = refs
        wait_all(start_all([(ref, got_ref.at[at_c(at, k)]) for k, ref in enumerate(far_refs)], sem))
        for ctx in range(ctxs):
            for part in range(3):
                for i in range(heads):
                    put = head_lanes(ctx, part, i, heads, group, lanes, width)
                    take = (part * heads + i) * HEAD_DIM
                    out_ref[:, put : put + HEAD_DIM] = got_ref[
                        ctx, :, take : take + HEAD_DIM
                    ].astype(f32)
        sums = sum(got_ref[ctx, :, wide - SMALL :].astype(f32) for ctx in range(ctxs))
        for kind, n, ref in zip(kind_of, sizes, small_refs):
            value = sums[kind : kind + 1, :]
            if parts == 2:
                value = value + sums[kinds + kind : kinds + kind + 1, :]
            ref[...] = value[:, :n]

    return call(
        kernel,
        [shape((share, 3 * width), f32)] + [shape((1, n), f32) for n in sizes],
        [pltpu.VMEM((ctxs, share, wide), bf16), sems(ctxs)],
        scalars,
        (),
        far=pieces,
        after=after,
        room=4,
    )


def finish_call(scalars, x, dy, gain, keep, parts):
    count = len(parts)

    def kernel(at, x_ref, dy_ref, gain_ref, keep_ref, *refs):
        far_refs, (out_ref, got, sem) = refs[:count], refs[count:]
        copies = start_all([(ref, got.at[k]) for k, ref in enumerate(far_refs)], sem)
        here = x_ref[...].astype(f32)
        centred = here - jnp.mean(here, axis=1, keepdims=True)
        rstd = lax.rsqrt(jnp.mean(centred * centred, axis=1, keepdims=True) + norm_eps)
        xhat = centred * rstd
        wait_all(copies)
        dh = keep_ref[...] + sum(got[k].astype(f32) for k in range(count))
        scaled = dh * gain_ref[...]
        out_ref[...] = dy_ref[...].astype(f32) + rstd * (
            scaled
            - jnp.mean(scaled, axis=1, keepdims=True)
            - xhat * jnp.mean(scaled * xhat, axis=1, keepdims=True)
        )

    return call(
        kernel,
        [shape(x.shape, f32)],
        [pltpu.VMEM((count, *x.shape), bf16), sems(count)],
        scalars,
        (x, dy, gain, keep),
        far=parts,
        room=6,
    )[0]


def body(
    block_in,
    cotangent,
    segments,
    ln_gain,
    ln_bias,
    w_qkv,
    b_qkv,
    w_out,
    b_out,
    w_fc1,
    b_fc1,
    w_fc2,
    b_fc2,
):
    seqs, ctxs = lax.axis_size("seq"), lax.axis_size("ctx")
    s, c = lax.axis_index("seq"), lax.axis_index("ctx")
    _, piece, width = block_in.shape
    seq_len = piece * ctxs
    share = w_qkv.shape[0]
    hidden = w_fc1.shape[1]
    cut = hidden // ctxs
    heads = HEADS // ctxs
    group = HEAD_DIM // share
    lanes = ctxs // group
    rows = ctxs * share
    zs = ctxs // 2
    sub, lane = c % group, c // group
    scalars = jnp.stack([c % 2, c // 2, s, sub, lane, c]).astype(jnp.int32)
    total = 3 * heads * HEAD_DIM
    x_here, dy_here = block_in[0], cotangent[0]

    def from_z(k):
        return [(i, ((i // 2 - k) % zs) * 2 + i % 2) for i in range(ctxs)]

    def from_s(k):
        return [(i, (i - k) % seqs) for i in range(seqs)]

    def partner(k):
        return [(i, i ^ k) for i in range(ctxs)]

    def along(axis, parts, pairs):
        out = []
        for part, pair in zip(parts, pairs):
            out.append(lax.ppermute(part, axis, pair))
        return out

    hops_z = [from_z(k) for k in range(1, zs)]
    hops_s = [from_s(k) for k in range(1, seqs)]
    hops_c = [partner(k) for k in range(1, ctxs)]
    hops_g = [partner(k) for k in range(1, group)]

    def spread_ctx(local):
        mine = [local] + along("ctx", [local] * (zs - 1), hops_z)
        return mine + along("ctx", mine, [partner(1)] * zs)

    packed = pack_call(
        scalars,
        group,
        heads,
        lanes,
        w_qkv,
        w_fc1,
        w_fc2,
        (ln_gain, ln_bias, b_out, b_fc2, b_qkv, b_fc1),
        segments,
    )
    wide = padded(total) + SMALL
    got = packed[:1] + along("ctx", packed[1:], hops_c)
    joint, fc_here = collect_call(scalars, got, w_out, wide)
    joint = [joint] + along("seq", [joint] * (seqs - 1), hops_s)
    w_fc = [fc_here] + along("seq", [fc_here] * (seqs - 1), hops_s)
    x_all = spread_ctx(x_here)
    dy_all = spread_ctx(dy_here)

    tables = tables_call(scalars, joint[0], rows, share, piece)
    gain, shift, bias_out, bias_qkv, bias_fc1, *out_parts = spread_out_call(
        scalars, joint, rows, share, width, group, heads, lanes, cut
    )
    out_parts = out_parts[:1] + along("ctx", out_parts[1:], hops_g)

    block = min(256, seq_len)
    h, xhat, attn, lse, kept, turned, w_qkv_c = attend_call(
        scalars, block, heads, rows, x_all, gain, shift, joint, bias_qkv, tables
    )
    w_fc_c, slope, act, out_mine, w_out_c, out_theirs = forward_call(
        scalars, rows, piece, h, w_fc, bias_fc1, attn, out_parts
    )
    out_theirs = along("ctx", [out_theirs], [partner(1)])[0]
    out_keep, *out_sends = middle_call(scalars, piece, out_mine, out_theirs)
    out_parts = along("ctx", out_sends, hops_z)
    block_out = x_here.astype(f32) + out_keep + bias_out
    for part in out_parts:
        block_out = block_out + part.astype(f32)
    block_out = block_out.astype(bf16)

    dy, dfc, dattn, sum_fc1 = backward_call(scalars, dy_all, w_fc_c, w_out_c, slope)
    grad_fc1 = rows_dot(h, dfc).astype(bf16)
    grad_fc2 = rows_dot(dy, act).astype(bf16)
    fc_parts = split_fc_call(scalars, seqs, grad_fc1, grad_fc2)
    fc_parts = fc_parts[:1] + along("seq", fc_parts[1:], hops_s)
    grad_out = rows_dot(attn, dy).astype(bf16)
    blocks = grad_out.reshape(heads, group, share, width)
    halves = [lax.dynamic_index_in_dim(blocks, sub ^ k, 1, keepdims=False) for k in range(1, group)]
    halves = along("ctx", halves, hops_g)
    dqkv, sum_qkv = attend_back_call(
        scalars, block, heads, kept, turned, dattn, lse, tables, (fc_parts[0],)
    )
    dh_mine, sum_gain, sum_shift, dh_theirs = input_grad_call(
        scalars, piece, dfc, w_fc_c, dqkv, w_qkv_c, xhat
    )
    dh_theirs = along("ctx", [dh_theirs], [partner(1)])[0]
    grad_qkv = rows_dot(h, dqkv).astype(bf16)
    qkv_parts = split_qkv_call(
        scalars,
        seqs,
        share,
        group,
        heads,
        lanes,
        grad_qkv,
        grad_out,
        halves,
        (sum_gain, sum_shift, dy_here, sum_qkv, sum_fc1),
    )
    qkv_parts = qkv_parts[:1] + along("seq", qkv_parts[1:], hops_s)
    dh_keep, *dh_sends = middle_call(scalars, piece, dh_mine, dh_theirs)
    dh_parts = along("ctx", dh_sends, hops_z)

    fc_home = sum_fc_call(scalars, share, fc_parts)
    fc_home = fc_home[:1] + along("ctx", fc_home[1:], hops_c)
    out_wout, *qkv_home = sum_qkv_call(scalars, share, width, rows, qkv_parts)
    qkv_home = qkv_home[:1] + along("ctx", qkv_home[1:], hops_c)
    grad_in = finish_call(scalars, x_here, dy_here, gain, dh_keep, dh_parts)
    out_wfc1, out_wfc2 = home_fc_call(scalars, fc_home, (grad_in,))
    out_wqkv, *small = home_qkv_call(
        scalars, group, heads, lanes, width, qkv_home, (out_wfc1,)
    )
    small = [value.reshape(-1) for value in small]
    return (
        block_out[None],
        grad_in[None],
        small[0],
        small[1],
        out_wqkv,
        small[3],
        out_wout,
        small[2],
        out_wfc1,
        small[4],
        out_wfc2,
        small[5],
    )


def solution(mesh):
    both = ("seq", "ctx")
    tokens, flat, matrix = P("seq", "ctx", None), P(both), P(both, None)
    in_specs = (tokens, tokens, P("seq", "ctx"), flat, flat) + (matrix, flat) * 4
    out_specs = (tokens, tokens, flat, flat) + (matrix, flat) * 4
    return jax.shard_map(body, mesh=mesh, in_specs=in_specs, out_specs=out_specs, check_vma=False)
```

```python
import math

import jax
import jax.numpy as jnp
from jax import lax
from jax.experimental import pallas as pl
from jax.experimental.pallas import tpu as pltpu
from jax.sharding import PartitionSpec as P

HEADS = 16
HEAD_DIM = 64
ROT = 16
HALF = ROT // 2
SMALL = 128

norm_eps = 1e-05
big_negative = -1e30
f32 = jnp.float32
bf16 = jnp.bfloat16


def dot(left, right):
    return lax.dot_general(left, right, (((1,), (0,)), ((), ())), preferred_element_type=f32)


def rows_dot(left, right):
    return lax.dot_general(left, right, (((0,), (0,)), ((), ())), preferred_element_type=f32)


def cols_dot(left, right):
    return lax.dot_general(left, right, (((1,), (1,)), ((), ())), preferred_element_type=f32)


def shape(dims, kind=bf16):
    return jax.ShapeDtypeStruct(dims, kind)


def held(array):
    *lead, low, high = (1, 1, *array.shape)
    size = jnp.dtype(array.dtype).itemsize
    lines = 32 // size
    return math.prod(lead) * (-(-low // lines) * lines) * (-(-high // 128) * 128) * size


def call(kernel, outs, scratch, scalars, operands, far=(), far_outs=(), after=(), room=3, cost=None):
    vmem = pl.BlockSpec(memory_space=pltpu.VMEM)
    hbm = pl.BlockSpec(memory_space=pl.ANY)
    count = len(operands) + len(far)

    def wrapped(*refs):
        kernel(places(scalars), *refs[:count], *refs[count + len(after) :])

    flops, moved = cost or (0, 0)
    moved = moved or sum(held(a) for a in [*operands, *far])
    limit = None
    if room:
        limit = sum(held(a) for a in scratch if "sem" not in str(a.dtype)) + (room << 20)
    results = pl.pallas_call(
        wrapped,
        in_specs=[vmem] * len(operands)
        + [hbm] * len(far)
        + [pl.BlockSpec(memory_space=pl.ANY)] * len(after),
        out_specs=[vmem] * len(outs) + [hbm] * len(far_outs),
        out_shape=[*outs, *far_outs],
        scratch_shapes=scratch,
        compiler_params=pltpu.CompilerParams(vmem_limit_bytes=limit),
        cost_estimate=pl.CostEstimate(flops=flops, bytes_accessed=moved, transcendentals=0),
    )(*operands, *far, *after)
    return list(results)


def places(group):
    s, c = lax.axis_index("seq"), lax.axis_index("ctx")
    return (lax.rem(c, 2), lax.div(c, 2), s, lax.rem(c, group), lax.div(c, group), c)


def start_all(pairs, sems):
    copies = [
        pltpu.make_async_copy(source, target, sems.at[at]) for at, (source, target) in enumerate(pairs)
    ]
    for copy in copies:
        copy.start()
    return copies


def wait_all(copies):
    for copy in copies:
        copy.wait()


def sems(count):
    return pltpu.SemaphoreType.DMA((count,))


def rows_at(index, count):
    return pl.ds(pl.multiple_of(index * count, count), count)


CORE, Z, S, SUB, LANE, CTX = range(6)


def at_c(at, k):
    return at[CTX] ^ k


def padded(total):
    return -(-total // 128) * 128


def head_lanes(to, part, i, heads, group, lanes, width):
    return part * width + (((to % group) * heads + i) * lanes + to // group) * HEAD_DIM


def pack_call(scalars, group, heads, lanes, w_qkv, w_fc1, w_fc2, vectors, seg):
    share, hidden = w_fc1.shape
    count = group * lanes
    cut = hidden // count
    total = 3 * heads * HEAD_DIM
    width = w_qkv.shape[1] // 3

    def kernel(at, qkv_ref, fc1_ref, fc2_ref, *refs):
        small_refs, seg_ref = refs[:6], refs[6]
        outs, (out_ref, small, sem) = refs[7 : 7 + count], refs[7 + count :]
        small[...] = jnp.zeros_like(small)
        for row, ref in enumerate(small_refs):
            small[row : row + 1, : ref.shape[0]] = ref[...].astype(f32).reshape(1, -1)
        last = len(small_refs)
        small[last : last + 1, : seg_ref.shape[1]] = seg_ref[...].astype(f32)
        rounded = small[...].astype(bf16)
        for to in range(count):
            for part in range(3):
                for i in range(heads):
                    begin = head_lanes(to, part, i, heads, group, lanes, width)
                    put = (part * heads + i) * HEAD_DIM
                    out_ref[to, :, put : put + HEAD_DIM] = qkv_ref[:, begin : begin + HEAD_DIM]
            base = padded(total) + SMALL
            out_ref[to, :, base - SMALL : base] = rounded
            out_ref[to, :, base : base + cut] = fc1_ref[:, to * cut : (to + 1) * cut]
            out_ref[to, :, base + cut :] = fc2_ref[:, to * cut : (to + 1) * cut]
        wait_all(start_all([(out_ref.at[at_c(at, k)], ref) for k, ref in enumerate(outs)], sem))

    return call(
        kernel,
        [],
        [
            pltpu.VMEM((count, share, padded(total) + SMALL + 2 * cut), bf16),
            pltpu.VMEM((share, SMALL), f32),
            sems(count),
        ],
        scalars,
        (w_qkv, w_fc1, w_fc2, *vectors, seg),
        far_outs=[shape((share, padded(total) + SMALL + 2 * cut))] * count,
        room=0,
    )


def collect_call(scalars, pieces, w_out, wide):
    count = len(pieces)
    share, lanes = pieces[0].shape
    width = w_out.shape[1]
    chunks = -(-width // wide)
    rows = count * share

    def kernel(at, *refs):
        far_refs, w_out_ref, (joint_ref, fc_ref, sem) = refs[:count], refs[count], refs[count + 1 :]
        pairs = []
        for k, ref in enumerate(far_refs):
            here = rows_at(at_c(at, k), share)
            pairs += [
                (ref.at[:, :wide], joint_ref.at[here, :]),
                (ref.at[:, wide:], fc_ref.at[here, :]),
            ]
        for j in range(chunks):
            upto = min(width - j * wide, wide)
            begin = rows + j * share
            pairs.append(
                (
                    w_out_ref.at[:, j * wide : j * wide + upto],
                    joint_ref.at[begin : begin + share, :upto],
                )
            )
        wait_all(start_all(pairs, sem))

    return call(
        kernel,
        [shape((rows + chunks * share, wide)), shape((rows, lanes - wide))],
        [sems(2 * count + chunks)],
        scalars,
        (),
        far=(*pieces, w_out),
    )


def spread_out_call(scalars, pieces, rows, share, width, group, heads, lanes, cut):
    seqs = len(pieces)
    wide = pieces[0].shape[1]
    chunks = -(-width // wide)
    total = 3 * heads * HEAD_DIM
    ctxs = rows // share
    sizes = (share, share, share, share, 3 * share, 4 * share)

    def kernel(at, *refs):
        far_refs, refs = refs[:seqs], refs[seqs:]
        *refs, local, sem = refs
        wait_all(start_all([(ref, local.at[k]) for k, ref in enumerate(far_refs)], sem))
        in_refs = [local.at[k] for k in range(seqs)]
        gain_ref, shift_ref, out_ref, qkv_ref, fc_ref = refs[:5]
        part_refs, stage, rows_refs, full = refs[5 : 5 + group], refs[5 + group], refs[6 + group : -1], refs[-1]
        for k, ref in enumerate(in_refs):
            slot = lax.rem(at[S] + k, seqs)
            for ctx in range(ctxs):
                block = ref[ctx * share : ctx * share + len(sizes), wide - SMALL :].astype(f32)
                for kind, n in enumerate(sizes):
                    rows_refs[kind][slot, :, ctx * n : (ctx + 1) * n] = block[kind : kind + 1, :n]
            for j in range(chunks):
                upto = min(width - j * wide, wide)
                begin = rows + j * share
                stage[slot, :, j * wide : j * wide + upto] = ref[begin : begin + share, :upto]
        for seq in range(seqs):
            cols = slice(seq * rows, (seq + 1) * rows)
            gain_ref[:, cols] = rows_refs[0][seq]
            shift_ref[:, cols] = rows_refs[1][seq]
            out_ref[:, cols] = rows_refs[2][seq] + rows_refs[3][seq]
            full[:, 3 * seq * rows : 3 * (seq + 1) * rows] = rows_refs[4][seq]
        for part in range(3):
            for i in range(heads):
                head = (at[SUB] * heads + i) * lanes + at[LANE]
                pair = full[:, pl.ds(pl.multiple_of(part * width + head // 2 * 128, 128), 128)]
                put = (part * heads + i) * HEAD_DIM
                low = jnp.full((1, HEAD_DIM), lax.rem(head, 2), jnp.int32) == 0
                qkv_ref[:, put : put + HEAD_DIM] = jnp.where(
                    low, pair[:, :HEAD_DIM], pair[:, HEAD_DIM:]
                )
        per_seq = 4 * rows
        begin = (at[LANE] * group + at[SUB]) * cut
        fc_ref[...] = rows_refs[5][
            begin // per_seq, :, pl.ds(pl.multiple_of(lax.rem(begin, per_seq), 128), cut)
        ]
        for k, ref in enumerate(part_refs):
            for i in range(heads):
                ref[i] = stage[(at[SUB] ^ k) * heads + i]

    return call(
        kernel,
        [shape((1, width), f32)] * 3
        + [shape((1, total), f32), shape((1, cut), f32)]
        + [shape((heads, share, width))] * group,
        [pltpu.VMEM((seqs, share, width), bf16)]
        + [pltpu.VMEM((seqs, 1, ctxs * n), f32) for n in sizes]
        + [pltpu.VMEM((1, 3 * width), f32), pltpu.VMEM((seqs, *pieces[0].shape), bf16), sems(seqs)],
        scalars,
        (),
        far=pieces,
    )


def tables_call(scalars, joint, rows, share, piece):
    ctxs = rows // share
    seq_len = ctxs * piece
    total = joint.shape[1] - SMALL
    powers = [float(10000.0 ** (-2.0 * i / ROT)) for i in range(HALF)]

    def kernel(at, far_ref, first_ref, cos_ref, sin_ref, seg_ref, joint_ref, sem):
        wait_all(start_all([(far_ref, joint_ref)], sem))
        for ctx in range(ctxs):
            block = joint_ref[ctx * share : ctx * share + 8, total : total + piece].astype(f32)
            seg_ref[:, ctx * piece : (ctx + 1) * piece] = block[6:7]
        seg = seg_ref[...]
        first = jnp.zeros((1, seq_len), f32)
        for name in range(1, 4):
            begin = jnp.sum((seg < name).astype(f32), axis=1, keepdims=True)
            first = jnp.where(seg >= name, begin, first)
        first_ref[...] = first.astype(jnp.int32)
        pos = lax.broadcasted_iota(jnp.int32, (HALF, seq_len), 1).astype(f32) - first
        which = lax.broadcasted_iota(jnp.int32, (HALF, seq_len), 0)
        freq = jnp.full((HALF, seq_len), powers[0], f32)
        for i in range(1, HALF):
            freq = jnp.where(which == i, powers[i], freq)
        angle = pos * freq
        cos_ref[...] = jnp.cos(angle)
        sin_ref[...] = jnp.sin(angle)

    return call(
        kernel,
        [shape((1, seq_len), jnp.int32), shape((HALF, seq_len), f32), shape((HALF, seq_len), f32)],
        [pltpu.VMEM((1, seq_len), f32), pltpu.VMEM(joint.shape, bf16), sems(1)],
        scalars,
        (),
        far=(joint,),
    )


def rope_t(x_t, cos_t, sin_t):
    parts = []
    for base in range(0, x_t.shape[0], HEAD_DIM):
        one, two = x_t[base : base + HALF], x_t[base + HALF : base + ROT]
        parts += [
            one * cos_t - two * sin_t,
            two * cos_t + one * sin_t,
            x_t[base + ROT : base + HEAD_DIM],
        ]
    return jnp.concatenate(parts, axis=0)


def scores_of(keys, queries_t, first, begin, here, limit):
    raw = dot(keys[:limit], queries_t[:, begin : begin + here])
    first = first[:, begin : begin + here]
    key_at = lax.broadcasted_iota(jnp.int32, (here, here), 0)
    query_at = lax.broadcasted_iota(jnp.int32, (here, here), 1)
    causal = (key_at <= query_at) & (key_at + begin >= first)
    parts = []
    if begin:
        early = lax.broadcasted_iota(jnp.int32, (begin, here), 0) >= first
        parts.append(jnp.where(early, raw[:begin], big_negative))
    parts.append(jnp.where(causal, raw[begin:], big_negative))
    return jnp.concatenate(parts, axis=0) if begin else parts[0]


def slots(at, refs):
    count = len(refs) // 2
    for k in range(count):
        here = 2 * lax.rem(at[Z] + k, count)
        yield refs[k], here + at[CORE]
        yield refs[count + k], here + 1 - at[CORE]


def attend_call(scalars, block, heads, rows, pieces, gain, shift, weights, bias, tables):
    piece, width = pieces[0].shape
    seq_len = piece * len(pieces)
    seqs = len(weights)
    total = 3 * heads * HEAD_DIM
    own = heads * HEAD_DIM
    tile = min(256, seq_len)

    def kernel(at, *refs):
        n = len(pieces)
        gain_ref, shift_ref, bias_ref, first_ref, cos_ref, sin_ref = refs[:6]
        x_refs, w_refs = refs[6 : 6 + n], refs[6 + n : 6 + n + seqs]
        h_ref, xhat_ref, out_ref, lse_ref, kept_ref, turned_ref, w_ref = refs[
            6 + n + seqs : 13 + n + seqs
        ]
        x_all, qkv, out_t, sem = refs[13 + n + seqs :]
        pairs = [(ref, x_all.at[rows_at(slot, piece), :]) for ref, slot in slots(at, x_refs)]
        pairs += [
            (ref.at[:rows, : padded(total)], w_ref.at[rows_at(lax.rem(at[S] + k, seqs), rows), :])
            for k, ref in enumerate(w_refs)
        ]
        wait_all(start_all(pairs, sem))

        def norm_tile(t, carry):
            here = rows_at(t, tile)
            x = x_all[here, :].astype(f32)
            centred = x - jnp.mean(x, axis=1, keepdims=True)
            rstd = lax.rsqrt(jnp.mean(centred * centred, axis=1, keepdims=True) + norm_eps)
            xhat = centred * rstd
            xhat_ref[here, :] = xhat.astype(bf16)
            h = (xhat * gain_ref[...] + shift_ref[...]).astype(bf16)
            h_ref[here, :] = h
            qkv[here, :] = dot(h, w_ref[:, :total]) + bias_ref[...]
            return carry

        lax.fori_loop(0, seq_len // tile, norm_tile, 0)
        cos_t, sin_t = cos_ref[...], sin_ref[...]
        q_t = rope_t(qkv[:, :own].T, cos_t, sin_t) * 0.125
        k_t = rope_t(qkv[:, own : 2 * own].T, cos_t, sin_t)
        v = qkv[:, 2 * own :]
        kb = k_t.T.astype(bf16)
        kept_ref[:, :own] = q_t.T.astype(bf16)
        kept_ref[:, own : 2 * own] = kb
        kept_ref[:, 2 * own :] = v.astype(bf16)
        q_t = q_t.astype(bf16)
        v_t = v.T.astype(bf16)
        turned_ref[:own] = q_t
        turned_ref[own:] = k_t.astype(bf16)
        begins = first_ref[...]
        for head in range(heads):
            lanes = slice(head * HEAD_DIM, (head + 1) * HEAD_DIM)
            keys, queries_t, values_t = kb[:, lanes], q_t[lanes], v_t[lanes]
            for begin in range(0, seq_len, block):
                limit = begin + block
                scores = scores_of(keys, queries_t, begins, begin, block, limit)
                top = jnp.max(scores, axis=0, keepdims=True)
                expd = jnp.exp(scores - top)
                sums = jnp.sum(expd, axis=0, keepdims=True)
                out = dot(values_t[:, :limit], expd.astype(bf16))
                out_t[lanes, begin:limit] = out * (1.0 / sums)
                lse_ref[head : head + 1, begin:limit] = top + jnp.log(sums)
        out_ref[...] = out_t[...].T.astype(bf16)

    return call(
        kernel,
        [
            shape((seq_len, width)),
            shape((seq_len, width)),
            shape((seq_len, own)),
            shape((heads, seq_len), f32),
            shape((seq_len, total)),
            shape((2 * own, seq_len)),
            shape((width, padded(total))),
        ],
        [
            pltpu.VMEM((seq_len, width), bf16),
            pltpu.VMEM((seq_len, total), f32),
            pltpu.VMEM((own, seq_len), f32),
            sems(len(pieces) + seqs),
        ],
        scalars,
        (gain, shift, bias, *tables),
        far=(*pieces, *weights),
        room=8 * (seq_len // 1024) ** 2,
        cost=(4 * seq_len * width * total, 0),
    )


def attend_back_call(scalars, block, heads, kept, turned, grad, lse, tables, after):
    seq_len, total = kept.shape
    own = total // 3

    def kernel(
        at, kept_ref, turned_ref, grad_ref, lse_ref, first_ref, cos_ref, sin_ref, out_ref, sum_ref, dq_t, dk, dv
    ):
        q = kept_ref[:, :own]
        k = kept_ref[:, own : 2 * own]
        v = kept_ref[:, 2 * own :]
        grad = grad_ref[...]
        q_t, k_t = turned_ref[:own], turned_ref[own:]
        grad_t = grad.astype(f32).T.astype(bf16)
        begins = first_ref[...]
        for head in range(heads):
            lanes = slice(head * HEAD_DIM, (head + 1) * HEAD_DIM)
            q_h, k_h, v_h, grad_h = q[:, lanes], k[:, lanes], v[:, lanes], grad[:, lanes]
            for begin in reversed(range(0, seq_len, block)):
                limit = begin + block
                scores = scores_of(k_h, q_t[lanes], begins, begin, block, limit)
                probs = jnp.exp(scores - lse_ref[head : head + 1, begin:limit])
                grad_p = dot(v_h[:limit], grad_t[lanes, begin:limit])
                delta = jnp.sum(probs * grad_p, axis=0, keepdims=True)
                grad_s = (probs * (grad_p - delta)).astype(bf16)
                dk_here = dot(grad_s, q_h[begin:limit])
                dv_here = dot(probs.astype(bf16), grad_h[begin:limit])
                if limit == seq_len:
                    dk[head] = dk_here
                    dv[head] = dv_here
                else:
                    dk[head, :limit] += dk_here
                    dv[head, :limit] += dv_here
                dq_t[lanes, begin:limit] = dot(k_t[lanes, :limit], grad_s)
        cos_t, sin_t = cos_ref[...], -sin_ref[...]
        dk_all = jnp.concatenate([dk[head] for head in range(heads)], axis=1)
        dv_all = jnp.concatenate([dv[head] for head in range(heads)], axis=1)
        for part, value in (
            (0, rope_t(dq_t[...] * 0.125, cos_t, sin_t).T),
            (1, rope_t(dk_all.T, cos_t, sin_t).T),
            (2, dv_all),
        ):
            rounded = value.astype(bf16)
            cols = slice(part * own, (part + 1) * own)
            out_ref[:, cols] = rounded
            sum_ref[:, cols] = jnp.sum(rounded.astype(f32), axis=0, keepdims=True)

    return call(
        kernel,
        [shape((seq_len, total)), shape((1, total), f32)],
        [
            pltpu.VMEM((own, seq_len), f32),
            pltpu.VMEM((heads, seq_len, HEAD_DIM), f32),
            pltpu.VMEM((heads, seq_len, HEAD_DIM), f32),
        ],
        scalars,
        (kept, turned, grad, lse, *tables),
        after=after,
        room=8 * (seq_len // 1024) ** 2,
        cost=(10 * seq_len * seq_len * own, 0),
    )


ROOT = 0.7978845608028654
CUBIC = 0.044715


def split_rows(at, z, piece, value, stage, mine_ref, theirs_ref, sem):
    stage[z] = value.astype(bf16)
    mine_ref[rows_at(z, piece), :] = stage[z, rows_at(at[CORE], piece), :]
    out_rows(at, z, piece, stage, theirs_ref, sem).start()


def out_rows(at, z, piece, stage, theirs_ref, sem):
    return pltpu.make_async_copy(
        stage.at[z, rows_at(1 - at[CORE], piece), :], theirs_ref.at[rows_at(z, piece), :], sem.at[z]
    )


def forward_call(scalars, rows, piece, h, weights, bias, attn, out_parts):
    seq_len, width = h.shape
    cut = weights[0].shape[1] // 2
    seqs = len(weights)
    tile = 2 * piece
    half = seq_len // 2
    count = seq_len // tile

    heads, share, _ = out_parts[0].shape
    group = len(out_parts)

    def kernel(at, h_ref, bias_ref, attn_ref, *refs):
        w_refs, part_refs, refs = refs[:seqs], refs[seqs : seqs + group], refs[seqs + group :]
        w_ref, slope_ref, act_ref, mine_ref, w_out_ref, theirs_ref, stage, sem, sem_out = refs
        pairs = [
            (ref, w_ref.at[rows_at(lax.rem(at[S] + k, seqs), rows), :])
            for k, ref in enumerate(w_refs)
        ]
        for k, ref in enumerate(part_refs):
            for i in range(heads):
                begin = i * HEAD_DIM + (at[SUB] ^ k) * share
                here = pl.ds(pl.multiple_of(begin, share), share)
                pairs.append((ref.at[i], w_out_ref.at[here, :]))
        wait_all(start_all(pairs, sem))

        def step(t, carry):
            here = rows_at(t, tile)
            v = dot(h_ref[here, :], w_ref[:, :cut]) + bias_ref[...]
            square = v * v
            t_v = jnp.tanh(ROOT * (v + CUBIC * (square * v)))
            halved = 0.5 * (1.0 + t_v)
            act = (v * halved).astype(bf16)
            act_ref[here, :] = act
            slope = halved + 0.5 * v * (1.0 - t_v * t_v) * (ROOT * (1.0 + (3.0 * CUBIC) * square))
            slope_ref[here, :] = slope.astype(bf16)
            out = dot(attn_ref[here, :], w_out_ref[...]) + cols_dot(act, w_ref[:, cut:])
            split_rows(at, t, piece, out, stage, mine_ref, theirs_ref, sem_out)
            return carry

        lax.fori_loop(0, count, step, 0)
        wait_all([out_rows(at, z, piece, stage, theirs_ref, sem_out) for z in range(count)])

    return call(
        kernel,
        [
            shape((width, 2 * cut)),
            shape((seq_len, cut)),
            shape((seq_len, cut)),
            shape((half, width)),
            shape((heads * HEAD_DIM, width)),
        ],
        [pltpu.VMEM((count, tile, width), bf16), sems(seqs + group * heads), sems(count)],
        scalars,
        (h, bias, attn),
        far=(*weights, *out_parts),
        far_outs=[shape((half, width))],
        cost=(4 * seq_len * width * cut, 0),
    )


def middle_call(scalars, piece, mine, theirs):
    half, width = mine.shape
    count = half // piece

    def kernel(at, mine_ref, theirs_ref, keep_ref, *refs):
        sends, (got, made, sem, sem_out) = refs[: count - 1], refs[count - 1 :]
        here = [rows_at(lax.rem(at[Z] + count - k, count), piece) for k in range(count)]
        order = [*range(1, count), 0]
        copies = start_all([(theirs_ref.at[here[k], :], got.at[k]) for k in order], sem)
        outs = []
        for copy, k in zip(copies, order):
            copy.wait()
            value = mine_ref[here[k], :].astype(f32) + got[k].astype(f32)
            if k == 0:
                keep_ref[...] = value
            else:
                made[k - 1] = value.astype(bf16)
                out = pltpu.make_async_copy(made.at[k - 1], sends[k - 1], sem_out.at[k - 1])
                out.start()
                outs.append(out)
        wait_all(outs)

    return call(
        kernel,
        [shape((piece, width), f32)],
        [
            pltpu.VMEM((count, piece, width), bf16),
            pltpu.VMEM((count - 1, piece, width), bf16),
            sems(count),
            sems(count - 1),
        ],
        scalars,
        (mine,),
        far=(theirs,),
        far_outs=[shape((piece, width))] * (count - 1),
    )


def backward_call(scalars, pieces, weight, w_out, slope):
    piece, width = pieces[0].shape
    seq_len, cut = slope.shape
    own = w_out.shape[0]
    tile = min(256, seq_len)

    def kernel(at, *refs):
        n = len(pieces)
        (w_ref, w_out_ref, slope_ref), dy_refs = refs[:3], refs[3 : 3 + n]
        dy_ref, dfc_ref, dattn_ref, sum_ref, sem = refs[3 + n :]
        pairs = [(ref, dy_ref.at[rows_at(slot, piece), :]) for ref, slot in slots(at, dy_refs)]
        wait_all(start_all(pairs, sem))
        sum_ref[...] = jnp.zeros_like(sum_ref)

        def step(t, carry):
            here = rows_at(t, tile)
            dy = dy_ref[here, :]
            dfc = (dot(dy, w_ref[:, cut:]) * slope_ref[here, :].astype(f32)).astype(bf16)
            dfc_ref[here, :] = dfc
            sum_ref[...] += jnp.sum(dfc.astype(f32), axis=0, keepdims=True)
            dattn_ref[here, :] = cols_dot(dy, w_out_ref[...]).astype(bf16)
            return carry

        lax.fori_loop(0, seq_len // tile, step, 0)

    return call(
        kernel,
        [shape((seq_len, width)), shape((seq_len, cut)), shape((seq_len, own)), shape((1, cut), f32)],
        [sems(len(pieces))],
        scalars,
        (weight, w_out, slope),
        far=pieces,
        cost=(2 * seq_len * width * cut, 0),
    )


def input_grad_call(scalars, piece, dfc, weight, dqkv, w_qkv, xhat):
    seq_len, cut = dfc.shape
    width = weight.shape[0]
    total = dqkv.shape[1]
    tile = 2 * piece
    half = seq_len // 2
    count = seq_len // tile

    def kernel(at, dfc_ref, w_ref, dqkv_ref, w_qkv_ref, xhat_ref, mine_ref, gain_ref, shift_ref, theirs_ref, stage, sem_out):
        gain_ref[...] = jnp.zeros_like(gain_ref)
        shift_ref[...] = jnp.zeros_like(shift_ref)

        def step(t, carry):
            here = rows_at(t, tile)
            value = cols_dot(dfc_ref[here, :], w_ref[:, :cut]) + cols_dot(
                dqkv_ref[here, :], w_qkv_ref[:, :total]
            )
            gain_ref[...] += jnp.sum(value * xhat_ref[here, :].astype(f32), axis=0, keepdims=True)
            shift_ref[...] += jnp.sum(value, axis=0, keepdims=True)
            split_rows(at, t, piece, value, stage, mine_ref, theirs_ref, sem_out)
            return carry

        lax.fori_loop(0, count, step, 0)
        wait_all([out_rows(at, z, piece, stage, theirs_ref, sem_out) for z in range(count)])

    return call(
        kernel,
        [shape((half, width)), shape((1, width), f32), shape((1, width), f32)],
        [pltpu.VMEM((count, tile, width), bf16), sems(count)],
        scalars,
        (dfc, weight, dqkv, w_qkv, xhat),
        far_outs=[shape((half, width))],
        cost=(2 * seq_len * width * cut, 0),
    )


def split_fc_call(scalars, seqs, share, group, grad_fc1, grad_fc2, grad_out):
    width, cut = grad_fc1.shape
    rows = width // seqs
    heads = grad_out.shape[0] // HEAD_DIM

    def kernel(at, one_ref, two_ref, out_grad_ref, *refs):
        outs, halves, sem = refs[:seqs], refs[seqs:-1], refs[-1]
        pairs = []
        for k, ref in enumerate(halves):
            for i in range(heads):
                begin = i * HEAD_DIM + (at[SUB] ^ (k + 1)) * share
                here = pl.ds(pl.multiple_of(begin, share), share)
                pairs.append((out_grad_ref.at[here, :], ref.at[i]))
        for k, ref in enumerate(outs):
            here = rows_at(lax.rem(at[S] + seqs - k, seqs), rows)
            pairs += [
                (one_ref.at[here, :], ref.at[:, :cut]),
                (two_ref.at[here, :], ref.at[:, cut:]),
            ]
        wait_all(start_all(pairs, sem))

    return call(
        kernel,
        [],
        [sems(2 * seqs + (group - 1) * heads)],
        scalars,
        (grad_fc1, grad_fc2, grad_out),
        far_outs=[shape((rows, 2 * cut))] * seqs + [shape((heads, share, width))] * (group - 1),
    )


def sum_fc_call(scalars, share, pieces):
    rows, lanes = pieces[0].shape
    count = len(pieces)
    tiles = 2
    ctxs = rows // share
    tile = rows // tiles

    def kernel(at, *refs):
        far_refs, outs, (got, made, sem, sem_out) = (
            refs[:count],
            refs[count : count + ctxs],
            refs[count + ctxs :],
        )
        starts = [slice(t * tile, (t + 1) * tile) for t in range(tiles)]
        copies = start_all(
            [(ref.at[here, :], got.at[k, here, :]) for here in starts for k, ref in enumerate(far_refs)],
            sem,
        )
        for t, here in enumerate(starts):
            wait_all(copies[t * count : (t + 1) * count])
            made[here, :] = sum(got[k, here, :].astype(f32) for k in range(count)).astype(bf16)
        wait_all(
            start_all(
                [(made.at[rows_at(at_c(at, k), share), :], ref) for k, ref in enumerate(outs)], sem_out
            )
        )

    return call(
        kernel,
        [],
        [
            pltpu.VMEM((count, rows, lanes), bf16),
            pltpu.VMEM((rows, lanes), bf16),
            sems(tiles * count),
            sems(ctxs),
        ],
        scalars,
        (),
        far=pieces,
        far_outs=[shape((share, lanes))] * ctxs,
    )


def small_rows(share):
    return 5, (2 if share >= 10 else 1)


def put_small(block_ref, base, share, lane0, values):
    kinds, parts = small_rows(share)
    for kind, value in enumerate(values):
        high = value.astype(bf16)
        block_ref[base + kind : base + kind + 1, lane0 : lane0 + value.shape[1]] = high.astype(f32)
        if parts == 2:
            row = base + kinds + kind
            block_ref[row : row + 1, lane0 : lane0 + value.shape[1]] = value - high.astype(f32)


def split_qkv_call(scalars, seqs, share, group, heads, lanes_c, grad_qkv, grad_out, halves, vectors):
    width, total = grad_qkv.shape
    rows = width // seqs
    lanes = padded(total) + SMALL
    chunks = -(-width // lanes)
    out_rows = rows + chunks * share
    ctxs = rows // share

    def kernel(at, qkv_ref, out_grad_ref, *refs):
        half_refs, refs = refs[: group - 1], refs[group - 1 :]
        (gain_ref, shift_ref, dy_ref, sum_qkv_ref, sum_fc_ref) = refs[:5]
        outs, (stage, small, full_y, full_qkv, full_fc, sem) = refs[5 : 5 + seqs], refs[5 + seqs :]
        full_y[...] = jnp.sum(dy_ref[...].astype(f32), axis=0, keepdims=True)
        full_qkv[...] = jnp.zeros_like(full_qkv)
        full_fc[...] = jnp.zeros_like(full_fc)
        cut = sum_fc_ref.shape[1]
        begin = (at[LANE] * group + at[SUB]) * cut
        full_fc[:, pl.ds(pl.multiple_of(begin, cut), cut)] = sum_fc_ref[...]
        nothing = jnp.zeros((1, HEAD_DIM), f32)
        for part in range(3):
            for i in range(heads):
                head = (at[SUB] * heads + i) * lanes_c + at[LANE]
                take = (part * heads + i) * HEAD_DIM
                value = sum_qkv_ref[:, take : take + HEAD_DIM]
                low = jnp.full((1, 2 * HEAD_DIM), lax.rem(head, 2), jnp.int32) == 0
                put = pl.ds(pl.multiple_of(part * width + head // 2 * 128, 128), 128)
                full_qkv[:, put] = jnp.where(
                    low,
                    jnp.concatenate([value, nothing], axis=1),
                    jnp.concatenate([nothing, value], axis=1),
                )
        vector_refs = (gain_ref, shift_ref, full_y, full_qkv, full_fc)

        def put_out(slot, value):
            for j in range(chunks):
                upto = min(width - j * lanes, lanes)
                begin = rows + j * share
                stage[slot, begin : begin + share, :upto] = value[:, j * lanes : j * lanes + upto]

        for k in range(group):
            for i in range(heads):
                slot = (at[SUB] ^ k) * heads + i
                if k:
                    put_out(slot, half_refs[k - 1][i])
                else:
                    here = pl.ds(pl.multiple_of(i * HEAD_DIM + at[SUB] * share, share), share)
                    put_out(slot, out_grad_ref[here, :])
        small[...] = jnp.zeros_like(small)
        sizes = [ref.shape[1] // (seqs * ctxs) for ref in vector_refs]
        for seq in range(seqs):
            for ctx in range(ctxs):
                owner = seq * ctxs + ctx
                values = [
                    ref[:, owner * n : (owner + 1) * n] for ref, n in zip(vector_refs, sizes)
                ]
                put_small(small, ctx * share, share, 0, values)
            stage[seq, :rows, :total] = qkv_ref[seq * rows : (seq + 1) * rows, :]
            stage[seq, :rows, lanes - SMALL :] = small[...].astype(bf16)
        wait_all(
            start_all(
                [(stage.at[lax.rem(at[S] + seqs - k, seqs)], ref) for k, ref in enumerate(outs)], sem
            )
        )

    return call(
        kernel,
        [],
        [
            pltpu.VMEM((seqs, out_rows, lanes), bf16),
            pltpu.VMEM((rows, SMALL), f32),
            pltpu.VMEM((1, width), f32),
            pltpu.VMEM((1, 3 * width), f32),
            pltpu.VMEM((1, 4 * width), f32),
            sems(seqs),
        ],
        scalars,
        (grad_qkv, grad_out, *halves, *vectors),
        far_outs=[shape((out_rows, lanes))] * seqs,
    )


def sum_qkv_call(scalars, share, width, rows, pieces):
    lanes = pieces[0].shape[1]
    chunks = -(-width // lanes)
    kinds, parts = small_rows(share)
    ctxs = rows // share

    def kernel(at, *refs):
        far_refs, w_out_ref, refs = refs[: len(pieces)], refs[len(pieces)], refs[len(pieces) + 1 :]
        outs, (sums, got, made, sem, sem_out) = refs[:ctxs], refs[ctxs:]
        wait_all(start_all([(ref, got.at[k]) for k, ref in enumerate(far_refs)], sem))
        sums[...] = sum(got[k].astype(f32) for k in range(len(pieces)))
        for j in range(chunks):
            upto = min(width - j * lanes, lanes)
            begin = rows + j * share
            w_out_ref[:, j * lanes : j * lanes + upto] = sums[begin : begin + share, :upto]
        if parts == 2:
            for ctx in range(ctxs):
                base = ctx * share
                here = sums[base : base + kinds, lanes - SMALL :]
                left = sums[base + kinds : base + 2 * kinds, lanes - SMALL :]
                value = here + left
                high = value.astype(bf16).astype(f32)
                sums[base : base + kinds, lanes - SMALL :] = high
                sums[base + kinds : base + 2 * kinds, lanes - SMALL :] = value - high
        made[...] = sums[:rows, :].astype(bf16)
        wait_all(
            start_all(
                [(made.at[rows_at(at_c(at, k), share), :], ref) for k, ref in enumerate(outs)], sem_out
            )
        )

    return call(
        kernel,
        [shape((share, width), f32)],
        [
            pltpu.VMEM(pieces[0].shape, f32),
            pltpu.VMEM((len(pieces), *pieces[0].shape), bf16),
            pltpu.VMEM((rows, lanes), bf16),
            sems(len(pieces)),
            sems(ctxs),
        ],
        scalars,
        (),
        far=pieces,
        far_outs=[shape((share, lanes))] * ctxs,
    )


def home_fc_call(scalars, pieces, after):
    ctxs = len(pieces)
    share, double = pieces[0].shape
    cut = double // 2

    def kernel(at, *refs):
        far_refs, (one_ref, two_ref, got, sem) = refs[:ctxs], refs[ctxs:]
        wait_all(start_all([(ref, got.at[at_c(at, k)]) for k, ref in enumerate(far_refs)], sem))
        for ctx in range(ctxs):
            cols = slice(ctx * cut, (ctx + 1) * cut)
            one_ref[:, cols] = got[ctx, :, :cut].astype(f32)
            two_ref[:, cols] = got[ctx, :, cut:].astype(f32)

    return call(
        kernel,
        [shape((share, ctxs * cut), f32)] * 2,
        [pltpu.VMEM((ctxs, share, double), bf16), sems(ctxs)],
        scalars,
        (),
        far=pieces,
        after=after,
        room=4,
    )


def home_qkv_call(scalars, group, heads, lanes, width, pieces, after):
    ctxs = len(pieces)
    share, wide = pieces[0].shape
    kinds, parts = small_rows(share)
    sizes = (share, share, share, 3 * share, 4 * share, share)
    kind_of = (0, 1, 2, 3, 4, 2)

    def kernel(at, *refs):
        far_refs, out_ref, refs = refs[:ctxs], refs[ctxs], refs[ctxs + 1 :]
        *small_refs, got_ref, sem = refs
        wait_all(start_all([(ref, got_ref.at[at_c(at, k)]) for k, ref in enumerate(far_refs)], sem))
        for ctx in range(ctxs):
            for part in range(3):
                for i in range(heads):
                    put = head_lanes(ctx, part, i, heads, group, lanes, width)
                    take = (part * heads + i) * HEAD_DIM
                    out_ref[:, put : put + HEAD_DIM] = got_ref[
                        ctx, :, take : take + HEAD_DIM
                    ].astype(f32)
        sums = sum(got_ref[ctx, :, wide - SMALL :].astype(f32) for ctx in range(ctxs))
        for kind, n, ref in zip(kind_of, sizes, small_refs):
            value = sums[kind : kind + 1, :]
            if parts == 2:
                value = value + sums[kinds + kind : kinds + kind + 1, :]
            ref[...] = value[:, :n]

    return call(
        kernel,
        [shape((share, 3 * width), f32)] + [shape((1, n), f32) for n in sizes],
        [pltpu.VMEM((ctxs, share, wide), bf16), sems(ctxs)],
        scalars,
        (),
        far=pieces,
        after=after,
        room=4,
    )


def finish_call(scalars, x, dy, gain, keep, parts):
    count = len(parts)

    def kernel(at, x_ref, dy_ref, gain_ref, keep_ref, *refs):
        far_refs, (out_ref, got, sem) = refs[:count], refs[count:]
        copies = start_all([(ref, got.at[k]) for k, ref in enumerate(far_refs)], sem)
        here = x_ref[...].astype(f32)
        centred = here - jnp.mean(here, axis=1, keepdims=True)
        rstd = lax.rsqrt(jnp.mean(centred * centred, axis=1, keepdims=True) + norm_eps)
        xhat = centred * rstd
        wait_all(copies)
        dh = keep_ref[...] + sum(got[k].astype(f32) for k in range(count))
        scaled = dh * gain_ref[...]
        out_ref[...] = dy_ref[...].astype(f32) + rstd * (
            scaled
            - jnp.mean(scaled, axis=1, keepdims=True)
            - xhat * jnp.mean(scaled * xhat, axis=1, keepdims=True)
        )

    return call(
        kernel,
        [shape(x.shape, f32)],
        [pltpu.VMEM((count, *x.shape), bf16), sems(count)],
        scalars,
        (x, dy, gain, keep),
        far=parts,
        room=6,
    )[0]


def body(
    block_in,
    cotangent,
    segments,
    ln_gain,
    ln_bias,
    w_qkv,
    b_qkv,
    w_out,
    b_out,
    w_fc1,
    b_fc1,
    w_fc2,
    b_fc2,
):
    seqs, ctxs = lax.axis_size("seq"), lax.axis_size("ctx")
    _, piece, width = block_in.shape
    seq_len = piece * ctxs
    share = w_qkv.shape[0]
    hidden = w_fc1.shape[1]
    cut = hidden // ctxs
    heads = HEADS // ctxs
    group = HEAD_DIM // share
    lanes = ctxs // group
    rows = ctxs * share
    zs = ctxs // 2
    scalars = group
    total = 3 * heads * HEAD_DIM
    x_here, dy_here = block_in[0], cotangent[0]

    def from_z(k):
        return [(i, ((i // 2 - k) % zs) * 2 + i % 2) for i in range(ctxs)]

    def from_s(k):
        return [(i, (i - k) % seqs) for i in range(seqs)]

    def partner(k):
        return [(i, i ^ k) for i in range(ctxs)]

    def along(axis, parts, pairs):
        out = []
        for part, pair in zip(parts, pairs):
            out.append(lax.ppermute(part, axis, pair))
        return out

    hops_z = [from_z(k) for k in range(1, zs)]
    hops_s = [from_s(k) for k in range(1, seqs)]
    hops_c = [partner(k) for k in range(1, ctxs)]
    hops_g = [partner(k) for k in range(1, group)]

    def spread_ctx(local):
        mine = [local] + along("ctx", [local] * (zs - 1), hops_z)
        return mine + along("ctx", mine, [partner(1)] * zs)

    packed = pack_call(
        scalars,
        group,
        heads,
        lanes,
        w_qkv,
        w_fc1,
        w_fc2,
        (ln_gain, ln_bias, b_out, b_fc2, b_qkv, b_fc1),
        segments,
    )
    wide = padded(total) + SMALL
    got = packed[:1] + along("ctx", packed[1:], hops_c)
    joint, fc_here = collect_call(scalars, got, w_out, wide)
    joint = [joint] + along("seq", [joint] * (seqs - 1), hops_s)
    w_fc = [fc_here] + along("seq", [fc_here] * (seqs - 1), hops_s)
    x_all = spread_ctx(x_here)
    dy_all = spread_ctx(dy_here)

    tables = tables_call(scalars, joint[0], rows, share, piece)
    gain, shift, bias_out, bias_qkv, bias_fc1, *out_parts = spread_out_call(
        scalars, joint, rows, share, width, group, heads, lanes, cut
    )
    out_parts = out_parts[:1] + along("ctx", out_parts[1:], hops_g)

    block = min(256, seq_len)
    h, xhat, attn, lse, kept, turned, w_qkv_c = attend_call(
        scalars, block, heads, rows, x_all, gain, shift, joint, bias_qkv, tables
    )
    w_fc_c, slope, act, out_mine, w_out_c, out_theirs = forward_call(
        scalars, rows, piece, h, w_fc, bias_fc1, attn, out_parts
    )
    out_theirs = along("ctx", [out_theirs], [partner(1)])[0]
    out_keep, *out_sends = middle_call(scalars, piece, out_mine, out_theirs)
    out_parts = along("ctx", out_sends, hops_z)
    block_out = x_here.astype(f32) + out_keep + bias_out
    for part in out_parts:
        block_out = block_out + part.astype(f32)
    block_out = block_out.astype(bf16)

    dy, dfc, dattn, sum_fc1 = backward_call(scalars, dy_all, w_fc_c, w_out_c, slope)
    grad_fc1 = rows_dot(h, dfc).astype(bf16)
    grad_fc2 = rows_dot(dy, act).astype(bf16)
    grad_out = rows_dot(attn, dy).astype(bf16)
    split = split_fc_call(scalars, seqs, share, group, grad_fc1, grad_fc2, grad_out)
    fc_parts, halves = split[:seqs], split[seqs:]
    fc_parts = fc_parts[:1] + along("seq", fc_parts[1:], hops_s)
    halves = along("ctx", halves, hops_g)
    dqkv, sum_qkv = attend_back_call(
        scalars, block, heads, kept, turned, dattn, lse, tables, (fc_parts[0],)
    )
    dh_mine, sum_gain, sum_shift, dh_theirs = input_grad_call(
        scalars, piece, dfc, w_fc_c, dqkv, w_qkv_c, xhat
    )
    dh_theirs = along("ctx", [dh_theirs], [partner(1)])[0]
    grad_qkv = rows_dot(h, dqkv).astype(bf16)
    qkv_parts = split_qkv_call(
        scalars,
        seqs,
        share,
        group,
        heads,
        lanes,
        grad_qkv,
        grad_out,
        halves,
        (sum_gain, sum_shift, dy_here, sum_qkv, sum_fc1),
    )
    qkv_parts = qkv_parts[:1] + along("seq", qkv_parts[1:], hops_s)
    dh_keep, *dh_sends = middle_call(scalars, piece, dh_mine, dh_theirs)
    dh_parts = along("ctx", dh_sends, hops_z)

    fc_home = sum_fc_call(scalars, share, fc_parts)
    fc_home = fc_home[:1] + along("ctx", fc_home[1:], hops_c)
    out_wout, *qkv_home = sum_qkv_call(scalars, share, width, rows, qkv_parts)
    qkv_home = qkv_home[:1] + along("ctx", qkv_home[1:], hops_c)
    grad_in = finish_call(scalars, x_here, dy_here, gain, dh_keep, dh_parts)
    out_wfc1, out_wfc2 = home_fc_call(scalars, fc_home, (grad_in,))
    out_wqkv, *small = home_qkv_call(
        scalars, group, heads, lanes, width, qkv_home, (out_wfc1,)
    )
    small = [value.reshape(-1) for value in small]
    return (
        block_out[None],
        grad_in[None],
        small[0],
        small[1],
        out_wqkv,
        small[3],
        out_wout,
        small[2],
        out_wfc1,
        small[4],
        out_wfc2,
        small[5],
    )


def solution(mesh):
    both = ("seq", "ctx")
    tokens, flat, matrix = P("seq", "ctx", None), P(both), P(both, None)
    in_specs = (tokens, tokens, P("seq", "ctx"), flat, flat) + (matrix, flat) * 4
    out_specs = (tokens, tokens, flat, flat) + (matrix, flat) * 4
    return jax.shard_map(body, mesh=mesh, in_specs=in_specs, out_specs=out_specs, check_vma=False)
```

```python
import math

import jax
import jax.numpy as jnp
from jax import lax
from jax.experimental import pallas as pl
from jax.experimental.pallas import tpu as pltpu
from jax.sharding import PartitionSpec as P

HEADS = 16
HEAD_DIM = 64
ROT = 16
HALF = ROT // 2
SMALL = 128

norm_eps = 1e-05
big_negative = -1e30
f32 = jnp.float32
bf16 = jnp.bfloat16


def dot(left, right):
    return lax.dot_general(left, right, (((1,), (0,)), ((), ())), preferred_element_type=f32)


def rows_dot(left, right):
    return lax.dot_general(left, right, (((0,), (0,)), ((), ())), preferred_element_type=f32)


def cols_dot(left, right):
    return lax.dot_general(left, right, (((1,), (1,)), ((), ())), preferred_element_type=f32)


def shape(dims, kind=bf16):
    return jax.ShapeDtypeStruct(dims, kind)


def held(array):
    *lead, low, high = (1, 1, *array.shape)
    size = jnp.dtype(array.dtype).itemsize
    lines = 32 // size
    return math.prod(lead) * (-(-low // lines) * lines) * (-(-high // 128) * 128) * size


def call(kernel, outs, scratch, scalars, operands, far=(), far_outs=(), after=(), room=3, cost=None):
    vmem = pl.BlockSpec(memory_space=pltpu.VMEM)
    hbm = pl.BlockSpec(memory_space=pl.ANY)
    count = len(operands) + len(far)

    def wrapped(*refs):
        kernel(places(scalars), *refs[:count], *refs[count + len(after) :])

    flops, moved = cost or (0, 0)
    moved = moved or sum(held(a) for a in [*operands, *far])
    limit = None
    if room:
        limit = sum(held(a) for a in scratch if "sem" not in str(a.dtype)) + (room << 20)
    results = pl.pallas_call(
        wrapped,
        in_specs=[vmem] * len(operands)
        + [hbm] * len(far)
        + [pl.BlockSpec(memory_space=pl.ANY)] * len(after),
        out_specs=[vmem] * len(outs) + [hbm] * len(far_outs),
        out_shape=[*outs, *far_outs],
        scratch_shapes=scratch,
        compiler_params=pltpu.CompilerParams(vmem_limit_bytes=limit),
        cost_estimate=pl.CostEstimate(flops=flops, bytes_accessed=moved, transcendentals=0),
    )(*operands, *far, *after)
    return list(results)


def places(group):
    s, c = lax.axis_index("seq"), lax.axis_index("ctx")
    return (lax.rem(c, 2), lax.div(c, 2), s, lax.rem(c, group), lax.div(c, group), c)


def start_all(pairs, sems):
    copies = [
        pltpu.make_async_copy(source, target, sems.at[at]) for at, (source, target) in enumerate(pairs)
    ]
    for copy in copies:
        copy.start()
    return copies


def wait_all(copies):
    for copy in copies:
        copy.wait()


def sems(count):
    return pltpu.SemaphoreType.DMA((count,))


def rows_at(index, count):
    return pl.ds(pl.multiple_of(index * count, count), count)


CORE, Z, S, SUB, LANE, CTX = range(6)


def at_c(at, k):
    return at[CTX] ^ k


def padded(total):
    return -(-total // 128) * 128


def head_lanes(to, part, i, heads, group, lanes, width):
    return part * width + (((to % group) * heads + i) * lanes + to // group) * HEAD_DIM


def pack_call(scalars, group, heads, lanes, w_qkv, w_fc1, w_fc2, vectors, seg):
    share, hidden = w_fc1.shape
    count = group * lanes
    cut = hidden // count
    total = 3 * heads * HEAD_DIM
    width = w_qkv.shape[1] // 3

    def kernel(at, qkv_ref, fc1_ref, fc2_ref, *refs):
        small_refs, seg_ref = refs[:6], refs[6]
        outs, (out_ref, small, sem) = refs[7 : 7 + count], refs[7 + count :]
        small[...] = jnp.zeros_like(small)
        for row, ref in enumerate(small_refs):
            small[row : row + 1, : ref.shape[0]] = ref[...].astype(f32).reshape(1, -1)
        last = len(small_refs)
        small[last : last + 1, : seg_ref.shape[1]] = seg_ref[...].astype(f32)
        rounded = small[...].astype(bf16)
        for to in range(count):
            for part in range(3):
                for i in range(heads):
                    begin = head_lanes(to, part, i, heads, group, lanes, width)
                    put = (part * heads + i) * HEAD_DIM
                    out_ref[to, :, put : put + HEAD_DIM] = qkv_ref[:, begin : begin + HEAD_DIM]
            base = padded(total) + SMALL
            out_ref[to, :, base - SMALL : base] = rounded
            out_ref[to, :, base : base + cut] = fc1_ref[:, to * cut : (to + 1) * cut]
            out_ref[to, :, base + cut :] = fc2_ref[:, to * cut : (to + 1) * cut]
        wait_all(start_all([(out_ref.at[at_c(at, k)], ref) for k, ref in enumerate(outs)], sem))

    return call(
        kernel,
        [],
        [
            pltpu.VMEM((count, share, padded(total) + SMALL + 2 * cut), bf16),
            pltpu.VMEM((share, SMALL), f32),
            sems(count),
        ],
        scalars,
        (w_qkv, w_fc1, w_fc2, *vectors, seg),
        far_outs=[shape((share, padded(total) + SMALL + 2 * cut))] * count,
        room=0,
    )


def stash_call(scalars, own, w_out):
    def kernel(at, own_ref, w_out_ref, near_ref, near_out_ref):
        near_ref[...] = own_ref[...]
        near_out_ref[...] = w_out_ref[...]

    return call(kernel, [shape(own.shape), shape(w_out.shape)], [], scalars, (own, w_out))


def collect_call(scalars, pieces, w_out, wide):
    count = len(pieces)
    share, lanes = pieces[0].shape
    width = w_out.shape[1]
    chunks = -(-width // wide)
    rows = count * share

    def kernel(at, *refs):
        far_refs, w_out_ref, (joint_ref, fc_ref, sem) = refs[:count], refs[count], refs[count + 1 :]
        pairs = []
        for k, ref in enumerate(far_refs):
            here = rows_at(at_c(at, k), share)
            pairs += [
                (ref.at[:, :wide], joint_ref.at[here, :]),
                (ref.at[:, wide:], fc_ref.at[here, :]),
            ]
        for j in range(chunks):
            upto = min(width - j * wide, wide)
            begin = rows + j * share
            pairs.append(
                (
                    w_out_ref.at[:, j * wide : j * wide + upto],
                    joint_ref.at[begin : begin + share, :upto],
                )
            )
        wait_all(start_all(pairs, sem))

    return call(
        kernel,
        [shape((rows + chunks * share, wide)), shape((rows, lanes - wide))],
        [sems(2 * count + chunks)],
        scalars,
        (),
        far=(*pieces, w_out),
    )


def spread_out_call(scalars, pieces, rows, share, width, group, heads, lanes, cut):
    seqs = len(pieces)
    wide = pieces[0].shape[1]
    chunks = -(-width // wide)
    total = 3 * heads * HEAD_DIM
    ctxs = rows // share
    sizes = (share, share, share, share, 3 * share, 4 * share)

    def kernel(at, *refs):
        far_refs, refs = refs[:seqs], refs[seqs:]
        *refs, local, sem = refs
        wait_all(start_all([(ref, local.at[k]) for k, ref in enumerate(far_refs)], sem))
        in_refs = [local.at[k] for k in range(seqs)]
        gain_ref, shift_ref, out_ref, qkv_ref, fc_ref = refs[:5]
        part_refs, stage, rows_refs, full = refs[5 : 5 + group], refs[5 + group], refs[6 + group : -1], refs[-1]
        for k, ref in enumerate(in_refs):
            slot = lax.rem(at[S] + k, seqs)
            for ctx in range(ctxs):
                block = ref[ctx * share : ctx * share + len(sizes), wide - SMALL :].astype(f32)
                for kind, n in enumerate(sizes):
                    rows_refs[kind][slot, :, ctx * n : (ctx + 1) * n] = block[kind : kind + 1, :n]
            for j in range(chunks):
                upto = min(width - j * wide, wide)
                begin = rows + j * share
                stage[slot, :, j * wide : j * wide + upto] = ref[begin : begin + share, :upto]
        for seq in range(seqs):
            cols = slice(seq * rows, (seq + 1) * rows)
            gain_ref[:, cols] = rows_refs[0][seq]
            shift_ref[:, cols] = rows_refs[1][seq]
            out_ref[:, cols] = rows_refs[2][seq] + rows_refs[3][seq]
            full[:, 3 * seq * rows : 3 * (seq + 1) * rows] = rows_refs[4][seq]
        for part in range(3):
            for i in range(heads):
                head = (at[SUB] * heads + i) * lanes + at[LANE]
                pair = full[:, pl.ds(pl.multiple_of(part * width + head // 2 * 128, 128), 128)]
                put = (part * heads + i) * HEAD_DIM
                low = jnp.full((1, HEAD_DIM), lax.rem(head, 2), jnp.int32) == 0
                qkv_ref[:, put : put + HEAD_DIM] = jnp.where(
                    low, pair[:, :HEAD_DIM], pair[:, HEAD_DIM:]
                )
        per_seq = 4 * rows
        begin = (at[LANE] * group + at[SUB]) * cut
        fc_ref[...] = rows_refs[5][
            begin // per_seq, :, pl.ds(pl.multiple_of(lax.rem(begin, per_seq), 128), cut)
        ]
        for k, ref in enumerate(part_refs):
            for i in range(heads):
                ref[i] = stage[(at[SUB] ^ k) * heads + i]

    return call(
        kernel,
        [shape((1, width), f32)] * 3
        + [shape((1, total), f32), shape((1, cut), f32)]
        + [shape((heads, share, width))] * group,
        [pltpu.VMEM((seqs, share, width), bf16)]
        + [pltpu.VMEM((seqs, 1, ctxs * n), f32) for n in sizes]
        + [pltpu.VMEM((1, 3 * width), f32), pltpu.VMEM((seqs, *pieces[0].shape), bf16), sems(seqs)],
        scalars,
        (),
        far=pieces,
    )


def tables_call(scalars, joint, rows, share, piece):
    ctxs = rows // share
    seq_len = ctxs * piece
    total = joint.shape[1] - SMALL
    powers = [float(10000.0 ** (-2.0 * i / ROT)) for i in range(HALF)]

    def kernel(at, far_ref, first_ref, cos_ref, sin_ref, seg_ref, joint_ref, sem):
        wait_all(start_all([(far_ref, joint_ref)], sem))
        for ctx in range(ctxs):
            block = joint_ref[ctx * share : ctx * share + 8, total : total + piece].astype(f32)
            seg_ref[:, ctx * piece : (ctx + 1) * piece] = block[6:7]
        seg = seg_ref[...]
        first = jnp.zeros((1, seq_len), f32)
        for name in range(1, 4):
            begin = jnp.sum((seg < name).astype(f32), axis=1, keepdims=True)
            first = jnp.where(seg >= name, begin, first)
        first_ref[...] = first.astype(jnp.int32)
        pos = lax.broadcasted_iota(jnp.int32, (HALF, seq_len), 1).astype(f32) - first
        which = lax.broadcasted_iota(jnp.int32, (HALF, seq_len), 0)
        freq = jnp.full((HALF, seq_len), powers[0], f32)
        for i in range(1, HALF):
            freq = jnp.where(which == i, powers[i], freq)
        angle = pos * freq
        cos_ref[...] = jnp.cos(angle)
        sin_ref[...] = jnp.sin(angle)

    return call(
        kernel,
        [shape((1, seq_len), jnp.int32), shape((HALF, seq_len), f32), shape((HALF, seq_len), f32)],
        [pltpu.VMEM((1, seq_len), f32), pltpu.VMEM(joint.shape, bf16), sems(1)],
        scalars,
        (),
        far=(joint,),
    )


def rope_t(x_t, cos_t, sin_t):
    parts = []
    for base in range(0, x_t.shape[0], HEAD_DIM):
        one, two = x_t[base : base + HALF], x_t[base + HALF : base + ROT]
        parts += [
            one * cos_t - two * sin_t,
            two * cos_t + one * sin_t,
            x_t[base + ROT : base + HEAD_DIM],
        ]
    return jnp.concatenate(parts, axis=0)


def scores_of(keys, queries_t, first, begin, here, limit):
    raw = dot(keys[:limit], queries_t[:, begin : begin + here])
    first = first[:, begin : begin + here]
    key_at = lax.broadcasted_iota(jnp.int32, (here, here), 0)
    query_at = lax.broadcasted_iota(jnp.int32, (here, here), 1)
    causal = (key_at <= query_at) & (key_at + begin >= first)
    parts = []
    if begin:
        early = lax.broadcasted_iota(jnp.int32, (begin, here), 0) >= first
        parts.append(jnp.where(early, raw[:begin], big_negative))
    parts.append(jnp.where(causal, raw[begin:], big_negative))
    return jnp.concatenate(parts, axis=0) if begin else parts[0]


def slots(at, refs):
    count = len(refs) // 2
    for k in range(count):
        here = 2 * lax.rem(at[Z] + k, count)
        yield refs[k], here + at[CORE]
        yield refs[count + k], here + 1 - at[CORE]


def attend_call(scalars, block, heads, rows, pieces, gain, shift, weights, bias, tables):
    piece, width = pieces[0].shape
    seq_len = piece * len(pieces)
    seqs = len(weights)
    total = 3 * heads * HEAD_DIM
    own = heads * HEAD_DIM
    tile = min(256, seq_len)

    def kernel(at, *refs):
        n = len(pieces)
        gain_ref, shift_ref, bias_ref, first_ref, cos_ref, sin_ref = refs[:6]
        x_refs, w_refs = refs[6 : 6 + n], refs[6 + n : 6 + n + seqs]
        h_ref, xhat_ref, out_ref, lse_ref, kept_ref, turned_ref, w_ref = refs[
            6 + n + seqs : 13 + n + seqs
        ]
        x_all, qkv, out_t, sem = refs[13 + n + seqs :]
        pairs = [(ref, x_all.at[rows_at(slot, piece), :]) for ref, slot in slots(at, x_refs)]
        pairs += [
            (ref.at[:rows, : padded(total)], w_ref.at[rows_at(lax.rem(at[S] + k, seqs), rows), :])
            for k, ref in enumerate(w_refs)
        ]
        wait_all(start_all(pairs, sem))

        def norm_tile(t, carry):
            here = rows_at(t, tile)
            x = x_all[here, :].astype(f32)
            centred = x - jnp.mean(x, axis=1, keepdims=True)
            rstd = lax.rsqrt(jnp.mean(centred * centred, axis=1, keepdims=True) + norm_eps)
            xhat = centred * rstd
            xhat_ref[here, :] = xhat.astype(bf16)
            h = (xhat * gain_ref[...] + shift_ref[...]).astype(bf16)
            h_ref[here, :] = h
            qkv[here, :] = dot(h, w_ref[:, :total]) + bias_ref[...]
            return carry

        lax.fori_loop(0, seq_len // tile, norm_tile, 0)
        cos_t, sin_t = cos_ref[...], sin_ref[...]
        q_t = rope_t(qkv[:, :own].T, cos_t, sin_t) * 0.125
        k_t = rope_t(qkv[:, own : 2 * own].T, cos_t, sin_t)
        v = qkv[:, 2 * own :]
        kb = k_t.T.astype(bf16)
        kept_ref[:, :own] = q_t.T.astype(bf16)
        kept_ref[:, own : 2 * own] = kb
        kept_ref[:, 2 * own :] = v.astype(bf16)
        q_t = q_t.astype(bf16)
        v_t = v.T.astype(bf16)
        turned_ref[:own] = q_t
        turned_ref[own:] = k_t.astype(bf16)
        begins = first_ref[...]
        for head in range(heads):
            lanes = slice(head * HEAD_DIM, (head + 1) * HEAD_DIM)
            keys, queries_t, values_t = kb[:, lanes], q_t[lanes], v_t[lanes]
            for begin in range(0, seq_len, block):
                limit = begin + block
                scores = scores_of(keys, queries_t, begins, begin, block, limit)
                top = jnp.max(scores, axis=0, keepdims=True)
                expd = jnp.exp(scores - top)
                sums = jnp.sum(expd, axis=0, keepdims=True)
                out = dot(values_t[:, :limit], expd.astype(bf16))
                out_t[lanes, begin:limit] = out * (1.0 / sums)
                lse_ref[head : head + 1, begin:limit] = top + jnp.log(sums)
        out_ref[...] = out_t[...].T.astype(bf16)

    return call(
        kernel,
        [
            shape((seq_len, width)),
            shape((seq_len, width)),
            shape((seq_len, own)),
            shape((heads, seq_len), f32),
            shape((seq_len, total)),
            shape((2 * own, seq_len)),
            shape((width, padded(total))),
        ],
        [
            pltpu.VMEM((seq_len, width), bf16),
            pltpu.VMEM((seq_len, total), f32),
            pltpu.VMEM((own, seq_len), f32),
            sems(len(pieces) + seqs),
        ],
        scalars,
        (gain, shift, bias, *tables),
        far=(*pieces, *weights),
        room=8 * (seq_len // 1024) ** 2,
        cost=(4 * seq_len * width * total, 0),
    )


def attend_back_call(scalars, block, heads, kept, turned, grad, lse, tables, after):
    seq_len, total = kept.shape
    own = total // 3

    def kernel(
        at, kept_ref, turned_ref, grad_ref, lse_ref, first_ref, cos_ref, sin_ref, out_ref, sum_ref, dq_t, dk, dv
    ):
        q = kept_ref[:, :own]
        k = kept_ref[:, own : 2 * own]
        v = kept_ref[:, 2 * own :]
        grad = grad_ref[...]
        q_t, k_t = turned_ref[:own], turned_ref[own:]
        grad_t = grad.astype(f32).T.astype(bf16)
        begins = first_ref[...]
        for head in range(heads):
            lanes = slice(head * HEAD_DIM, (head + 1) * HEAD_DIM)
            q_h, k_h, v_h, grad_h = q[:, lanes], k[:, lanes], v[:, lanes], grad[:, lanes]
            for begin in reversed(range(0, seq_len, block)):
                limit = begin + block
                scores = scores_of(k_h, q_t[lanes], begins, begin, block, limit)
                probs = jnp.exp(scores - lse_ref[head : head + 1, begin:limit])
                grad_p = dot(v_h[:limit], grad_t[lanes, begin:limit])
                delta = jnp.sum(probs * grad_p, axis=0, keepdims=True)
                grad_s = (probs * (grad_p - delta)).astype(bf16)
                dk_here = dot(grad_s, q_h[begin:limit])
                dv_here = dot(probs.astype(bf16), grad_h[begin:limit])
                if limit == seq_len:
                    dk[head] = dk_here
                    dv[head] = dv_here
                else:
                    dk[head, :limit] += dk_here
                    dv[head, :limit] += dv_here
                dq_t[lanes, begin:limit] = dot(k_t[lanes, :limit], grad_s)
        cos_t, sin_t = cos_ref[...], -sin_ref[...]
        dk_all = jnp.concatenate([dk[head] for head in range(heads)], axis=1)
        dv_all = jnp.concatenate([dv[head] for head in range(heads)], axis=1)
        for part, value in (
            (0, rope_t(dq_t[...] * 0.125, cos_t, sin_t).T),
            (1, rope_t(dk_all.T, cos_t, sin_t).T),
            (2, dv_all),
        ):
            rounded = value.astype(bf16)
            cols = slice(part * own, (part + 1) * own)
            out_ref[:, cols] = rounded
            sum_ref[:, cols] = jnp.sum(rounded.astype(f32), axis=0, keepdims=True)

    return call(
        kernel,
        [shape((seq_len, total)), shape((1, total), f32)],
        [
            pltpu.VMEM((own, seq_len), f32),
            pltpu.VMEM((heads, seq_len, HEAD_DIM), f32),
            pltpu.VMEM((heads, seq_len, HEAD_DIM), f32),
        ],
        scalars,
        (kept, turned, grad, lse, *tables),
        after=after,
        room=8 * (seq_len // 1024) ** 2,
        cost=(10 * seq_len * seq_len * own, 0),
    )


ROOT = 0.7978845608028654
CUBIC = 0.044715


def split_rows(at, z, piece, value, stage, mine_ref, theirs_ref, sem):
    stage[z] = value.astype(bf16)
    mine_ref[rows_at(z, piece), :] = stage[z, rows_at(at[CORE], piece), :]
    out_rows(at, z, piece, stage, theirs_ref, sem).start()


def out_rows(at, z, piece, stage, theirs_ref, sem):
    return pltpu.make_async_copy(
        stage.at[z, rows_at(1 - at[CORE], piece), :], theirs_ref.at[rows_at(z, piece), :], sem.at[z]
    )


def forward_call(scalars, rows, piece, h, weights, bias, attn, out_parts):
    seq_len, width = h.shape
    cut = weights[0].shape[1] // 2
    seqs = len(weights)
    tile = 2 * piece
    half = seq_len // 2
    count = seq_len // tile

    heads, share, _ = out_parts[0].shape
    group = len(out_parts)

    def kernel(at, h_ref, bias_ref, attn_ref, *refs):
        w_refs, part_refs, refs = refs[:seqs], refs[seqs : seqs + group], refs[seqs + group :]
        w_ref, slope_ref, act_ref, mine_ref, w_out_ref, theirs_ref, stage, sem, sem_out = refs
        pairs = [
            (ref, w_ref.at[rows_at(lax.rem(at[S] + k, seqs), rows), :])
            for k, ref in enumerate(w_refs)
        ]
        for k, ref in enumerate(part_refs):
            for i in range(heads):
                begin = i * HEAD_DIM + (at[SUB] ^ k) * share
                here = pl.ds(pl.multiple_of(begin, share), share)
                pairs.append((ref.at[i], w_out_ref.at[here, :]))
        wait_all(start_all(pairs, sem))

        def step(t, carry):
            here = rows_at(t, tile)
            v = dot(h_ref[here, :], w_ref[:, :cut]) + bias_ref[...]
            square = v * v
            t_v = jnp.tanh(ROOT * (v + CUBIC * (square * v)))
            halved = 0.5 * (1.0 + t_v)
            act = (v * halved).astype(bf16)
            act_ref[here, :] = act
            slope = halved + 0.5 * v * (1.0 - t_v * t_v) * (ROOT * (1.0 + (3.0 * CUBIC) * square))
            slope_ref[here, :] = slope.astype(bf16)
            out = dot(attn_ref[here, :], w_out_ref[...]) + cols_dot(act, w_ref[:, cut:])
            split_rows(at, t, piece, out, stage, mine_ref, theirs_ref, sem_out)
            return carry

        lax.fori_loop(0, count, step, 0)
        wait_all([out_rows(at, z, piece, stage, theirs_ref, sem_out) for z in range(count)])

    return call(
        kernel,
        [
            shape((width, 2 * cut)),
            shape((seq_len, cut)),
            shape((seq_len, cut)),
            shape((half, width)),
            shape((heads * HEAD_DIM, width)),
        ],
        [pltpu.VMEM((count, tile, width), bf16), sems(seqs + group * heads), sems(count)],
        scalars,
        (h, bias, attn),
        far=(*weights, *out_parts),
        far_outs=[shape((half, width))],
        cost=(4 * seq_len * width * cut, 0),
    )


def middle_call(scalars, piece, mine, theirs):
    half, width = mine.shape
    count = half // piece

    def kernel(at, mine_ref, theirs_ref, keep_ref, *refs):
        sends, (got, made, sem, sem_out) = refs[: count - 1], refs[count - 1 :]
        here = [rows_at(lax.rem(at[Z] + count - k, count), piece) for k in range(count)]
        order = [*range(1, count), 0]
        copies = start_all([(theirs_ref.at[here[k], :], got.at[k]) for k in order], sem)
        outs = []
        for copy, k in zip(copies, order):
            copy.wait()
            value = mine_ref[here[k], :].astype(f32) + got[k].astype(f32)
            if k == 0:
                keep_ref[...] = value
            else:
                made[k - 1] = value.astype(bf16)
                out = pltpu.make_async_copy(made.at[k - 1], sends[k - 1], sem_out.at[k - 1])
                out.start()
                outs.append(out)
        wait_all(outs)

    return call(
        kernel,
        [shape((piece, width), f32)],
        [
            pltpu.VMEM((count, piece, width), bf16),
            pltpu.VMEM((count - 1, piece, width), bf16),
            sems(count),
            sems(count - 1),
        ],
        scalars,
        (mine,),
        far=(theirs,),
        far_outs=[shape((piece, width))] * (count - 1),
    )


def backward_call(scalars, pieces, weight, w_out, slope):
    piece, width = pieces[0].shape
    seq_len, cut = slope.shape
    own = w_out.shape[0]
    tile = min(256, seq_len)

    def kernel(at, *refs):
        n = len(pieces)
        (w_ref, w_out_ref, slope_ref), dy_refs = refs[:3], refs[3 : 3 + n]
        dy_ref, dfc_ref, dattn_ref, sum_ref, sem = refs[3 + n :]
        pairs = [(ref, dy_ref.at[rows_at(slot, piece), :]) for ref, slot in slots(at, dy_refs)]
        wait_all(start_all(pairs, sem))
        sum_ref[...] = jnp.zeros_like(sum_ref)

        def step(t, carry):
            here = rows_at(t, tile)
            dy = dy_ref[here, :]
            dfc = (dot(dy, w_ref[:, cut:]) * slope_ref[here, :].astype(f32)).astype(bf16)
            dfc_ref[here, :] = dfc
            sum_ref[...] += jnp.sum(dfc.astype(f32), axis=0, keepdims=True)
            dattn_ref[here, :] = cols_dot(dy, w_out_ref[...]).astype(bf16)
            return carry

        lax.fori_loop(0, seq_len // tile, step, 0)

    return call(
        kernel,
        [shape((seq_len, width)), shape((seq_len, cut)), shape((seq_len, own)), shape((1, cut), f32)],
        [sems(len(pieces))],
        scalars,
        (weight, w_out, slope),
        far=pieces,
        cost=(2 * seq_len * width * cut, 0),
    )


def input_grad_call(scalars, piece, dfc, weight, dqkv, w_qkv, xhat):
    seq_len, cut = dfc.shape
    width = weight.shape[0]
    total = dqkv.shape[1]
    tile = 2 * piece
    half = seq_len // 2
    count = seq_len // tile

    def kernel(at, dfc_ref, w_ref, dqkv_ref, w_qkv_ref, xhat_ref, mine_ref, gain_ref, shift_ref, theirs_ref, stage, sem_out):
        gain_ref[...] = jnp.zeros_like(gain_ref)
        shift_ref[...] = jnp.zeros_like(shift_ref)

        def step(t, carry):
            here = rows_at(t, tile)
            value = cols_dot(dfc_ref[here, :], w_ref[:, :cut]) + cols_dot(
                dqkv_ref[here, :], w_qkv_ref[:, :total]
            )
            gain_ref[...] += jnp.sum(value * xhat_ref[here, :].astype(f32), axis=0, keepdims=True)
            shift_ref[...] += jnp.sum(value, axis=0, keepdims=True)
            split_rows(at, t, piece, value, stage, mine_ref, theirs_ref, sem_out)
            return carry

        lax.fori_loop(0, count, step, 0)
        wait_all([out_rows(at, z, piece, stage, theirs_ref, sem_out) for z in range(count)])

    return call(
        kernel,
        [shape((half, width)), shape((1, width), f32), shape((1, width), f32)],
        [pltpu.VMEM((count, tile, width), bf16), sems(count)],
        scalars,
        (dfc, weight, dqkv, w_qkv, xhat),
        far_outs=[shape((half, width))],
        cost=(2 * seq_len * width * cut, 0),
    )


def split_fc_call(scalars, seqs, share, group, grad_fc1, grad_fc2, grad_out):
    width, cut = grad_fc1.shape
    rows = width // seqs
    heads = grad_out.shape[0] // HEAD_DIM

    def kernel(at, one_ref, two_ref, out_grad_ref, *refs):
        outs, halves, sem = refs[:seqs], refs[seqs:-1], refs[-1]
        pairs = []
        for k, ref in enumerate(halves):
            for i in range(heads):
                begin = i * HEAD_DIM + (at[SUB] ^ (k + 1)) * share
                here = pl.ds(pl.multiple_of(begin, share), share)
                pairs.append((out_grad_ref.at[here, :], ref.at[i]))
        for k, ref in enumerate(outs):
            here = rows_at(lax.rem(at[S] + seqs - k, seqs), rows)
            pairs += [
                (one_ref.at[here, :], ref.at[:, :cut]),
                (two_ref.at[here, :], ref.at[:, cut:]),
            ]
        wait_all(start_all(pairs, sem))

    return call(
        kernel,
        [],
        [sems(2 * seqs + (group - 1) * heads)],
        scalars,
        (grad_fc1, grad_fc2, grad_out),
        far_outs=[shape((rows, 2 * cut))] * seqs + [shape((heads, share, width))] * (group - 1),
    )


def sum_fc_call(scalars, share, pieces):
    rows, lanes = pieces[0].shape
    count = len(pieces)
    tiles = 2
    ctxs = rows // share
    tile = rows // tiles

    def kernel(at, *refs):
        far_refs, outs, (got, made, sem, sem_out) = (
            refs[:count],
            refs[count : count + ctxs],
            refs[count + ctxs :],
        )
        starts = [slice(t * tile, (t + 1) * tile) for t in range(tiles)]
        copies = start_all(
            [(ref.at[here, :], got.at[k, here, :]) for here in starts for k, ref in enumerate(far_refs)],
            sem,
        )
        for t, here in enumerate(starts):
            wait_all(copies[t * count : (t + 1) * count])
            made[here, :] = sum(got[k, here, :].astype(f32) for k in range(count)).astype(bf16)
        wait_all(
            start_all(
                [(made.at[rows_at(at_c(at, k), share), :], ref) for k, ref in enumerate(outs)], sem_out
            )
        )

    return call(
        kernel,
        [],
        [
            pltpu.VMEM((count, rows, lanes), bf16),
            pltpu.VMEM((rows, lanes), bf16),
            sems(tiles * count),
            sems(ctxs),
        ],
        scalars,
        (),
        far=pieces,
        far_outs=[shape((share, lanes))] * ctxs,
    )


def small_rows(share):
    return 5, (2 if share >= 10 else 1)


def put_small(block_ref, base, share, lane0, values):
    kinds, parts = small_rows(share)
    for kind, value in enumerate(values):
        high = value.astype(bf16)
        block_ref[base + kind : base + kind + 1, lane0 : lane0 + value.shape[1]] = high.astype(f32)
        if parts == 2:
            row = base + kinds + kind
            block_ref[row : row + 1, lane0 : lane0 + value.shape[1]] = value - high.astype(f32)


def split_qkv_call(scalars, seqs, share, group, heads, lanes_c, grad_qkv, grad_out, halves, vectors):
    width, total = grad_qkv.shape
    rows = width // seqs
    lanes = padded(total) + SMALL
    chunks = -(-width // lanes)
    out_rows = rows + chunks * share
    ctxs = rows // share

    def kernel(at, qkv_ref, out_grad_ref, *refs):
        half_refs, refs = refs[: group - 1], refs[group - 1 :]
        (gain_ref, shift_ref, dy_ref, sum_qkv_ref, sum_fc_ref) = refs[:5]
        outs, (stage, small, full_y, full_qkv, full_fc, sem) = refs[5 : 5 + seqs], refs[5 + seqs :]
        full_y[...] = jnp.sum(dy_ref[...].astype(f32), axis=0, keepdims=True)
        full_qkv[...] = jnp.zeros_like(full_qkv)
        full_fc[...] = jnp.zeros_like(full_fc)
        cut = sum_fc_ref.shape[1]
        begin = (at[LANE] * group + at[SUB]) * cut
        full_fc[:, pl.ds(pl.multiple_of(begin, cut), cut)] = sum_fc_ref[...]
        nothing = jnp.zeros((1, HEAD_DIM), f32)
        for part in range(3):
            for i in range(heads):
                head = (at[SUB] * heads + i) * lanes_c + at[LANE]
                take = (part * heads + i) * HEAD_DIM
                value = sum_qkv_ref[:, take : take + HEAD_DIM]
                low = jnp.full((1, 2 * HEAD_DIM), lax.rem(head, 2), jnp.int32) == 0
                put = pl.ds(pl.multiple_of(part * width + head // 2 * 128, 128), 128)
                full_qkv[:, put] = jnp.where(
                    low,
                    jnp.concatenate([value, nothing], axis=1),
                    jnp.concatenate([nothing, value], axis=1),
                )
        vector_refs = (gain_ref, shift_ref, full_y, full_qkv, full_fc)

        def put_out(slot, value):
            for j in range(chunks):
                upto = min(width - j * lanes, lanes)
                begin = rows + j * share
                stage[slot, begin : begin + share, :upto] = value[:, j * lanes : j * lanes + upto]

        for k in range(group):
            for i in range(heads):
                slot = (at[SUB] ^ k) * heads + i
                if k:
                    put_out(slot, half_refs[k - 1][i])
                else:
                    here = pl.ds(pl.multiple_of(i * HEAD_DIM + at[SUB] * share, share), share)
                    put_out(slot, out_grad_ref[here, :])
        small[...] = jnp.zeros_like(small)
        sizes = [ref.shape[1] // (seqs * ctxs) for ref in vector_refs]
        for seq in range(seqs):
            for ctx in range(ctxs):
                owner = seq * ctxs + ctx
                values = [
                    ref[:, owner * n : (owner + 1) * n] for ref, n in zip(vector_refs, sizes)
                ]
                put_small(small, ctx * share, share, 0, values)
            stage[seq, :rows, :total] = qkv_ref[seq * rows : (seq + 1) * rows, :]
            stage[seq, :rows, lanes - SMALL :] = small[...].astype(bf16)
        wait_all(
            start_all(
                [(stage.at[lax.rem(at[S] + seqs - k, seqs)], ref) for k, ref in enumerate(outs)], sem
            )
        )

    return call(
        kernel,
        [],
        [
            pltpu.VMEM((seqs, out_rows, lanes), bf16),
            pltpu.VMEM((rows, SMALL), f32),
            pltpu.VMEM((1, width), f32),
            pltpu.VMEM((1, 3 * width), f32),
            pltpu.VMEM((1, 4 * width), f32),
            sems(seqs),
        ],
        scalars,
        (grad_qkv, grad_out, *halves, *vectors),
        far_outs=[shape((out_rows, lanes))] * seqs,
    )


def sum_qkv_call(scalars, share, width, rows, pieces):
    lanes = pieces[0].shape[1]
    chunks = -(-width // lanes)
    kinds, parts = small_rows(share)
    ctxs = rows // share

    def kernel(at, *refs):
        far_refs, w_out_ref, refs = refs[: len(pieces)], refs[len(pieces)], refs[len(pieces) + 1 :]
        outs, (sums, got, made, sem, sem_out) = refs[:ctxs], refs[ctxs:]
        wait_all(start_all([(ref, got.at[k]) for k, ref in enumerate(far_refs)], sem))
        sums[...] = sum(got[k].astype(f32) for k in range(len(pieces)))
        for j in range(chunks):
            upto = min(width - j * lanes, lanes)
            begin = rows + j * share
            w_out_ref[:, j * lanes : j * lanes + upto] = sums[begin : begin + share, :upto]
        if parts == 2:
            for ctx in range(ctxs):
                base = ctx * share
                here = sums[base : base + kinds, lanes - SMALL :]
                left = sums[base + kinds : base + 2 * kinds, lanes - SMALL :]
                value = here + left
                high = value.astype(bf16).astype(f32)
                sums[base : base + kinds, lanes - SMALL :] = high
                sums[base + kinds : base + 2 * kinds, lanes - SMALL :] = value - high
        made[...] = sums[:rows, :].astype(bf16)
        wait_all(
            start_all(
                [(made.at[rows_at(at_c(at, k), share), :], ref) for k, ref in enumerate(outs)], sem_out
            )
        )

    return call(
        kernel,
        [shape((share, width), f32)],
        [
            pltpu.VMEM(pieces[0].shape, f32),
            pltpu.VMEM((len(pieces), *pieces[0].shape), bf16),
            pltpu.VMEM((rows, lanes), bf16),
            sems(len(pieces)),
            sems(ctxs),
        ],
        scalars,
        (),
        far=pieces,
        far_outs=[shape((share, lanes))] * ctxs,
    )


def home_fc_call(scalars, pieces, after):
    ctxs = len(pieces)
    share, double = pieces[0].shape
    cut = double // 2

    def kernel(at, *refs):
        far_refs, (one_ref, two_ref, done_ref, got, sem) = refs[:ctxs], refs[ctxs:]
        done_ref[...] = jnp.zeros_like(done_ref)
        wait_all(start_all([(ref, got.at[at_c(at, k)]) for k, ref in enumerate(far_refs)], sem))
        for ctx in range(ctxs):
            cols = slice(ctx * cut, (ctx + 1) * cut)
            one_ref[:, cols] = got[ctx, :, :cut].astype(f32)
            two_ref[:, cols] = got[ctx, :, cut:].astype(f32)

    return call(
        kernel,
        [shape((share, ctxs * cut), f32)] * 2 + [shape((1, 128), f32)],
        [pltpu.VMEM((ctxs, share, double), bf16), sems(ctxs)],
        scalars,
        (),
        far=pieces,
        after=after,
        room=4,
    )


def home_qkv_call(scalars, group, heads, lanes, width, pieces, after):
    ctxs = len(pieces)
    share, wide = pieces[0].shape
    kinds, parts = small_rows(share)
    sizes = (share, share, share, 3 * share, 4 * share, share)
    kind_of = (0, 1, 2, 3, 4, 2)

    def kernel(at, *refs):
        far_refs, out_ref, refs = refs[:ctxs], refs[ctxs], refs[ctxs + 1 :]
        *small_refs, got_ref, sem = refs
        wait_all(start_all([(ref, got_ref.at[at_c(at, k)]) for k, ref in enumerate(far_refs)], sem))
        for ctx in range(ctxs):
            for part in range(3):
                for i in range(heads):
                    put = head_lanes(ctx, part, i, heads, group, lanes, width)
                    take = (part * heads + i) * HEAD_DIM
                    out_ref[:, put : put + HEAD_DIM] = got_ref[
                        ctx, :, take : take + HEAD_DIM
                    ].astype(f32)
        sums = sum(got_ref[ctx, :, wide - SMALL :].astype(f32) for ctx in range(ctxs))
        for kind, n, ref in zip(kind_of, sizes, small_refs):
            value = sums[kind : kind + 1, :]
            if parts == 2:
                value = value + sums[kinds + kind : kinds + kind + 1, :]
            ref[...] = value[:, :n]

    return call(
        kernel,
        [shape((share, 3 * width), f32)] + [shape((1, n), f32) for n in sizes],
        [pltpu.VMEM((ctxs, share, wide), bf16), sems(ctxs)],
        scalars,
        (),
        far=pieces,
        after=after,
        room=4,
    )


def emit_call(scalars, x, bias, keep, parts):
    count = len(parts)

    def kernel(at, x_ref, bias_ref, keep_ref, *refs):
        far_refs, (out_ref, got, sem) = refs[:count], refs[count:]
        wait_all(start_all([(ref, got.at[k]) for k, ref in enumerate(far_refs)], sem))
        value = x_ref[...].astype(f32) + keep_ref[...] + bias_ref[...]
        out_ref[...] = (value + sum(got[k].astype(f32) for k in range(count))).astype(bf16)

    return call(
        kernel,
        [shape(x.shape)],
        [pltpu.VMEM((count, *x.shape), bf16), sems(count)],
        scalars,
        (x, bias, keep),
        far=parts,
    )[0]


def finish_call(scalars, x, dy, gain, keep, parts):
    count = len(parts)

    def kernel(at, x_ref, dy_ref, gain_ref, keep_ref, *refs):
        far_refs, (out_ref, done_ref, got, sem) = refs[:count], refs[count:]
        done_ref[...] = jnp.zeros_like(done_ref)
        copies = start_all([(ref, got.at[k]) for k, ref in enumerate(far_refs)], sem)
        here = x_ref[...].astype(f32)
        centred = here - jnp.mean(here, axis=1, keepdims=True)
        rstd = lax.rsqrt(jnp.mean(centred * centred, axis=1, keepdims=True) + norm_eps)
        xhat = centred * rstd
        wait_all(copies)
        dh = keep_ref[...] + sum(got[k].astype(f32) for k in range(count))
        scaled = dh * gain_ref[...]
        out_ref[...] = dy_ref[...].astype(f32) + rstd * (
            scaled
            - jnp.mean(scaled, axis=1, keepdims=True)
            - xhat * jnp.mean(scaled * xhat, axis=1, keepdims=True)
        )

    return call(
        kernel,
        [shape(x.shape, f32), shape((1, 128), f32)],
        [pltpu.VMEM((count, *x.shape), bf16), sems(count)],
        scalars,
        (x, dy, gain, keep),
        far=parts,
        room=6,
    )


def body(
    block_in,
    cotangent,
    segments,
    ln_gain,
    ln_bias,
    w_qkv,
    b_qkv,
    w_out,
    b_out,
    w_fc1,
    b_fc1,
    w_fc2,
    b_fc2,
):
    seqs, ctxs = lax.axis_size("seq"), lax.axis_size("ctx")
    _, piece, width = block_in.shape
    seq_len = piece * ctxs
    share = w_qkv.shape[0]
    hidden = w_fc1.shape[1]
    cut = hidden // ctxs
    heads = HEADS // ctxs
    group = HEAD_DIM // share
    lanes = ctxs // group
    rows = ctxs * share
    zs = ctxs // 2
    scalars = group
    total = 3 * heads * HEAD_DIM
    x_here, dy_here = block_in[0], cotangent[0]

    def from_z(k):
        return [(i, ((i // 2 - k) % zs) * 2 + i % 2) for i in range(ctxs)]

    def from_s(k):
        return [(i, (i - k) % seqs) for i in range(seqs)]

    def partner(k):
        return [(i, i ^ k) for i in range(ctxs)]

    def along(axis, parts, pairs):
        out = []
        for part, pair in zip(parts, pairs):
            out.append(lax.ppermute(part, axis, pair))
        return out

    hops_z = [from_z(k) for k in range(1, zs)]
    hops_s = [from_s(k) for k in range(1, seqs)]
    hops_c = [partner(k) for k in range(1, ctxs)]
    hops_g = [partner(k) for k in range(1, group)]

    def spread_ctx(local):
        mine = [local] + along("ctx", [local] * (zs - 1), hops_z)
        return mine + along("ctx", mine, [partner(1)] * zs)

    packed = pack_call(
        scalars,
        group,
        heads,
        lanes,
        w_qkv,
        w_fc1,
        w_fc2,
        (ln_gain, ln_bias, b_out, b_fc2, b_qkv, b_fc1),
        segments,
    )
    wide = padded(total) + SMALL
    near, near_out = stash_call(scalars, packed[0], w_out)
    got = [near] + along("ctx", packed[1:], hops_c)
    joint, fc_here = collect_call(scalars, got, near_out, wide)
    joint = [joint] + along("seq", [joint] * (seqs - 1), hops_s)
    w_fc = [fc_here] + along("seq", [fc_here] * (seqs - 1), hops_s)
    x_all = spread_ctx(x_here)
    dy_all = spread_ctx(dy_here)

    tables = tables_call(scalars, joint[0], rows, share, piece)
    gain, shift, bias_out, bias_qkv, bias_fc1, *out_parts = spread_out_call(
        scalars, joint, rows, share, width, group, heads, lanes, cut
    )
    out_parts = out_parts[:1] + along("ctx", out_parts[1:], hops_g)

    block = min(256, seq_len)
    h, xhat, attn, lse, kept, turned, w_qkv_c = attend_call(
        scalars, block, heads, rows, x_all, gain, shift, joint, bias_qkv, tables
    )
    w_fc_c, slope, act, out_mine, w_out_c, out_theirs = forward_call(
        scalars, rows, piece, h, w_fc, bias_fc1, attn, out_parts
    )
    out_theirs = along("ctx", [out_theirs], [partner(1)])[0]
    out_keep, *out_sends = middle_call(scalars, piece, out_mine, out_theirs)
    out_parts = along("ctx", out_sends, hops_z)
    block_out = emit_call(scalars, x_here, bias_out, out_keep, out_parts)

    dy, dfc, dattn, sum_fc1 = backward_call(scalars, dy_all, w_fc_c, w_out_c, slope)
    grad_fc1 = rows_dot(h, dfc).astype(bf16)
    grad_fc2 = rows_dot(dy, act).astype(bf16)
    grad_out = rows_dot(attn, dy).astype(bf16)
    split = split_fc_call(scalars, seqs, share, group, grad_fc1, grad_fc2, grad_out)
    fc_parts, halves = split[:seqs], split[seqs:]
    fc_parts = fc_parts[:1] + along("seq", fc_parts[1:], hops_s)
    halves = along("ctx", halves, hops_g)
    dqkv, sum_qkv = attend_back_call(
        scalars, block, heads, kept, turned, dattn, lse, tables, (fc_parts[0],)
    )
    dh_mine, sum_gain, sum_shift, dh_theirs = input_grad_call(
        scalars, piece, dfc, w_fc_c, dqkv, w_qkv_c, xhat
    )
    dh_theirs = along("ctx", [dh_theirs], [partner(1)])[0]
    grad_qkv = rows_dot(h, dqkv).astype(bf16)
    qkv_parts = split_qkv_call(
        scalars,
        seqs,
        share,
        group,
        heads,
        lanes,
        grad_qkv,
        grad_out,
        halves,
        (sum_gain, sum_shift, dy_here, sum_qkv, sum_fc1),
    )
    qkv_parts = qkv_parts[:1] + along("seq", qkv_parts[1:], hops_s)
    dh_keep, *dh_sends = middle_call(scalars, piece, dh_mine, dh_theirs)
    dh_parts = along("ctx", dh_sends, hops_z)

    fc_home = sum_fc_call(scalars, share, fc_parts)
    fc_home = fc_home[:1] + along("ctx", fc_home[1:], hops_c)
    out_wout, *qkv_home = sum_qkv_call(scalars, share, width, rows, qkv_parts)
    qkv_home = qkv_home[:1] + along("ctx", qkv_home[1:], hops_c)
    grad_in, finished = finish_call(scalars, x_here, dy_here, gain, dh_keep, dh_parts)
    out_wfc1, out_wfc2, finished = home_fc_call(scalars, fc_home, (finished,))
    out_wqkv, *small = home_qkv_call(
        scalars, group, heads, lanes, width, qkv_home, (finished,)
    )
    small = [value.reshape(-1) for value in small]
    return (
        block_out[None],
        grad_in[None],
        small[0],
        small[1],
        out_wqkv,
        small[3],
        out_wout,
        small[2],
        out_wfc1,
        small[4],
        out_wfc2,
        small[5],
    )


def solution(mesh):
    both = ("seq", "ctx")
    tokens, flat, matrix = P("seq", "ctx", None), P(both), P(both, None)
    in_specs = (tokens, tokens, P("seq", "ctx"), flat, flat) + (matrix, flat) * 4
    out_specs = (tokens, tokens, flat, flat) + (matrix, flat) * 4
    return jax.shard_map(body, mesh=mesh, in_specs=in_specs, out_specs=out_specs, check_vma=False)
```

```python
import math

import jax
import jax.numpy as jnp
from jax import lax
from jax.experimental import pallas as pl
from jax.experimental.pallas import tpu as pltpu
from jax.sharding import PartitionSpec as P

HEADS = 16
HEAD_DIM = 64
ROT = 16
HALF = ROT // 2
SMALL = 128

norm_eps = 1e-05
big_negative = -1e30
f32 = jnp.float32
bf16 = jnp.bfloat16


def dot(left, right):
    return lax.dot_general(left, right, (((1,), (0,)), ((), ())), preferred_element_type=f32)


def rows_dot(left, right):
    return lax.dot_general(left, right, (((0,), (0,)), ((), ())), preferred_element_type=f32)


def cols_dot(left, right):
    return lax.dot_general(left, right, (((1,), (1,)), ((), ())), preferred_element_type=f32)


def shape(dims, kind=bf16):
    return jax.ShapeDtypeStruct(dims, kind)


def held(array):
    *lead, low, high = (1, 1, *array.shape)
    size = jnp.dtype(array.dtype).itemsize
    lines = 32 // size
    return math.prod(lead) * (-(-low // lines) * lines) * (-(-high // 128) * 128) * size


def call(kernel, outs, scratch, scalars, operands, far=(), far_outs=(), after=(), room=3, cost=None):
    vmem = pl.BlockSpec(memory_space=pltpu.VMEM)
    hbm = pl.BlockSpec(memory_space=pl.ANY)
    count = len(operands) + len(far)

    def wrapped(*refs):
        kernel(places(scalars), *refs[:count], *refs[count + len(after) :])

    flops, moved = cost or (0, 0)
    moved = moved or sum(held(a) for a in [*operands, *far])
    limit = None
    if room:
        limit = sum(held(a) for a in scratch if "sem" not in str(a.dtype)) + (room << 20)
    results = pl.pallas_call(
        wrapped,
        in_specs=[vmem] * len(operands)
        + [hbm] * len(far)
        + [pl.BlockSpec(memory_space=pl.ANY)] * len(after),
        out_specs=[vmem] * len(outs) + [hbm] * len(far_outs),
        out_shape=[*outs, *far_outs],
        scratch_shapes=scratch,
        compiler_params=pltpu.CompilerParams(vmem_limit_bytes=limit),
        cost_estimate=pl.CostEstimate(flops=flops, bytes_accessed=moved, transcendentals=0),
    )(*operands, *far, *after)
    return list(results)


def places(group):
    s, c = lax.axis_index("seq"), lax.axis_index("ctx")
    return (lax.rem(c, 2), lax.div(c, 2), s, lax.rem(c, group), lax.div(c, group), c)


def start_all(pairs, sems):
    copies = [
        pltpu.make_async_copy(source, target, sems.at[at]) for at, (source, target) in enumerate(pairs)
    ]
    for copy in copies:
        copy.start()
    return copies


def wait_all(copies):
    for copy in copies:
        copy.wait()


def sems(count):
    return pltpu.SemaphoreType.DMA((count,))


def rows_at(index, count):
    return pl.ds(pl.multiple_of(index * count, count), count)


CORE, Z, S, SUB, LANE, CTX = range(6)


def at_c(at, k):
    return at[CTX] ^ k


def padded(total):
    return -(-total // 128) * 128


def packed_rows(kinds, wide):
    return -(-kinds // (wide // SMALL))


def packed_at(ctx, kind, kinds, wide):
    a_row = wide // SMALL
    row = ctx * packed_rows(kinds, wide) + kind // a_row
    return slice(row, row + 1), kind % a_row * SMALL


GIVEN = 7
SUMS = 10


def head_lanes(to, part, i, heads, group, lanes, width):
    return part * width + (((to % group) * heads + i) * lanes + to // group) * HEAD_DIM


def pack_call(scalars, group, heads, lanes, w_qkv, w_fc1, w_fc2, vectors, seg):
    share, hidden = w_fc1.shape
    count = group * lanes
    cut = hidden // count
    total = 3 * heads * HEAD_DIM
    width = w_qkv.shape[1] // 3

    def kernel(at, qkv_ref, fc1_ref, fc2_ref, *refs):
        small_refs, seg_ref = refs[:6], refs[6]
        outs, (out_ref, small, sem) = refs[7 : 7 + count], refs[7 + count :]
        small[...] = jnp.zeros_like(small)
        for row, ref in enumerate(small_refs):
            small[row : row + 1, : ref.shape[0]] = ref[...].astype(f32).reshape(1, -1)
        last = len(small_refs)
        small[last : last + 1, : seg_ref.shape[1]] = seg_ref[...].astype(f32)
        rounded = small[...].astype(bf16)
        for to in range(count):
            for part in range(3):
                for i in range(heads):
                    begin = head_lanes(to, part, i, heads, group, lanes, width)
                    put = (part * heads + i) * HEAD_DIM
                    out_ref[to, :, put : put + HEAD_DIM] = qkv_ref[:, begin : begin + HEAD_DIM]
            base = padded(total) + SMALL
            out_ref[to, :, base - SMALL : base] = rounded
            out_ref[to, :, base : base + cut] = fc1_ref[:, to * cut : (to + 1) * cut]
            out_ref[to, :, base + cut :] = fc2_ref[:, to * cut : (to + 1) * cut]
        wait_all(start_all([(out_ref.at[at_c(at, k)], ref) for k, ref in enumerate(outs)], sem))

    return call(
        kernel,
        [],
        [
            pltpu.VMEM((count, share, padded(total) + SMALL + 2 * cut), bf16),
            pltpu.VMEM((share, SMALL), f32),
            sems(count),
        ],
        scalars,
        (w_qkv, w_fc1, w_fc2, *vectors, seg),
        far_outs=[shape((share, padded(total) + SMALL + 2 * cut))] * count,
        room=0,
    )


def stash_call(scalars, own, w_out):
    def kernel(at, own_ref, w_out_ref, near_ref, near_out_ref):
        near_ref[...] = own_ref[...]
        near_out_ref[...] = w_out_ref[...]

    return call(kernel, [shape(own.shape), shape(w_out.shape)], [], scalars, (own, w_out))


def collect_call(scalars, pieces, w_out, wide):
    count = len(pieces)
    share, lanes = pieces[0].shape
    width = w_out.shape[1]
    base = wide - SMALL
    rows = count * share
    extra = count * packed_rows(GIVEN, wide)
    few = min(share, 16)

    def kernel(at, *refs):
        far_refs, w_out_ref, (joint_ref, fc_ref, small, spread, sem) = (
            refs[:count],
            refs[count],
            refs[count + 1 :],
        )
        pairs = []
        for k, ref in enumerate(far_refs):
            here = rows_at(at_c(at, k), share)
            pairs += [
                (ref.at[:few, base:wide], small.at[at_c(at, k)]),
                (ref.at[:, :base], joint_ref.at[here, :base]),
                (ref.at[:, wide:], fc_ref.at[here, :]),
            ]
        for j in range(width // SMALL):
            pairs.append(
                (
                    w_out_ref.at[:, j * SMALL : (j + 1) * SMALL],
                    joint_ref.at[j * share : (j + 1) * share, base:],
                )
            )
        copies = start_all(pairs, sem)
        for copy in copies[: 3 * count : 3]:
            copy.wait()
        spread[...] = jnp.zeros_like(spread)
        for ctx in range(count):
            block = small[ctx].astype(f32)
            for kind in range(GIVEN):
                row, lane = packed_at(ctx, kind, GIVEN, wide)
                spread[row, lane : lane + SMALL] = block[kind : kind + 1]
        joint_ref[rows:, :] = spread[...].astype(bf16)
        for index, copy in enumerate(copies):
            if index >= 3 * count or index % 3:
                copy.wait()

    return call(
        kernel,
        [shape((rows + extra, wide)), shape((rows, lanes - wide))],
        [
            pltpu.VMEM((count, few, SMALL), bf16),
            pltpu.VMEM((extra, wide), f32),
            sems(3 * count + width // SMALL),
        ],
        scalars,
        (),
        far=(*pieces, w_out),
    )


def spread_out_call(scalars, pieces, rows, share, width, group, heads, lanes, cut):
    seqs = len(pieces)
    wide = pieces[0].shape[1]
    total = 3 * heads * HEAD_DIM
    ctxs = rows // share
    sizes = (share, share, share, share, 3 * share, 4 * share)

    def kernel(at, *refs):
        far_refs, refs = refs[:seqs], refs[seqs:]
        *refs, local, sem = refs
        wait_all(start_all([(ref, local.at[k]) for k, ref in enumerate(far_refs)], sem))
        in_refs = [local.at[k] for k in range(seqs)]
        gain_ref, shift_ref, out_ref, qkv_ref, fc_ref = refs[:5]
        part_refs, stage, rows_refs, full = refs[5 : 5 + group], refs[5 + group], refs[6 + group : -1], refs[-1]
        for k, ref in enumerate(in_refs):
            slot = lax.rem(at[S] + k, seqs)
            block = ref[rows:, :].astype(f32)
            for ctx in range(ctxs):
                for kind, n in enumerate(sizes):
                    row, lane_at = packed_at(ctx, kind, GIVEN, wide)
                    rows_refs[kind][slot, :, ctx * n : (ctx + 1) * n] = block[
                        row, lane_at : lane_at + n
                    ]
            for j in range(width // SMALL):
                stage[slot, :, j * SMALL : (j + 1) * SMALL] = ref[
                    j * share : (j + 1) * share, wide - SMALL :
                ]
        for seq in range(seqs):
            cols = slice(seq * rows, (seq + 1) * rows)
            gain_ref[:, cols] = rows_refs[0][seq]
            shift_ref[:, cols] = rows_refs[1][seq]
            out_ref[:, cols] = rows_refs[2][seq] + rows_refs[3][seq]
            full[:, 3 * seq * rows : 3 * (seq + 1) * rows] = rows_refs[4][seq]
        for part in range(3):
            for i in range(heads):
                head = (at[SUB] * heads + i) * lanes + at[LANE]
                pair = full[:, pl.ds(pl.multiple_of(part * width + head // 2 * 128, 128), 128)]
                put = (part * heads + i) * HEAD_DIM
                low = jnp.full((1, HEAD_DIM), lax.rem(head, 2), jnp.int32) == 0
                qkv_ref[:, put : put + HEAD_DIM] = jnp.where(
                    low, pair[:, :HEAD_DIM], pair[:, HEAD_DIM:]
                )
        per_seq = 4 * rows
        begin = (at[LANE] * group + at[SUB]) * cut
        fc_ref[...] = rows_refs[5][
            begin // per_seq, :, pl.ds(pl.multiple_of(lax.rem(begin, per_seq), 128), cut)
        ]
        for k, ref in enumerate(part_refs):
            for i in range(heads):
                ref[i] = stage[(at[SUB] ^ k) * heads + i]

    return call(
        kernel,
        [shape((1, width), f32)] * 3
        + [shape((1, total), f32), shape((1, cut), f32)]
        + [shape((heads, share, width))] * group,
        [pltpu.VMEM((seqs, share, width), bf16)]
        + [pltpu.VMEM((seqs, 1, ctxs * n), f32) for n in sizes]
        + [pltpu.VMEM((1, 3 * width), f32), pltpu.VMEM((seqs, *pieces[0].shape), bf16), sems(seqs)],
        scalars,
        (),
        far=pieces,
    )


def tables_call(scalars, joint, rows, share, piece):
    ctxs = rows // share
    seq_len = ctxs * piece
    wide = joint.shape[1]
    powers = [float(10000.0 ** (-2.0 * i / ROT)) for i in range(HALF)]

    def kernel(at, far_ref, first_ref, cos_ref, sin_ref, seg_ref, joint_ref, sem):
        wait_all(start_all([(far_ref, joint_ref)], sem))
        block = joint_ref[rows:, :].astype(f32)
        for ctx in range(ctxs):
            row, lane = packed_at(ctx, GIVEN - 1, GIVEN, wide)
            seg_ref[:, ctx * piece : (ctx + 1) * piece] = block[row, lane : lane + piece]
        seg = seg_ref[...]
        first = jnp.zeros((1, seq_len), f32)
        for name in range(1, 4):
            begin = jnp.sum((seg < name).astype(f32), axis=1, keepdims=True)
            first = jnp.where(seg >= name, begin, first)
        first_ref[...] = first.astype(jnp.int32)
        pos = lax.broadcasted_iota(jnp.int32, (HALF, seq_len), 1).astype(f32) - first
        which = lax.broadcasted_iota(jnp.int32, (HALF, seq_len), 0)
        freq = jnp.full((HALF, seq_len), powers[0], f32)
        for i in range(1, HALF):
            freq = jnp.where(which == i, powers[i], freq)
        angle = pos * freq
        cos_ref[...] = jnp.cos(angle)
        sin_ref[...] = jnp.sin(angle)

    return call(
        kernel,
        [shape((1, seq_len), jnp.int32), shape((HALF, seq_len), f32), shape((HALF, seq_len), f32)],
        [pltpu.VMEM((1, seq_len), f32), pltpu.VMEM(joint.shape, bf16), sems(1)],
        scalars,
        (),
        far=(joint,),
    )


def rope_t(x_t, cos_t, sin_t):
    parts = []
    for base in range(0, x_t.shape[0], HEAD_DIM):
        one, two = x_t[base : base + HALF], x_t[base + HALF : base + ROT]
        parts += [
            one * cos_t - two * sin_t,
            two * cos_t + one * sin_t,
            x_t[base + ROT : base + HEAD_DIM],
        ]
    return jnp.concatenate(parts, axis=0)


def scores_of(keys, queries_t, first, begin, here, limit):
    raw = dot(keys[:limit], queries_t[:, begin : begin + here])
    first = first[:, begin : begin + here]
    key_at = lax.broadcasted_iota(jnp.int32, (here, here), 0)
    query_at = lax.broadcasted_iota(jnp.int32, (here, here), 1)
    causal = (key_at <= query_at) & (key_at + begin >= first)
    parts = []
    if begin:
        early = lax.broadcasted_iota(jnp.int32, (begin, here), 0) >= first
        parts.append(jnp.where(early, raw[:begin], big_negative))
    parts.append(jnp.where(causal, raw[begin:], big_negative))
    return jnp.concatenate(parts, axis=0) if begin else parts[0]


def slots(at, refs):
    count = len(refs) // 2
    for k in range(count):
        here = 2 * lax.rem(at[Z] + k, count)
        yield refs[k], here + at[CORE]
        yield refs[count + k], here + 1 - at[CORE]


def attend_call(scalars, block, heads, rows, pieces, gain, shift, weights, bias, tables):
    piece, width = pieces[0].shape
    seq_len = piece * len(pieces)
    seqs = len(weights)
    total = 3 * heads * HEAD_DIM
    own = heads * HEAD_DIM
    tile = min(512, seq_len)

    def kernel(at, *refs):
        n = len(pieces)
        gain_ref, shift_ref, bias_ref, first_ref, cos_ref, sin_ref = refs[:6]
        x_refs, w_refs = refs[6 : 6 + n], refs[6 + n : 6 + n + seqs]
        h_ref, xhat_ref, out_ref, lse_ref, kept_ref, turned_ref, w_ref = refs[
            6 + n + seqs : 13 + n + seqs
        ]
        x_all, qkv, out_t, sem = refs[13 + n + seqs :]
        pairs = [(ref, x_all.at[rows_at(slot, piece), :]) for ref, slot in slots(at, x_refs)]
        pairs += [
            (ref.at[:rows, : padded(total)], w_ref.at[rows_at(lax.rem(at[S] + k, seqs), rows), :])
            for k, ref in enumerate(w_refs)
        ]
        wait_all(start_all(pairs, sem))

        def norm_tile(t, carry):
            here = rows_at(t, tile)
            x = x_all[here, :].astype(f32)
            centred = x - jnp.mean(x, axis=1, keepdims=True)
            rstd = lax.rsqrt(jnp.mean(centred * centred, axis=1, keepdims=True) + norm_eps)
            xhat = centred * rstd
            xhat_ref[here, :] = xhat.astype(bf16)
            h = (xhat * gain_ref[...] + shift_ref[...]).astype(bf16)
            h_ref[here, :] = h
            qkv[here, :] = dot(h, w_ref[:, :total]) + bias_ref[...]
            return carry

        lax.fori_loop(0, seq_len // tile, norm_tile, 0)
        cos_t, sin_t = cos_ref[...], sin_ref[...]
        q_t = rope_t(qkv[:, :own].T, cos_t, sin_t) * 0.125
        k_t = rope_t(qkv[:, own : 2 * own].T, cos_t, sin_t)
        v = qkv[:, 2 * own :]
        kb = k_t.T.astype(bf16)
        kept_ref[:, :own] = q_t.T.astype(bf16)
        kept_ref[:, own : 2 * own] = kb
        kept_ref[:, 2 * own :] = v.astype(bf16)
        q_t = q_t.astype(bf16)
        v_t = v.T.astype(bf16)
        turned_ref[:own] = q_t
        turned_ref[own:] = k_t.astype(bf16)
        begins = first_ref[...]
        for head in range(heads):
            lanes = slice(head * HEAD_DIM, (head + 1) * HEAD_DIM)
            keys, queries_t, values_t = kb[:, lanes], q_t[lanes], v_t[lanes]
            for begin in range(0, seq_len, block):
                limit = begin + block
                scores = scores_of(keys, queries_t, begins, begin, block, limit)
                top = jnp.max(scores, axis=0, keepdims=True)
                expd = jnp.exp(scores - top)
                sums = jnp.sum(expd, axis=0, keepdims=True)
                out = dot(values_t[:, :limit], expd.astype(bf16))
                out_t[lanes, begin:limit] = out * (1.0 / sums)
                lse_ref[head : head + 1, begin:limit] = top + jnp.log(sums)
        out_ref[...] = out_t[...].T.astype(bf16)

    return call(
        kernel,
        [
            shape((seq_len, width)),
            shape((seq_len, width)),
            shape((seq_len, own)),
            shape((heads, seq_len), f32),
            shape((seq_len, total)),
            shape((2 * own, seq_len)),
            shape((width, padded(total))),
        ],
        [
            pltpu.VMEM((seq_len, width), bf16),
            pltpu.VMEM((seq_len, total), f32),
            pltpu.VMEM((own, seq_len), f32),
            sems(len(pieces) + seqs),
        ],
        scalars,
        (gain, shift, bias, *tables),
        far=(*pieces, *weights),
        room=8 * (seq_len // 1024) ** 2,
        cost=(4 * seq_len * width * total, 0),
    )


def attend_back_call(scalars, block, heads, kept, turned, grad, lse, tables, after):
    seq_len, total = kept.shape
    own = total // 3

    def kernel(
        at, kept_ref, turned_ref, grad_ref, lse_ref, first_ref, cos_ref, sin_ref, out_ref, sum_ref, dq_t, dk, dv
    ):
        q = kept_ref[:, :own]
        k = kept_ref[:, own : 2 * own]
        v = kept_ref[:, 2 * own :]
        grad = grad_ref[...]
        q_t, k_t = turned_ref[:own], turned_ref[own:]
        grad_t = grad.astype(f32).T.astype(bf16)
        begins = first_ref[...]
        for head in range(heads):
            lanes = slice(head * HEAD_DIM, (head + 1) * HEAD_DIM)
            q_h, k_h, v_h, grad_h = q[:, lanes], k[:, lanes], v[:, lanes], grad[:, lanes]
            for begin in reversed(range(0, seq_len, block)):
                limit = begin + block
                scores = scores_of(k_h, q_t[lanes], begins, begin, block, limit)
                probs = jnp.exp(scores - lse_ref[head : head + 1, begin:limit])
                grad_p = dot(v_h[:limit], grad_t[lanes, begin:limit])
                delta = jnp.sum(probs * grad_p, axis=0, keepdims=True)
                grad_s = (probs * (grad_p - delta)).astype(bf16)
                dk_here = dot(grad_s, q_h[begin:limit])
                dv_here = dot(probs.astype(bf16), grad_h[begin:limit])
                if limit == seq_len:
                    dk[head] = dk_here
                    dv[head] = dv_here
                else:
                    dk[head, :limit] += dk_here
                    dv[head, :limit] += dv_here
                dq_t[lanes, begin:limit] = dot(k_t[lanes, :limit], grad_s)
        cos_t, sin_t = cos_ref[...], -sin_ref[...]
        dk_all = jnp.concatenate([dk[head] for head in range(heads)], axis=1)
        dv_all = jnp.concatenate([dv[head] for head in range(heads)], axis=1)
        for part, value in (
            (0, rope_t(dq_t[...] * 0.125, cos_t, sin_t).T),
            (1, rope_t(dk_all.T, cos_t, sin_t).T),
            (2, dv_all),
        ):
            rounded = value.astype(bf16)
            cols = slice(part * own, (part + 1) * own)
            out_ref[:, cols] = rounded
            sum_ref[:, cols] = jnp.sum(rounded.astype(f32), axis=0, keepdims=True)

    return call(
        kernel,
        [shape((seq_len, total)), shape((1, total), f32)],
        [
            pltpu.VMEM((own, seq_len), f32),
            pltpu.VMEM((heads, seq_len, HEAD_DIM), f32),
            pltpu.VMEM((heads, seq_len, HEAD_DIM), f32),
        ],
        scalars,
        (kept, turned, grad, lse, *tables),
        after=after,
        room=8 * (seq_len // 1024) ** 2,
        cost=(10 * seq_len * seq_len * own, 0),
    )


ROOT = 0.7978845608028654
CUBIC = 0.044715


def split_rows(at, z, piece, value, stage, mine_ref, theirs_ref, sem):
    stage[z] = value.astype(bf16)
    mine_ref[rows_at(z, piece), :] = stage[z, rows_at(at[CORE], piece), :]
    out_rows(at, z, piece, stage, theirs_ref, sem).start()


def out_rows(at, z, piece, stage, theirs_ref, sem):
    return pltpu.make_async_copy(
        stage.at[z, rows_at(1 - at[CORE], piece), :], theirs_ref.at[rows_at(z, piece), :], sem.at[z]
    )


def forward_call(scalars, rows, piece, h, weights, bias, attn, out_parts):
    seq_len, width = h.shape
    cut = weights[0].shape[1] // 2
    seqs = len(weights)
    tile = 2 * piece
    half = seq_len // 2
    count = seq_len // tile

    heads, share, _ = out_parts[0].shape
    group = len(out_parts)

    def kernel(at, h_ref, bias_ref, attn_ref, *refs):
        w_refs, part_refs, refs = refs[:seqs], refs[seqs : seqs + group], refs[seqs + group :]
        w_ref, slope_ref, act_ref, mine_ref, w_out_ref, theirs_ref, stage, sem, sem_out = refs
        pairs = [
            (ref, w_ref.at[rows_at(lax.rem(at[S] + k, seqs), rows), :])
            for k, ref in enumerate(w_refs)
        ]
        for k, ref in enumerate(part_refs):
            for i in range(heads):
                begin = i * HEAD_DIM + (at[SUB] ^ k) * share
                here = pl.ds(pl.multiple_of(begin, share), share)
                pairs.append((ref.at[i], w_out_ref.at[here, :]))
        wait_all(start_all(pairs, sem))

        def step(t, carry):
            here = rows_at(t, 2 * tile)
            v = dot(h_ref[here, :], w_ref[:, :cut]) + bias_ref[...]
            square = v * v
            t_v = jnp.tanh(ROOT * (v + CUBIC * (square * v)))
            halved = 0.5 * (1.0 + t_v)
            act = (v * halved).astype(bf16)
            act_ref[here, :] = act
            slope = halved + 0.5 * v * (1.0 - t_v * t_v) * (ROOT * (1.0 + (3.0 * CUBIC) * square))
            slope_ref[here, :] = slope.astype(bf16)
            out = dot(attn_ref[here, :], w_out_ref[...]) + cols_dot(act, w_ref[:, cut:])
            for u in range(2):
                part = out[u * tile : (u + 1) * tile]
                split_rows(at, 2 * t + u, piece, part, stage, mine_ref, theirs_ref, sem_out)
            return carry

        lax.fori_loop(0, count // 2, step, 0)
        wait_all([out_rows(at, z, piece, stage, theirs_ref, sem_out) for z in range(count)])

    return call(
        kernel,
        [
            shape((width, 2 * cut)),
            shape((seq_len, cut)),
            shape((seq_len, cut)),
            shape((half, width)),
            shape((heads * HEAD_DIM, width)),
        ],
        [pltpu.VMEM((count, tile, width), bf16), sems(seqs + group * heads), sems(count)],
        scalars,
        (h, bias, attn),
        far=(*weights, *out_parts),
        far_outs=[shape((half, width))],
        room=8,
        cost=(4 * seq_len * width * cut, 0),
    )


def middle_call(scalars, piece, mine, theirs):
    half, width = mine.shape
    count = half // piece

    def kernel(at, mine_ref, theirs_ref, keep_ref, *refs):
        sends, (got, made, sem, sem_out) = refs[: count - 1], refs[count - 1 :]
        here = [rows_at(lax.rem(at[Z] + count - k, count), piece) for k in range(count)]
        order = [*range(1, count), 0]
        copies = start_all([(theirs_ref.at[here[k], :], got.at[k]) for k in order], sem)
        outs = []
        for copy, k in zip(copies, order):
            copy.wait()
            value = mine_ref[here[k], :].astype(f32) + got[k].astype(f32)
            if k == 0:
                keep_ref[...] = value
            else:
                made[k - 1] = value.astype(bf16)
                out = pltpu.make_async_copy(made.at[k - 1], sends[k - 1], sem_out.at[k - 1])
                out.start()
                outs.append(out)
        wait_all(outs)

    return call(
        kernel,
        [shape((piece, width), f32)],
        [
            pltpu.VMEM((count, piece, width), bf16),
            pltpu.VMEM((count - 1, piece, width), bf16),
            sems(count),
            sems(count - 1),
        ],
        scalars,
        (mine,),
        far=(theirs,),
        far_outs=[shape((piece, width))] * (count - 1),
    )


def backward_call(scalars, pieces, weight, w_out, slope):
    piece, width = pieces[0].shape
    seq_len, cut = slope.shape
    own = w_out.shape[0]
    tile = min(512, seq_len)

    def kernel(at, *refs):
        n = len(pieces)
        (w_ref, w_out_ref, slope_ref), dy_refs = refs[:3], refs[3 : 3 + n]
        dy_ref, dfc_ref, dattn_ref, sum_ref, sem = refs[3 + n :]
        pairs = [(ref, dy_ref.at[rows_at(slot, piece), :]) for ref, slot in slots(at, dy_refs)]
        wait_all(start_all(pairs, sem))
        sum_ref[...] = jnp.zeros_like(sum_ref)

        def step(t, carry):
            here = rows_at(t, tile)
            dy = dy_ref[here, :]
            dfc = (dot(dy, w_ref[:, cut:]) * slope_ref[here, :].astype(f32)).astype(bf16)
            dfc_ref[here, :] = dfc
            sum_ref[...] += jnp.sum(dfc.astype(f32), axis=0, keepdims=True)
            dattn_ref[here, :] = cols_dot(dy, w_out_ref[...]).astype(bf16)
            return carry

        lax.fori_loop(0, seq_len // tile, step, 0)

    return call(
        kernel,
        [shape((seq_len, width)), shape((seq_len, cut)), shape((seq_len, own)), shape((1, cut), f32)],
        [sems(len(pieces))],
        scalars,
        (weight, w_out, slope),
        far=pieces,
        room=6,
        cost=(2 * seq_len * width * cut, 0),
    )


def input_grad_call(scalars, piece, dfc, weight, dqkv, w_qkv, xhat):
    seq_len, cut = dfc.shape
    width = weight.shape[0]
    total = dqkv.shape[1]
    tile = 2 * piece
    half = seq_len // 2
    count = seq_len // tile

    def kernel(at, dfc_ref, w_ref, dqkv_ref, w_qkv_ref, xhat_ref, mine_ref, gain_ref, shift_ref, theirs_ref, stage, sem_out):
        gain_ref[...] = jnp.zeros_like(gain_ref)
        shift_ref[...] = jnp.zeros_like(shift_ref)

        def step(t, carry):
            here = rows_at(t, 2 * tile)
            value = cols_dot(dfc_ref[here, :], w_ref[:, :cut]) + cols_dot(
                dqkv_ref[here, :], w_qkv_ref[:, :total]
            )
            gain_ref[...] += jnp.sum(value * xhat_ref[here, :].astype(f32), axis=0, keepdims=True)
            shift_ref[...] += jnp.sum(value, axis=0, keepdims=True)
            for u in range(2):
                part = value[u * tile : (u + 1) * tile]
                split_rows(at, 2 * t + u, piece, part, stage, mine_ref, theirs_ref, sem_out)
            return carry

        lax.fori_loop(0, count // 2, step, 0)
        wait_all([out_rows(at, z, piece, stage, theirs_ref, sem_out) for z in range(count)])

    return call(
        kernel,
        [shape((half, width)), shape((1, width), f32), shape((1, width), f32)],
        [pltpu.VMEM((count, tile, width), bf16), sems(count)],
        scalars,
        (dfc, weight, dqkv, w_qkv, xhat),
        far_outs=[shape((half, width))],
        room=8,
        cost=(2 * seq_len * width * cut, 0),
    )


def split_fc_call(scalars, seqs, share, group, grad_fc1, grad_fc2, grad_out):
    width, cut = grad_fc1.shape
    rows = width // seqs
    heads = grad_out.shape[0] // HEAD_DIM

    def kernel(at, one_ref, two_ref, out_grad_ref, *refs):
        outs, halves, sem = refs[:seqs], refs[seqs:-1], refs[-1]
        pairs = []
        for k, ref in enumerate(halves):
            for i in range(heads):
                begin = i * HEAD_DIM + (at[SUB] ^ (k + 1)) * share
                here = pl.ds(pl.multiple_of(begin, share), share)
                pairs.append((out_grad_ref.at[here, :], ref.at[i]))
        for k, ref in enumerate(outs):
            here = rows_at(lax.rem(at[S] + seqs - k, seqs), rows)
            pairs += [
                (one_ref.at[here, :], ref.at[:, :cut]),
                (two_ref.at[here, :], ref.at[:, cut:]),
            ]
        wait_all(start_all(pairs, sem))

    return call(
        kernel,
        [],
        [sems(2 * seqs + (group - 1) * heads)],
        scalars,
        (grad_fc1, grad_fc2, grad_out),
        far_outs=[shape((rows, 2 * cut))] * seqs + [shape((heads, share, width))] * (group - 1),
    )


def sum_fc_call(scalars, share, pieces):
    rows, lanes = pieces[0].shape
    count = len(pieces)
    tiles = 2
    ctxs = rows // share
    tile = rows // tiles

    def kernel(at, *refs):
        far_refs, outs, (got, made, sem, sem_out) = (
            refs[:count],
            refs[count : count + ctxs],
            refs[count + ctxs :],
        )
        starts = [slice(t * tile, (t + 1) * tile) for t in range(tiles)]
        copies = start_all(
            [(ref.at[here, :], got.at[k, here, :]) for here in starts for k, ref in enumerate(far_refs)],
            sem,
        )
        for t, here in enumerate(starts):
            wait_all(copies[t * count : (t + 1) * count])
            made[here, :] = sum(got[k, here, :].astype(f32) for k in range(count)).astype(bf16)
        wait_all(
            start_all(
                [(made.at[rows_at(at_c(at, k), share), :], ref) for k, ref in enumerate(outs)], sem_out
            )
        )

    return call(
        kernel,
        [],
        [
            pltpu.VMEM((count, rows, lanes), bf16),
            pltpu.VMEM((rows, lanes), bf16),
            sems(tiles * count),
            sems(ctxs),
        ],
        scalars,
        (),
        far=pieces,
        far_outs=[shape((share, lanes))] * ctxs,
    )


def small_rows(share):
    return 5, (2 if share >= 10 else 1)


def split_qkv_call(scalars, seqs, share, group, heads, lanes_c, grad_qkv, grad_out, halves, vectors):
    width, total = grad_qkv.shape
    rows = width // seqs
    base = padded(total)
    lanes = base + SMALL
    ctxs = rows // share
    extra = ctxs * packed_rows(SUMS, lanes)
    out_rows = rows + extra

    def kernel(at, qkv_ref, out_grad_ref, *refs):
        half_refs, refs = refs[: group - 1], refs[group - 1 :]
        (gain_ref, shift_ref, dy_ref, sum_qkv_ref, sum_fc_ref) = refs[:5]
        outs, (stage, small, full_y, full_qkv, full_fc, sem) = refs[5 : 5 + seqs], refs[5 + seqs :]
        full_y[...] = jnp.sum(dy_ref[...].astype(f32), axis=0, keepdims=True)
        full_qkv[...] = jnp.zeros_like(full_qkv)
        full_fc[...] = jnp.zeros_like(full_fc)
        cut = sum_fc_ref.shape[1]
        begin = (at[LANE] * group + at[SUB]) * cut
        full_fc[:, pl.ds(pl.multiple_of(begin, cut), cut)] = sum_fc_ref[...]
        nothing = jnp.zeros((1, HEAD_DIM), f32)
        for part in range(3):
            for i in range(heads):
                head = (at[SUB] * heads + i) * lanes_c + at[LANE]
                take = (part * heads + i) * HEAD_DIM
                value = sum_qkv_ref[:, take : take + HEAD_DIM]
                low = jnp.full((1, 2 * HEAD_DIM), lax.rem(head, 2), jnp.int32) == 0
                put = pl.ds(pl.multiple_of(part * width + head // 2 * 128, 128), 128)
                full_qkv[:, put] = jnp.where(
                    low,
                    jnp.concatenate([value, nothing], axis=1),
                    jnp.concatenate([nothing, value], axis=1),
                )
        vector_refs = (gain_ref, shift_ref, full_y, full_qkv, full_fc)

        def put_out(slot, value):
            for j in range(width // SMALL):
                stage[slot, j * share : (j + 1) * share, base:] = value[
                    :, j * SMALL : (j + 1) * SMALL
                ]

        for k in range(group):
            for i in range(heads):
                slot = (at[SUB] ^ k) * heads + i
                if k:
                    put_out(slot, half_refs[k - 1][i])
                else:
                    here = pl.ds(pl.multiple_of(i * HEAD_DIM + at[SUB] * share, share), share)
                    put_out(slot, out_grad_ref[here, :])
        small[...] = jnp.zeros_like(small)
        sizes = [ref.shape[1] // (seqs * ctxs) for ref in vector_refs]
        for seq in range(seqs):
            for ctx in range(ctxs):
                owner = seq * ctxs + ctx
                for kind, (ref, n) in enumerate(zip(vector_refs, sizes)):
                    value = ref[:, owner * n : (owner + 1) * n]
                    high = value.astype(bf16).astype(f32)
                    row, lane = packed_at(ctx, kind, SUMS, lanes)
                    small[row, lane : lane + n] = high
                    row, lane = packed_at(ctx, kind + SUMS // 2, SUMS, lanes)
                    small[row, lane : lane + n] = value - high
            stage[seq, :rows, :total] = qkv_ref[seq * rows : (seq + 1) * rows, :]
            stage[seq, rows:, :] = small[...].astype(bf16)
        wait_all(
            start_all(
                [(stage.at[lax.rem(at[S] + seqs - k, seqs)], ref) for k, ref in enumerate(outs)], sem
            )
        )

    return call(
        kernel,
        [],
        [
            pltpu.VMEM((seqs, out_rows, lanes), bf16),
            pltpu.VMEM((extra, lanes), f32),
            pltpu.VMEM((1, width), f32),
            pltpu.VMEM((1, 3 * width), f32),
            pltpu.VMEM((1, 4 * width), f32),
            sems(seqs),
        ],
        scalars,
        (grad_qkv, grad_out, *halves, *vectors),
        far_outs=[shape((out_rows, lanes))] * seqs,
    )


def sum_qkv_call(scalars, share, width, rows, pieces):
    lanes = pieces[0].shape[1]
    base = lanes - SMALL
    kinds, parts = small_rows(share)
    ctxs = rows // share

    def kernel(at, *refs):
        far_refs, w_out_ref, refs = refs[: len(pieces)], refs[len(pieces)], refs[len(pieces) + 1 :]
        outs, (sums, small, got, made, sem, sem_out) = refs[:ctxs], refs[ctxs:]
        wait_all(start_all([(ref, got.at[k]) for k, ref in enumerate(far_refs)], sem))
        sums[...] = sum(got[k].astype(f32) for k in range(len(pieces)))
        for j in range(width // SMALL):
            w_out_ref[:, j * SMALL : (j + 1) * SMALL] = sums[j * share : (j + 1) * share, base:]
        small[...] = jnp.zeros_like(small)
        block = sums[rows:, :]
        for ctx in range(ctxs):
            for kind in range(kinds):
                row, lane = packed_at(ctx, kind, SUMS, lanes)
                left, left_lane = packed_at(ctx, kind + SUMS // 2, SUMS, lanes)
                value = block[row, lane : lane + SMALL] + block[left, left_lane : left_lane + SMALL]
                high = value.astype(bf16).astype(f32)
                put = ctx * share + kind
                small[put : put + 1] = high
                if parts == 2:
                    small[put + kinds : put + kinds + 1] = value - high
        made[:, :base] = sums[:rows, :base].astype(bf16)
        made[:, base:] = small[...].astype(bf16)
        wait_all(
            start_all(
                [(made.at[rows_at(at_c(at, k), share), :], ref) for k, ref in enumerate(outs)], sem_out
            )
        )

    return call(
        kernel,
        [shape((share, width), f32)],
        [
            pltpu.VMEM(pieces[0].shape, f32),
            pltpu.VMEM((rows, SMALL), f32),
            pltpu.VMEM((len(pieces), *pieces[0].shape), bf16),
            pltpu.VMEM((rows, lanes), bf16),
            sems(len(pieces)),
            sems(ctxs),
        ],
        scalars,
        (),
        far=pieces,
        far_outs=[shape((share, lanes))] * ctxs,
    )


def home_fc_call(scalars, pieces, after):
    ctxs = len(pieces)
    share, double = pieces[0].shape
    cut = double // 2

    def kernel(at, *refs):
        far_refs, (one_ref, two_ref, done_ref, got, sem) = refs[:ctxs], refs[ctxs:]
        done_ref[...] = jnp.zeros_like(done_ref)
        wait_all(start_all([(ref, got.at[at_c(at, k)]) for k, ref in enumerate(far_refs)], sem))
        for ctx in range(ctxs):
            cols = slice(ctx * cut, (ctx + 1) * cut)
            one_ref[:, cols] = got[ctx, :, :cut].astype(f32)
            two_ref[:, cols] = got[ctx, :, cut:].astype(f32)

    return call(
        kernel,
        [shape((share, ctxs * cut), f32)] * 2 + [shape((1, 128), f32)],
        [pltpu.VMEM((ctxs, share, double), bf16), sems(ctxs)],
        scalars,
        (),
        far=pieces,
        after=after,
        room=4,
    )


def home_qkv_call(scalars, group, heads, lanes, width, pieces, after):
    ctxs = len(pieces)
    share, wide = pieces[0].shape
    kinds, parts = small_rows(share)
    sizes = (share, share, share, 3 * share, 4 * share, share)
    kind_of = (0, 1, 2, 3, 4, 2)

    def kernel(at, *refs):
        far_refs, out_ref, refs = refs[:ctxs], refs[ctxs], refs[ctxs + 1 :]
        *small_refs, got_ref, sem = refs
        wait_all(start_all([(ref, got_ref.at[at_c(at, k)]) for k, ref in enumerate(far_refs)], sem))
        for ctx in range(ctxs):
            for part in range(3):
                for i in range(heads):
                    put = head_lanes(ctx, part, i, heads, group, lanes, width)
                    take = (part * heads + i) * HEAD_DIM
                    out_ref[:, put : put + HEAD_DIM] = got_ref[
                        ctx, :, take : take + HEAD_DIM
                    ].astype(f32)
        sums = sum(got_ref[ctx, :, wide - SMALL :].astype(f32) for ctx in range(ctxs))
        for kind, n, ref in zip(kind_of, sizes, small_refs):
            value = sums[kind : kind + 1, :]
            if parts == 2:
                value = value + sums[kinds + kind : kinds + kind + 1, :]
            ref[...] = value[:, :n]

    return call(
        kernel,
        [shape((share, 3 * width), f32)] + [shape((1, n), f32) for n in sizes],
        [pltpu.VMEM((ctxs, share, wide), bf16), sems(ctxs)],
        scalars,
        (),
        far=pieces,
        after=after,
        room=4,
    )


def emit_call(scalars, x, bias, keep, parts):
    count = len(parts)

    def kernel(at, x_ref, bias_ref, keep_ref, *refs):
        far_refs, (out_ref, got, sem) = refs[:count], refs[count:]
        wait_all(start_all([(ref, got.at[k]) for k, ref in enumerate(far_refs)], sem))
        value = x_ref[...].astype(f32) + keep_ref[...] + bias_ref[...]
        out_ref[...] = (value + sum(got[k].astype(f32) for k in range(count))).astype(bf16)

    return call(
        kernel,
        [shape(x.shape)],
        [pltpu.VMEM((count, *x.shape), bf16), sems(count)],
        scalars,
        (x, bias, keep),
        far=parts,
    )[0]


def finish_call(scalars, x, dy, gain, keep, parts):
    count = len(parts)

    def kernel(at, x_ref, dy_ref, gain_ref, keep_ref, *refs):
        far_refs, (out_ref, done_ref, got, sem) = refs[:count], refs[count:]
        done_ref[...] = jnp.zeros_like(done_ref)
        copies = start_all([(ref, got.at[k]) for k, ref in enumerate(far_refs)], sem)
        here = x_ref[...].astype(f32)
        centred = here - jnp.mean(here, axis=1, keepdims=True)
        rstd = lax.rsqrt(jnp.mean(centred * centred, axis=1, keepdims=True) + norm_eps)
        xhat = centred * rstd
        wait_all(copies)
        dh = keep_ref[...] + sum(got[k].astype(f32) for k in range(count))
        scaled = dh * gain_ref[...]
        out_ref[...] = dy_ref[...].astype(f32) + rstd * (
            scaled
            - jnp.mean(scaled, axis=1, keepdims=True)
            - xhat * jnp.mean(scaled * xhat, axis=1, keepdims=True)
        )

    return call(
        kernel,
        [shape(x.shape, f32), shape((1, 128), f32)],
        [pltpu.VMEM((count, *x.shape), bf16), sems(count)],
        scalars,
        (x, dy, gain, keep),
        far=parts,
        room=6,
    )


def body(
    block_in,
    cotangent,
    segments,
    ln_gain,
    ln_bias,
    w_qkv,
    b_qkv,
    w_out,
    b_out,
    w_fc1,
    b_fc1,
    w_fc2,
    b_fc2,
):
    seqs, ctxs = lax.axis_size("seq"), lax.axis_size("ctx")
    _, piece, width = block_in.shape
    seq_len = piece * ctxs
    share = w_qkv.shape[0]
    hidden = w_fc1.shape[1]
    cut = hidden // ctxs
    heads = HEADS // ctxs
    group = HEAD_DIM // share
    lanes = ctxs // group
    rows = ctxs * share
    zs = ctxs // 2
    scalars = group
    total = 3 * heads * HEAD_DIM
    x_here, dy_here = block_in[0], cotangent[0]

    def from_z(k):
        return [(i, ((i // 2 - k) % zs) * 2 + i % 2) for i in range(ctxs)]

    def from_s(k):
        return [(i, (i - k) % seqs) for i in range(seqs)]

    def partner(k):
        return [(i, i ^ k) for i in range(ctxs)]

    def along(axis, parts, pairs):
        out = []
        for part, pair in zip(parts, pairs):
            out.append(lax.ppermute(part, axis, pair))
        return out

    hops_z = [from_z(k) for k in range(1, zs)]
    hops_s = [from_s(k) for k in range(1, seqs)]
    hops_c = [partner(k) for k in range(1, ctxs)]
    hops_g = [partner(k) for k in range(1, group)]

    def spread_ctx(local):
        mine = [local] + along("ctx", [local] * (zs - 1), hops_z)
        return mine + along("ctx", mine, [partner(1)] * zs)

    packed = pack_call(
        scalars,
        group,
        heads,
        lanes,
        w_qkv,
        w_fc1,
        w_fc2,
        (ln_gain, ln_bias, b_out, b_fc2, b_qkv, b_fc1),
        segments,
    )
    wide = padded(total) + SMALL
    near, near_out = stash_call(scalars, packed[0], w_out)
    got = [near] + along("ctx", packed[1:], hops_c)
    joint, fc_here = collect_call(scalars, got, near_out, wide)
    joint = [joint] + along("seq", [joint] * (seqs - 1), hops_s)
    w_fc = [fc_here] + along("seq", [fc_here] * (seqs - 1), hops_s)
    x_all = spread_ctx(x_here)
    dy_all = spread_ctx(dy_here)

    tables = tables_call(scalars, joint[0], rows, share, piece)
    gain, shift, bias_out, bias_qkv, bias_fc1, *out_parts = spread_out_call(
        scalars, joint, rows, share, width, group, heads, lanes, cut
    )
    out_parts = out_parts[:1] + along("ctx", out_parts[1:], hops_g)

    block = min(256, seq_len)
    h, xhat, attn, lse, kept, turned, w_qkv_c = attend_call(
        scalars, block, heads, rows, x_all, gain, shift, joint, bias_qkv, tables
    )
    w_fc_c, slope, act, out_mine, w_out_c, out_theirs = forward_call(
        scalars, rows, piece, h, w_fc, bias_fc1, attn, out_parts
    )
    out_theirs = along("ctx", [out_theirs], [partner(1)])[0]
    out_keep, *out_sends = middle_call(scalars, piece, out_mine, out_theirs)
    out_parts = along("ctx", out_sends, hops_z)
    block_out = emit_call(scalars, x_here, bias_out, out_keep, out_parts)

    dy, dfc, dattn, sum_fc1 = backward_call(scalars, dy_all, w_fc_c, w_out_c, slope)
    grad_fc1 = rows_dot(h, dfc).astype(bf16)
    grad_fc2 = rows_dot(dy, act).astype(bf16)
    grad_out = rows_dot(attn, dy).astype(bf16)
    split = split_fc_call(scalars, seqs, share, group, grad_fc1, grad_fc2, grad_out)
    fc_parts, halves = split[:seqs], split[seqs:]
    fc_parts = fc_parts[:1] + along("seq", fc_parts[1:], hops_s)
    halves = along("ctx", halves, hops_g)
    dqkv, sum_qkv = attend_back_call(
        scalars, block, heads, kept, turned, dattn, lse, tables, (fc_parts[0],)
    )
    dh_mine, sum_gain, sum_shift, dh_theirs = input_grad_call(
        scalars, piece, dfc, w_fc_c, dqkv, w_qkv_c, xhat
    )
    dh_theirs = along("ctx", [dh_theirs], [partner(1)])[0]
    grad_qkv = rows_dot(h, dqkv).astype(bf16)
    qkv_parts = split_qkv_call(
        scalars,
        seqs,
        share,
        group,
        heads,
        lanes,
        grad_qkv,
        grad_out,
        halves,
        (sum_gain, sum_shift, dy_here, sum_qkv, sum_fc1),
    )
    qkv_parts = qkv_parts[:1] + along("seq", qkv_parts[1:], hops_s)
    dh_keep, *dh_sends = middle_call(scalars, piece, dh_mine, dh_theirs)
    dh_parts = along("ctx", dh_sends, hops_z)

    fc_home = sum_fc_call(scalars, share, fc_parts)
    fc_home = fc_home[:1] + along("ctx", fc_home[1:], hops_c)
    out_wout, *qkv_home = sum_qkv_call(scalars, share, width, rows, qkv_parts)
    qkv_home = qkv_home[:1] + along("ctx", qkv_home[1:], hops_c)
    grad_in, finished = finish_call(scalars, x_here, dy_here, gain, dh_keep, dh_parts)
    out_wfc1, out_wfc2, finished = home_fc_call(scalars, fc_home, (finished,))
    out_wqkv, *small = home_qkv_call(
        scalars, group, heads, lanes, width, qkv_home, (finished,)
    )
    small = [value.reshape(-1) for value in small]
    return (
        block_out[None],
        grad_in[None],
        small[0],
        small[1],
        out_wqkv,
        small[3],
        out_wout,
        small[2],
        out_wfc1,
        small[4],
        out_wfc2,
        small[5],
    )


def solution(mesh):
    both = ("seq", "ctx")
    tokens, flat, matrix = P("seq", "ctx", None), P(both), P(both, None)
    in_specs = (tokens, tokens, P("seq", "ctx"), flat, flat) + (matrix, flat) * 4
    out_specs = (tokens, tokens, flat, flat) + (matrix, flat) * 4
    return jax.shard_map(body, mesh=mesh, in_specs=in_specs, out_specs=out_specs, check_vma=False)
```
